32 devices in a mesh: acct: 8 (over z, y), rep: 4 (over x, core).
Axes of the slice: x: 2, y: 2, z: 4, core: 2. Of those that a mesh axis runs over, the one named last changes fastest.
Arguments:
- memory: bfloat16 [262144, 256], P(('acct', 'rep')), may hold values from -4 to 4
- features: bfloat16 [4096, 128], P(('acct', 'rep')), may hold values from -6 to 6
- buckets: int32 [4096], P(('acct', 'rep')), may hold values from 0 to 4095
- src_owner: int32 [4096, 1], P(('acct', 'rep')), may hold values from 0 to 31; in each aligned block of 128 rows (0 to 127, 128 to 255, ...) at most 8 rows name the same one
- src_slot: int32 [4096], P(('acct', 'rep')), may hold values from 0 to 8191
- dst_owner: int32 [4096, 1], P(('acct', 'rep')), may hold values from 0 to 31; in each aligned block of 128 rows (0 to 127, 128 to 255, ...) at most 8 rows name the same one
- dst_slot: int32 [4096], P(('acct', 'rep')), may hold values from 0 to 8191
- nb_owner: int32 [4096, 10, 1], P(('acct', 'rep')), may hold values from 0 to 31; in each aligned block of 1280 rows (0 to 1279, 1280 to 2559, ..., all dimensions but the last counted through in order) at most 80 rows name the same one
- nb_slot: int32 [4096, 10], P(('acct', 'rep')), may hold values from 0 to 8191
- w_msg: bfloat16 [512, 128], replicated, may hold values from -0.25 to 0.25
- w_in: bfloat16 [128, 768], replicated, may hold values from -0.5 to 0.5
- u_zr: bfloat16 [256, 512], replicated, may hold values from -0.375 to 0.375
- u_h: bfloat16 [256, 256], replicated, may hold values from -0.375 to 0.375
- w_query: bfloat16 [256, 256], replicated, may hold values from -0.375 to 0.375
- w_key: bfloat16 [256, 256], replicated, may hold values from -0.375 to 0.375
- w_value: bfloat16 [256, 256], replicated, may hold values from -0.375 to 0.375
- emb_grad: bfloat16 [4096, 256], P(('acct', 'rep')), may hold values from -6 to 6
Outputs:
- new_memory: bfloat16 [262144, 256], P(('acct', 'rep'))
- embedding: bfloat16 [4096, 256], P(('acct', 'rep'))
- grad_msg: float32 [512, 128], replicated
- grad_in: float32 [128, 768], replicated
- grad_zr: float32 [256, 512], replicated
- grad_h: float32 [256, 256], replicated
- grad_query: float32 [256, 256], replicated
- grad_key: float32 [256, 256], replicated
- grad_value: float32 [256, 256], replicated
The draws below stay inside these ranges and needn't reach their ends.
Inputs may be any that keep to these rules, and one draw needn't show every extreme that they name: `src_owner`: in each aligned block of 128 events (one device's events) at most 8 events name one owner, a bound that some block reaches. `dst_owner`: in each aligned block of 128 events at most 8 events name one owner, a bound that some block reaches. `nb_owner`: in each aligned block of 128 events (1280 entries) at most 80 entries name one owner, a bound that some block reaches.
All inputs are finite; a program needn't handle non-finite values.
Results may differ from the reference program's by a relative error of at most 0.01.
Values may be sent and summed in bfloat16 or wider, within the bound.
No kernel may reach another device: no remote copies, remote signals or barrier semaphores. Data moves between devices by JAX's collectives and lax.ppermute only.
A program may use at most 192 MiB of HBM per device.

```python
import math
import jax
import jax.numpy as jnp
import numpy as np
from jax import lax

M = 256
MSG = 128
FEAT = 128
TDIM = 128
HEADS = 2
K = 10
BUCKETS = 4096
E_DEV = 128
ACC_DEV = 8192
EVENTS = 4096
ACCOUNTS = 262144
CAP_E = 8
CAP_N = 80
DEVICES = 32


def touch_ends(result, own_key, smallest, top_value):
    longest = result.shape.index(max(result.shape))
    spots = []
    for shift in (0, 1):
        where = [jax.random.randint(jax.random.fold_in(own_key, axis), (), 0, length) for axis, length in enumerate(result.shape)]
        where[longest] = (where[longest] + shift) % result.shape[longest]
        spots.append(tuple(where))
    return result.at[spots[0]].set(smallest).at[spots[1]].set(top_value)


def steps_of(stream_key, extent, cuts, least, high):
    level = 1.0
    for dim, parts in cuts:
        steps = jax.random.uniform(jax.random.fold_in(jax.random.fold_in(stream_key, 6), dim), (parts,), jnp.float32, least / len(cuts), high / len(cuts))
        level = level * jnp.repeat(jnp.exp(steps), extent[dim] // parts).reshape((-1,) + (1,) * (len(extent) - 1 - dim))
    return level


def rank_table(number_of, skew):
    loads = [(1 << 20) // math.isqrt(rank ** skew) + 1 for rank in range(1, number_of + 1)]
    deviation = 1 + sum(loads) // (1 << 30)
    return np.cumsum(np.array([max(1, weight // deviation) for weight in loads]))


def ranked(key, dims, amount, slope):
    grid = rank_table(amount, slope)
    pick = jax.random.randint(jax.random.fold_in(key, 1), dims, 0, int(grid[amount - 1]))
    grade = jnp.searchsorted(jnp.asarray(grid, jnp.int32), pick, side="right")
    return jax.random.permutation(jax.random.fold_in(key, 2), amount)[grade].astype(jnp.int32)


def assign_block(key, own, number, rows, count, top, most, skew):
    ranking = jax.random.permutation(key, count)
    packed, ordinary = load_shares(count, rows * top, most, skew, True), load_shares(count, rows * top, most, skew, False)
    places = jnp.arange(count)

    def named(lengths, rotation):
        used = int((lengths > 0).sum())
        fixed = max(1, used // 4)
        moved = fixed + (places - fixed + rotation * (used - fixed)) % max(1, count - fixed)
        return jnp.zeros((count,), jnp.int32).at[ranking[jnp.where(places < fixed, places, moved)]].set(jnp.asarray(lengths, jnp.int32))

    lengths = jnp.where(number % 4 == 0, named(packed, number // 4), named(ordinary, number - number // 4 - 1))
    mixed = jax.random.permutation(jax.random.fold_in(own, 3), count)
    source_of, receiver = mixed[0:count // 2 * 2:2], mixed[1:count // 2 * 2:2]
    margin = jnp.minimum(lengths[source_of] - 1, most - lengths[receiver]) // 2
    margin = jnp.where((source_of == ranking[0]) | (receiver == ranking[0]) | (lengths[receiver] == 0), 0, jnp.maximum(margin, 0))
    moved = jax.random.randint(jax.random.fold_in(own, 4), (count // 2,), 0, 1 << 20) % (margin + 1)
    lengths = lengths.at[source_of].add(-moved).at[receiver].add(moved)
    items = jnp.searchsorted(jnp.cumsum(lengths), jnp.arange(rows * top), side="right").astype(jnp.int32)
    table = items.reshape(top, rows).T
    table = table[jax.random.permutation(jax.random.fold_in(own, 1), rows)]
    rotation = jax.random.randint(jax.random.fold_in(own, 2), (rows, 1), 0, top)
    return jnp.take_along_axis(table, (jnp.arange(top)[None, :] + rotation) % top, axis=1)


def load_shares(count, total, most, slope, full):
    weights = [(1 << 20) // math.isqrt(grade ** slope) + 1 for grade in range(1, count + 1)]
    largest = most if full else min(most, max(-(-total // count), total * weights[0] // sum(weights)))
    least = 1 if total - largest >= count - 1 else 0
    given, surplus = [largest] + [least] * (count - 1), total - largest - least * (count - 1)
    while surplus > 0:
        free = [i for i in range(1, count) if given[i] < largest] or [i for i in range(1, count) if given[i] < most]
        mass, left = sum([weights[i] for i in free]), surplus
        for i in free:
            addition = min(most - given[i], max(1, left * weights[i] // mass), surplus)
            given[i] = given[i] + addition
            surplus = surplus - addition
    return np.array(given)


def scatter_about(own_key, dims, width, limit, split=(), kind=jnp.bfloat16):
    factor_of = steps_of(own_key, dims, split, -0.22, 0.18) if split else 1.0
    entries = jax.random.normal(own_key, dims, jnp.float32) * width * factor_of
    return jnp.minimum(jnp.maximum(entries, -limit), limit).astype(kind)


def setup_inputs(seed: int = 0) -> dict:
    key_of = jax.random.split(jax.random.key(seed), 18)
    memory = scatter_about(key_of[0], (ACCOUNTS, M), 1.0, 4.0, ((0, 32),))
    features = scatter_about(key_of[1], (EVENTS, FEAT), 1.0, 6.0, ((0, 32),))
    buckets = touch_ends(jax.random.randint(key_of[2], (EVENTS,), 0, BUCKETS), jax.random.fold_in(key_of[2], 1), 0, BUCKETS - 1).astype(jnp.int32)
    src_owner_keys = jax.random.split(jax.random.fold_in(key_of[3], 1), EVENTS // E_DEV)
    src_owner_turns = jax.random.permutation(jax.random.fold_in(key_of[3], 3), EVENTS // E_DEV)
    src_owner = jax.vmap(lambda own, number: assign_block(jax.random.fold_in(key_of[3], 2), own, number, E_DEV, DEVICES, 1, CAP_E, 2))(src_owner_keys, src_owner_turns).reshape((EVENTS, 1))
    src_slot = touch_ends(ranked(key_of[4], (EVENTS,), ACC_DEV, 2), jax.random.fold_in(key_of[4], 3), 0, ACC_DEV - 1).astype(jnp.int32)
    dst_owner_keys = jax.random.split(jax.random.fold_in(key_of[5], 1), EVENTS // E_DEV)
    dst_owner_turns = jax.random.permutation(jax.random.fold_in(key_of[5], 3), EVENTS // E_DEV)
    dst_owner = jax.vmap(lambda own, number: assign_block(jax.random.fold_in(key_of[5], 2), own, number, E_DEV, DEVICES, 1, CAP_E, 2))(dst_owner_keys, dst_owner_turns).reshape((EVENTS, 1))
    dst_slot = touch_ends(ranked(key_of[6], (EVENTS,), ACC_DEV, 2), jax.random.fold_in(key_of[6], 3), 0, ACC_DEV - 1).astype(jnp.int32)
    nb_owner_keys = jax.random.split(jax.random.fold_in(key_of[7], 1), EVENTS * K // (E_DEV * K))
    nb_owner_turns = jax.random.permutation(jax.random.fold_in(key_of[7], 3), EVENTS * K // (E_DEV * K))
    nb_owner = jax.vmap(lambda own, number: assign_block(jax.random.fold_in(key_of[7], 2), own, number, E_DEV * K, DEVICES, 1, CAP_N, 2))(nb_owner_keys, nb_owner_turns).reshape((EVENTS, K, 1))
    nb_slot = touch_ends(ranked(key_of[8], (EVENTS, K), ACC_DEV, 2), jax.random.fold_in(key_of[8], 3), 0, ACC_DEV - 1).astype(jnp.int32)
    w_msg = scatter_about(key_of[9], (M + FEAT + TDIM, MSG), (M + FEAT + TDIM) ** -0.5, 0.25)
    w_in = scatter_about(key_of[10], (MSG, 3 * M), MSG ** -0.5, 0.5)
    u_zr = scatter_about(key_of[11], (M, 2 * M), M ** -0.5, 0.375)
    u_h = scatter_about(key_of[12], (M, M), M ** -0.5, 0.375)
    w_query = scatter_about(key_of[13], (M, M), M ** -0.5, 0.375)
    w_key = scatter_about(key_of[14], (M, M), M ** -0.5, 0.375)
    w_value = scatter_about(key_of[15], (M, M), M ** -0.5, 0.375)
    emb_grad = scatter_about(key_of[16], (EVENTS, M), 1.0, 6.0, ((0, 32),))
    return {"memory": memory, "features": features, "buckets": buckets, "src_owner": src_owner, "src_slot": src_slot, "dst_owner": dst_owner, "dst_slot": dst_slot, "nb_owner": nb_owner, "nb_slot": nb_slot, "w_msg": w_msg, "w_in": w_in, "u_zr": u_zr, "u_h": u_h, "w_query": w_query, "w_key": w_key, "w_value": w_value, "emb_grad": emb_grad}


cap_value = 10.0

def widen(tensor):
    return lax.optimization_barrier(tensor).astype(jnp.float32)

def time_code(buckets, code_width):
    column = jnp.arange(code_width, dtype=jnp.float32)
    frequency = jnp.exp(column * (-11.5 / code_width))
    return jnp.cos(buckets.astype(jnp.float32)[:, None] * frequency[None, :])

def message_forward(own_rows, features, buckets, w_msg):
    code_width = w_msg.shape[0] - own_rows.shape[1] - features.shape[1]
    encoded = time_code(buckets, code_width).astype(jnp.bfloat16)
    inputs = jnp.concatenate([own_rows, features, encoded], axis=1)
    pre_act = jnp.dot(inputs, w_msg, preferred_element_type=jnp.float32)
    message = jax.nn.silu(pre_act).astype(jnp.bfloat16)
    return (inputs, pre_act, message)

def message_backward(inputs, pre_act, d_message):
    sigmoid_pre = jax.nn.sigmoid(pre_act)
    d_pre = (d_message * sigmoid_pre * (1.0 + pre_act * (1.0 - sigmoid_pre))).astype(jnp.bfloat16)
    return jnp.dot(inputs.T, d_pre, preferred_element_type=jnp.float32)

def gru_forward(mean_rows, state_rows, touched, w_in, u_zr, u_h):
    row_width = state_rows.shape[1]
    from_input = jnp.dot(mean_rows, w_in, preferred_element_type=jnp.float32)
    from_state = jnp.dot(state_rows, u_zr, preferred_element_type=jnp.float32)
    update_gate = jax.nn.sigmoid(from_input[:, :row_width] + from_state[:, :row_width])
    reset_gate = jax.nn.sigmoid(from_input[:, row_width:2 * row_width] + from_state[:, row_width:])
    state_wide = state_rows.astype(jnp.float32)
    reset_state = (reset_gate * state_wide).astype(jnp.bfloat16)
    candidate = jnp.tanh(from_input[:, 2 * row_width:] + jnp.dot(reset_state, u_h, preferred_element_type=jnp.float32))
    updated = (1.0 - update_gate) * state_wide + update_gate * candidate
    new_rows = jnp.where(touched[:, None], updated, state_wide).astype(jnp.bfloat16)
    return (new_rows, (update_gate, reset_gate, candidate, reset_state, state_wide))

def gru_backward(d_rows, touched, kept_values, mean_rows, state_rows, w_in, u_h):
    update_gate, reset_gate, candidate, reset_state, state_wide = kept_values
    row_width = state_rows.shape[1]
    d_updated = jnp.where(touched[:, None], d_rows, jnp.zeros_like(d_rows))
    d_update = d_updated * (candidate - state_wide)
    d_candidate = (d_updated * update_gate * (1.0 - candidate * candidate)).astype(jnp.bfloat16)
    grad_h = jnp.dot(reset_state.T, d_candidate, preferred_element_type=jnp.float32)
    d_reset_state = jnp.dot(d_candidate, u_h.T, preferred_element_type=jnp.float32)
    d_reset = d_reset_state * state_wide * reset_gate * (1.0 - reset_gate)
    d_update_in = d_update * update_gate * (1.0 - update_gate)
    d_gates = jnp.concatenate([d_update_in.astype(jnp.bfloat16), d_reset.astype(jnp.bfloat16), d_candidate], axis=1)
    grad_in = jnp.dot(mean_rows.T, d_gates, preferred_element_type=jnp.float32)
    grad_zr = jnp.dot(state_rows.T, d_gates[:, :2 * row_width], preferred_element_type=jnp.float32)
    d_mean = jnp.dot(d_gates, w_in.T, preferred_element_type=jnp.float32)
    return (d_mean, grad_in, grad_zr, grad_h)

def attend(q_rows, k_rows, w_query, w_key, w_value, upstream):
    batch_rows, row_width = q_rows.shape
    neighbours = k_rows.shape[1]
    head_size = row_width // HEADS
    scaling = 1.0 / math.sqrt(head_size)
    flat_keys = k_rows.reshape(batch_rows * neighbours, row_width)
    query_proj = jnp.dot(q_rows, w_query, preferred_element_type=jnp.float32).astype(jnp.bfloat16)
    key_proj = jnp.dot(flat_keys, w_key, preferred_element_type=jnp.float32).astype(jnp.bfloat16)
    value_proj = jnp.dot(flat_keys, w_value, preferred_element_type=jnp.float32).astype(jnp.bfloat16)
    q_heads = widen(query_proj).reshape(batch_rows, HEADS, head_size)
    k_heads = widen(key_proj).reshape(batch_rows, neighbours, HEADS, head_size)
    v_heads = widen(value_proj).reshape(batch_rows, neighbours, HEADS, head_size)
    raw_scores = jnp.einsum('bhd,bkhd->bhk', q_heads, k_heads) * scaling
    capped = jnp.tanh(raw_scores / cap_value)
    weights = jnp.exp(cap_value * capped)
    attention = weights / lax.optimization_barrier(jnp.sum(weights, axis=2, keepdims=True))
    attention_b = widen(attention.astype(jnp.bfloat16))
    mixture = jnp.einsum('bhk,bkhd->bhd', attention_b, v_heads).reshape(batch_rows, row_width)
    embedded = (q_rows.astype(jnp.float32) + mixture).astype(jnp.bfloat16)
    up_heads = upstream.reshape(batch_rows, HEADS, head_size)
    d_probs = jnp.einsum('bhd,bkhd->bhk', up_heads, v_heads)
    d_scores = attention * (d_probs - lax.optimization_barrier(jnp.sum(attention * d_probs, axis=2, keepdims=True)))
    d_raw = d_scores * (1.0 - capped * capped) * scaling
    d_query = jnp.einsum('bhk,bkhd->bhd', d_raw, k_heads).reshape(batch_rows, row_width).astype(jnp.bfloat16)
    d_keys = jnp.einsum('bhk,bhd->bkhd', d_raw, q_heads).reshape(batch_rows * neighbours, row_width).astype(jnp.bfloat16)
    d_values = jnp.einsum('bhk,bhd->bkhd', attention_b, up_heads).reshape(batch_rows * neighbours, row_width).astype(jnp.bfloat16)
    grad_query = jnp.dot(q_rows.T, d_query, preferred_element_type=jnp.float32)
    grad_key = jnp.dot(flat_keys.T, d_keys, preferred_element_type=jnp.float32)
    grad_value = jnp.dot(flat_keys.T, d_values, preferred_element_type=jnp.float32)
    d_q_rows = upstream + jnp.dot(d_query, w_query.T, preferred_element_type=jnp.float32)
    d_k_rows = (jnp.dot(d_keys, w_key.T, preferred_element_type=jnp.float32) + jnp.dot(d_values, w_value.T, preferred_element_type=jnp.float32)).reshape(batch_rows, neighbours, row_width)
    return (embedded, d_q_rows, d_k_rows, grad_query, grad_key, grad_value)

def reference(memory, features, buckets, src_owner, src_slot, dst_owner, dst_slot, nb_owner, nb_slot, w_msg, w_in, u_zr, u_h, w_query, w_key, w_value, emb_grad):
    src_id = (src_owner[:, 0] * ACC_DEV + src_slot).astype(jnp.int32)
    dst_id = (dst_owner[:, 0] * ACC_DEV + dst_slot).astype(jnp.int32)
    nb_id = (nb_owner[:, :, 0] * ACC_DEV + nb_slot).astype(jnp.int32)
    side_id = jnp.concatenate([src_id, dst_id]).astype(jnp.int32)
    inputs, pre_act, message = message_forward(memory[side_id], jnp.concatenate([features, features]), jnp.concatenate([buckets, buckets]), w_msg)
    totals = jax.ops.segment_sum(message.astype(jnp.float32), side_id, ACCOUNTS)
    counts = jax.ops.segment_sum(jnp.ones(side_id.shape, jnp.float32), side_id, ACCOUNTS)
    divisor = jnp.maximum(counts, 1.0)[:, None]
    mean_rows = (totals / divisor).astype(jnp.bfloat16)
    touched = counts > 0.5
    block_rows = 8192
    blocks = ACCOUNTS // block_rows
    mean_blocks = mean_rows.reshape(blocks, block_rows, -1)
    state_blocks = memory.reshape(blocks, block_rows, -1)
    touched_blocks = touched.reshape(blocks, block_rows)

    def forward_block(pieces):
        return gru_forward(pieces[0], pieces[1], pieces[2], w_in, u_zr, u_h)[0]
    new_memory = lax.map(forward_block, (mean_blocks, state_blocks, touched_blocks)).reshape(ACCOUNTS, M)
    event_block = 4096
    event_blocks = EVENTS // event_block

    def advance(running, pieces):
        d_memory, sum_query, sum_key, sum_value = running
        dst_part, nb_part, grad_part = pieces
        embedded, d_q_rows, d_k_rows, grad_query, grad_key, grad_value = attend(new_memory[dst_part], new_memory[nb_part], w_query, w_key, w_value, grad_part.astype(jnp.float32))
        d_memory = d_memory.at[dst_part].add(d_q_rows)
        d_memory = d_memory.at[nb_part.reshape(-1)].add(d_k_rows.reshape(-1, M))
        return ((d_memory, sum_query + grad_query, sum_key + grad_key, sum_value + grad_value), embedded)
    square_zero = jnp.zeros((M, M), jnp.float32)
    start = (jnp.zeros((ACCOUNTS, M), jnp.float32), square_zero, square_zero, square_zero)
    finish, embedding = lax.scan(advance, start, (dst_id.reshape(event_blocks, event_block), nb_id.reshape(event_blocks, event_block, K), emb_grad.reshape(event_blocks, event_block, M)))
    d_memory, grad_query, grad_key, grad_value = finish
    embedding = embedding.reshape(EVENTS, M)

    def backward_block(pieces):
        new_rows, kept_values = gru_forward(pieces[0], pieces[1], pieces[2], w_in, u_zr, u_h)
        return gru_backward(pieces[3], pieces[2], kept_values, pieces[0], pieces[1], w_in, u_h)
    d_mean, grad_in, grad_zr, grad_h = lax.map(backward_block, (mean_blocks, state_blocks, touched_blocks, d_memory.reshape(blocks, block_rows, M)))
    d_mean = d_mean.reshape(ACCOUNTS, -1)
    d_message = (d_mean / divisor)[side_id]
    grad_msg = message_backward(inputs, pre_act, d_message)
    return (new_memory, embedding, grad_msg, lax.optimization_barrier(jnp.sum(grad_in, axis=0)), lax.optimization_barrier(jnp.sum(grad_zr, axis=0)), lax.optimization_barrier(jnp.sum(grad_h, axis=0)), grad_query, grad_key, grad_value)
```

```python
import functools
import math

import jax
import jax.numpy as jnp
from jax import lax
from jax.experimental import pallas as pl
from jax.experimental.pallas import tpu as pltpu
from jax.sharding import PartitionSpec as P

HEADS = 2
AXES = ("acct", "rep")
CAP_VALUE = 10.0
F32 = jnp.float32
BF16 = jnp.bfloat16
I32 = jnp.int32
EXACT = lax.Precision.HIGHEST
VMEM_LIMIT = 56 * 1024 * 1024


def dot(a, b, **kw):
    return jnp.dot(a, b, preferred_element_type=F32, **kw)


def dot_nt(a, b, **kw):
    return lax.dot_general(a, b, (((1,), (1,)), ((), ())), preferred_element_type=F32, **kw)


def dot_tn(a, b, **kw):
    return lax.dot_general(a, b, (((0,), (0,)), ((), ())), preferred_element_type=F32, **kw)


def iota(shape, axis):
    return lax.broadcasted_iota(I32, shape, axis)


def sigmoid(v):
    return 1.0 / (1.0 + jnp.exp(-v))


def call(body, outs, args, name, scratch=(), cost=None):
    vm = pl.BlockSpec(memory_space=pltpu.VMEM)
    return pl.pallas_call(
        body,
        out_shape=[jax.ShapeDtypeStruct(s, d) for s, d in outs],
        in_specs=[vm] * len(args),
        out_specs=[vm] * len(outs),
        scratch_shapes=list(scratch),
        compiler_params=pltpu.CompilerParams(vmem_limit_bytes=VMEM_LIMIT),
        cost_estimate=cost,
        name=name,
    )(*args)


def place_body(ce, cn, devices, so, ss, do, ds, no, ns, bk, feat, req, feats, dplace, nrank):
    events = so.shape[1]
    neighbours = no.shape[0]
    upper = (iota((events, events), 0) < iota((events, events), 1)).astype(BF16)
    own = iota((devices, events), 0)
    rows = iota((2 * devices * ce, events), 0)

    def fill(onehot, rank, value, cap):
        hits = (iota((cap, events), 0) == rank).astype(F32)
        return dot_nt(onehot, hits * value.astype(F32), precision=EXACT)

    chosen = jnp.zeros((2 * devices * ce, events), F32)
    for side, (o_ref, s_ref) in enumerate(((so, ss), (do, ds))):
        owner = o_ref[...]
        onehot = (own == owner).astype(F32)
        before = dot(onehot.astype(BF16), upper)
        rank = jnp.sum(onehot * before, axis=0, keepdims=True).astype(I32)
        req[:, side * ce : (side + 1) * ce] = (
            fill(onehot, rank, s_ref[...] + 1, ce).astype(I32) - 1
        )
        req[:, (2 + side) * ce : (3 + side) * ce] = fill(onehot, rank, bk[...], ce).astype(I32)
        chosen = chosen + (rows == owner * (2 * ce) + (side * ce + rank)).astype(F32)
        if side == 1:
            dplace[...] = owner * ce + rank
    feats[...] = dot(chosen.astype(BF16), feat[...]).astype(BF16)
    base = jnp.zeros((devices, 1), F32)
    total = jnp.zeros((devices, cn), F32)
    event = iota((1, events), 1)
    for k in range(neighbours):
        onehot = (own == no[k : k + 1, :]).astype(F32)
        before = dot(onehot.astype(BF16), upper) + base
        rank = jnp.sum(onehot * before, axis=0, keepdims=True).astype(I32)
        nrank[k : k + 1, :] = rank
        base = base + jnp.sum(onehot, axis=1, keepdims=True)
        total = total + fill(onehot, rank, ns[k : k + 1, :] * events + event + 1, cn)
    req[:, 4 * ce : 4 * ce + cn] = total.astype(I32) - 1


def owner_body(
    ce, rows, feats, scol, srow, bcol, w_msg, w_in, u_zr, u_h,
    new, dst_new, sfirst, fcol, code, pre, mean, div, upd, rst, cand, rstate, msg,
):
    n, m = rows.shape
    f = feats.shape[1]
    t = w_msg.shape[0] - m - f
    step = 128
    frequency = jnp.exp(iota((1, t), 1).astype(F32) * (-11.5 / t))

    def messages(i, carry):
        b = pl.ds(pl.multiple_of(i * step, step), step)
        enc = jnp.cos(bcol[b, :].astype(F32) * frequency).astype(BF16)
        code[b, :] = enc
        act = (
            dot(rows[b, :], w_msg[:m, :]) + dot(feats[b, :], w_msg[m : m + f, :])
        ) + dot(enc, w_msg[m + f :, :])
        pre[b, :] = act
        msg[b, :] = (act * sigmoid(act)).astype(BF16)
        return carry

    lax.fori_loop(0, n // step, messages, 0)
    slots = srow[...]

    def gru(i, early):
        b = pl.ds(pl.multiple_of(i * step, step), step)
        mine = scol[b, :]
        same = (mine == slots) & (mine >= 0)
        eq = same.astype(F32)
        eq_b = eq.astype(BF16)
        counts = dot(eq_b, jnp.ones((n, msg.shape[1]), BF16))
        divisor = jnp.maximum(counts, 1.0)
        div[b, :] = divisor
        earlier = jnp.where(iota((step, n), 1) < iota((step, n), 0) + i * step, eq, 0.0)
        fcol[b, :] = (jnp.sum(earlier, axis=1, keepdims=True) < 0.5).astype(F32)
        later = jnp.where(iota((step, n), 1) > iota((step, n), 0) + i * step, eq, 0.0)
        early = early + jnp.sum(later, axis=0, keepdims=True)
        mean_b = (dot(eq_b, msg[...]) / divisor).astype(BF16)
        mean[b, :] = mean_b
        state = rows[b, :]
        state_wide = state.astype(F32)
        from_input = dot(mean_b, w_in[...])
        from_state = dot(state, u_zr[...])
        update = sigmoid(from_input[:, :m] + from_state[:, :m])
        reset = sigmoid(from_input[:, m : 2 * m] + from_state[:, m:])
        reset_state = (reset * state_wide).astype(BF16)
        candidate = jnp.tanh(from_input[:, 2 * m :] + dot(reset_state, u_h[...]))
        upd[b, :] = update
        rst[b, :] = reset
        cand[b, :] = candidate
        rstate[b, :] = reset_state
        new[b, :] = ((1.0 - update) * state_wide + update * candidate).astype(BF16)
        return early

    early = lax.fori_loop(0, n // step, gru, jnp.zeros((1, n), F32))
    sfirst[...] = jnp.where(early < 0.5, slots, -2)
    half = n // 2
    r = iota((half, n), 0)
    pick = (iota((half, n), 1) == r + (r // ce + 1) * ce).astype(F32).astype(BF16)
    dst_new[...] = dot(pick, new[...]).astype(BF16)


def patch_body(old, ncol, sfirst, new, out):
    hit = (ncol[...] == sfirst[...]).astype(F32).astype(BF16)
    rows = dot(hit, new[...])
    found = dot(hit, jnp.ones((new.shape[0], 128), BF16)) > 0.5
    for h in range(rows.shape[1] // 128):
        c = slice(h * 128, (h + 1) * 128)
        out[:, c] = jnp.where(found, rows[:, c], old[:, c].astype(F32)).astype(BF16)


def patch(old, ncol, sfirst, new):
    n, m = old.shape
    s = new.shape[0]
    block = 512
    return pl.pallas_call(
        patch_body,
        grid=(n // block,),
        out_shape=jax.ShapeDtypeStruct((n, m), BF16),
        in_specs=[
            pl.BlockSpec((block, m), lambda i: (i, 0)),
            pl.BlockSpec((block, 1), lambda i: (i, 0)),
            pl.BlockSpec((1, s), lambda i: (0, 0)),
            pl.BlockSpec((s, m), lambda i: (0, 0)),
        ],
        out_specs=pl.BlockSpec((block, m), lambda i: (i, 0)),
        name="patch",
    )(old, ncol, sfirst, new)


def query_body(back, dplace, w_query, q_rows, q_proj):
    n = back.shape[0]
    events = dplace.shape[1]
    pick = (iota((n, events), 0) == dplace[...]).astype(F32).astype(BF16)
    q = dot_tn(pick, back[...]).astype(BF16)
    q_rows[...] = q
    q_proj[...] = dot(q, w_query[...]).astype(BF16)


def attend_body(
    cn, devices, keys, q_rows, q_proj, grad, w_query, w_key, w_value, dplace, no, nrank,
    emb, dq_out, scal, g_qkv, kp, vp, dk, dv,
):
    events, m = q_rows.shape
    neighbours = no.shape[0]
    hs = m // HEADS
    scaling = 1.0 / math.sqrt(hs)
    qf = q_proj[...].astype(F32)
    gf = grad[...].astype(F32)
    lane = iota((events, 128), 1)
    raw = jnp.zeros((events, 128), F32)
    probs = jnp.zeros((events, 128), F32)
    for k in range(neighbours):
        b = slice(k * events, (k + 1) * events)
        rows = keys[b, :]
        kpk = dot(rows, w_key[...]).astype(BF16)
        vpk = dot(rows, w_value[...]).astype(BF16)
        kp[b, :] = kpk
        vp[b, :] = vpk
        pk = qf * kpk.astype(F32)
        pv = gf * vpk.astype(F32)
        for h in range(HEADS):
            c = slice(h * hs, (h + 1) * hs)
            at = lane == h * 64 + k
            raw = jnp.where(at, jnp.sum(pk[:, c], axis=1, keepdims=True), raw)
            probs = jnp.where(at, jnp.sum(pv[:, c], axis=1, keepdims=True), probs)
    raw = raw * scaling
    capped = jnp.tanh(raw / CAP_VALUE)
    first = lane < 64
    live = jnp.where(first, lane, lane - 64) < neighbours
    weights = jnp.where(live, jnp.exp(CAP_VALUE * capped), 0.0)

    def per_head(v):
        a = jnp.sum(jnp.where(first, v, 0.0), axis=1, keepdims=True)
        b = jnp.sum(jnp.where(first, 0.0, v), axis=1, keepdims=True)
        return jnp.where(first, a, b)

    attention = weights / per_head(weights)
    att_b = attention.astype(BF16).astype(F32)
    d_scores = attention * (probs - per_head(attention * probs))
    d_raw = d_scores * (1.0 - capped * capped) * scaling
    mix = [jnp.zeros((events, hs), F32) for _ in range(HEADS)]
    dq = [jnp.zeros((events, hs), F32) for _ in range(HEADS)]
    for k in range(neighbours):
        b = slice(k * events, (k + 1) * events)
        for h in range(HEADS):
            c = slice(h * hs, (h + 1) * hs)
            i = h * 64 + k
            a = att_b[:, i : i + 1]
            d = d_raw[:, i : i + 1]
            mix[h] = mix[h] + a * vp[b, c].astype(F32)
            dq[h] = dq[h] + d * kp[b, c].astype(F32)
            dk[b, c] = (d * qf[:, c]).astype(BF16)
            dv[b, c] = (a * gf[:, c]).astype(BF16)
    q = q_rows[...]
    dq_b = jnp.concatenate(dq, axis=1).astype(BF16)
    emb[...] = (q.astype(F32) + jnp.concatenate(mix, axis=1)).astype(BF16)
    g_qkv[0:m, :] = dot_tn(q, dq_b).astype(BF16)
    g_qkv[m : 2 * m, :] = dot_tn(keys[...], dk[...]).astype(BF16)
    g_qkv[2 * m : 3 * m, :] = dot_tn(keys[...], dv[...]).astype(BF16)
    d_rows = (gf + dot_nt(dq_b, w_query[...])).astype(BF16)
    spots = (iota((dq_out.shape[0], events), 0) == dplace[...]).astype(F32).astype(BF16)
    dq_out[...] = dot(spots, d_rows).astype(BF16)
    att_t = att_b.T
    raw_t = d_raw.T
    own = iota((devices, events), 0)
    total = jnp.zeros((devices, 4 * cn), F32)
    for k in range(neighbours):
        onehot = (own == no[k : k + 1, :]).astype(F32).astype(BF16)
        hits = (iota((cn, events), 0) == nrank[k : k + 1, :]).astype(F32)
        values = jnp.concatenate(
            [
                hits * raw_t[k : k + 1, :],
                hits * raw_t[64 + k : 65 + k, :],
                hits * att_t[k : k + 1, :],
                hits * att_t[64 + k : 65 + k, :],
            ],
            axis=0,
        ).astype(BF16)
        total = total + dot_nt(onehot, values)
    scal[...] = total.astype(BF16)


def back_body(
    scal, nrow, qe, ge, dq, drow, scol, fcol, rows, feats, code, pre, mean, div,
    upd, rst, cand, rstate, w_in, u_h, w_key, w_value, out, gates, dpre,
):
    n, m = rows.shape
    f = feats.shape[1]
    hs = m // HEADS
    step = 256
    s = mean.shape[1]

    def block(i, carry):
        b = pl.ds(pl.multiple_of(i * step, step), step)
        mine = scol[b, :]
        mine = jnp.where(mine >= 0, mine, -7)
        hit = mine == nrow[...]
        parts = []
        for j in range(4):
            src = qe if j < 2 else ge
            h = j % 2
            a = jnp.where(hit, scal[j : j + 1, :].astype(F32), 0.0).astype(BF16)
            parts.append(dot(a, src[:, h * hs : (h + 1) * hs]).astype(BF16))
        dkey = jnp.concatenate(parts[:2], axis=1)
        dval = jnp.concatenate(parts[2:], axis=1)
        here = (mine == drow[...]).astype(F32).astype(BF16)
        du = dot(here, dq[...]) + dot_nt(dkey, w_key[...]) + dot_nt(dval, w_value[...])
        state = rows[b, :].astype(F32)
        update = upd[b, :]
        reset = rst[b, :]
        candidate = cand[b, :]
        d_cand = (du * update * (1.0 - candidate * candidate)).astype(BF16)
        d_reset = dot_nt(d_cand, u_h[...]) * state * reset * (1.0 - reset)
        d_update = du * (candidate - state) * update * (1.0 - update)
        d_gates = jnp.concatenate([d_update.astype(BF16), d_reset.astype(BF16), d_cand], axis=1)
        d_mean = dot_nt(d_gates, w_in[...]) / div[b, :]
        act = pre[b, :]
        sg = sigmoid(act)
        dpre[b, :] = (d_mean * sg * (1.0 + act * (1.0 - sg))).astype(BF16)
        gates[b, :] = jnp.where(fcol[b, :] > 0.5, d_gates.astype(F32), 0.0).astype(BF16)
        return carry

    lax.fori_loop(0, n // step, block, 0)
    at = 0
    g_in = dot_tn(mean[...], gates[...])
    for j in range(3):
        out[at : at + s, :] = g_in[:, j * m : (j + 1) * m].astype(BF16)
        at += s
    g_zr = dot_tn(rows[...], gates[:, : 2 * m])
    for j in range(2):
        out[at : at + m, :] = g_zr[:, j * m : (j + 1) * m].astype(BF16)
        at += m
    out[at : at + m, :] = dot_tn(rstate[...], gates[:, 2 * m :]).astype(BF16)
    at += m
    out[at : at + m, :s] = dot_tn(rows[...], dpre[...]).astype(BF16)
    out[at : at + f, s:] = dot_tn(feats[...], dpre[...]).astype(BF16)
    out[at + f : at + m, s:] = dot_tn(code[...], dpre[...]).astype(BF16)


def unpack_body(x, g_msg, g_in, g_zr, g_h, g_q, g_k, g_v):
    m = g_h.shape[0]
    s = g_in.shape[0]
    at = 0
    for j in range(3):
        g_in[:, j * m : (j + 1) * m] = x[at : at + s, :].astype(F32)
        at += s
    for j in range(2):
        g_zr[:, j * m : (j + 1) * m] = x[at : at + m, :].astype(F32)
        at += m
    g_h[...] = x[at : at + m, :].astype(F32)
    at += m
    g_msg[:m, :] = x[at : at + m, :s].astype(F32)
    g_msg[m:, :] = x[at : at + m, s:].astype(F32)
    at += m
    for ref in (g_q, g_k, g_v):
        ref[...] = x[at : at + m, :].astype(F32)
        at += m


def exchange(x):
    return lax.all_to_all(x, AXES, split_axis=0, concat_axis=0, tiled=True)


def body(
    memory, features, buckets, src_owner, src_slot, dst_owner, dst_slot, nb_owner, nb_slot,
    w_msg, w_in, u_zr, u_h, w_query, w_key, w_value, emb_grad,
):
    devices = lax.axis_size(AXES)
    events, m = emb_grad.shape
    acc_rows = memory.shape[0]
    neighbours = nb_slot.shape[1]
    feat = features.shape[1]
    width = w_msg.shape[1]
    ce = 2 * events // devices
    cn = 2 * events * neighbours // devices
    n_dst = devices * ce
    n_side = 2 * n_dst
    n_nb = devices * cn
    grad_all = lax.all_gather(emb_grad, AXES, axis=0, tiled=True)
    no = nb_owner.reshape(events, neighbours).T
    req, side_feats, dplace, nrank = call(
        functools.partial(place_body, ce, cn, devices),
        [
            ((devices, 4 * ce + cn), I32),
            ((n_side, feat), BF16),
            ((1, events), I32),
            ((neighbours, events), I32),
        ],
        (
            src_owner.reshape(1, events), src_slot.reshape(1, events),
            dst_owner.reshape(1, events), dst_slot.reshape(1, events),
            no, nb_slot.T, buckets.reshape(1, events), features,
        ),
        "place",
    )
    got = exchange(req.reshape(devices, 1, 4 * ce + cn)).reshape(devices, 4 * ce + cn)
    got_feats = exchange(side_feats.reshape(devices, 2 * ce, feat)).reshape(n_side, feat)
    side_slots = got[:, : 2 * ce].reshape(n_side)
    side_times = got[:, 2 * ce : 4 * ce].reshape(n_side)
    dst_slots = got[:, ce : 2 * ce].reshape(n_dst)
    nb_code = got[:, 4 * ce :].reshape(n_nb)
    nb_slots = jnp.where(nb_code >= 0, nb_code // events, -1)
    nb_event = jnp.maximum(nb_code, 0) % events
    nb_table = nb_event + (jnp.arange(n_nb, dtype=I32) // cn) * events
    fetched = memory[jnp.maximum(side_slots, 0)]
    old_nb = memory[jnp.maximum(nb_slots, 0)]
    (
        new_side, dst_new, sfirst, fcol, code, pre, mean, div, upd, rst, cand, rstate,
    ) = call(
        functools.partial(owner_body, ce),
        [
            ((n_side, m), BF16), ((n_dst, m), BF16), ((1, n_side), I32), ((n_side, 1), F32),
            ((n_side, w_msg.shape[0] - m - feat), BF16), ((n_side, width), F32),
            ((n_side, width), BF16), ((n_side, width), F32),
            ((n_side, m), F32), ((n_side, m), F32), ((n_side, m), F32), ((n_side, m), BF16),
        ],
        (
            fetched, got_feats, side_slots.reshape(n_side, 1), side_slots.reshape(1, n_side),
            side_times.reshape(n_side, 1), w_msg, w_in, u_zr, u_h,
        ),
        "owner",
        scratch=[pltpu.VMEM((n_side, width), BF16)],
    )
    back_dst = exchange(dst_new.reshape(devices, ce, m)).reshape(n_dst, m)
    nb_reply = patch(old_nb, nb_slots.reshape(n_nb, 1), sfirst, new_side)
    back_nb = exchange(nb_reply.reshape(devices, cn, m)).reshape(n_nb, m)
    new_memory = memory.at[jnp.where(side_slots >= 0, side_slots, acc_rows)].set(
        new_side, mode="drop"
    )
    q_rows, q_proj = call(
        query_body,
        [((events, m), BF16), ((events, m), BF16)],
        (back_dst, dplace, w_query),
        "query",
    )
    proj_all = lax.all_gather(q_proj, AXES, axis=0, tiled=True)
    ge = grad_all[nb_table]
    nb_place = (no * cn + nrank).reshape(-1)
    keys = back_nb[nb_place]
    embedding, dq_out, scal, g_qkv = call(
        functools.partial(attend_body, cn, devices),
        [
            ((events, m), BF16), ((n_dst, m), BF16), ((devices, 4 * cn), BF16),
            ((3 * m, m), BF16),
        ],
        (keys, q_rows, q_proj, emb_grad, w_query, w_key, w_value, dplace, no, nrank),
        "attend",
        scratch=[pltpu.VMEM((events * neighbours, m), BF16)] * 4,
    )
    scal_got = exchange(scal.reshape(devices, 4, cn))
    dq_got = exchange(dq_out.reshape(devices, ce, m)).reshape(n_dst, m)
    qe = proj_all[nb_table]
    late = call(
        back_body,
        [((3 * width + 4 * m, m), BF16)],
        (
            scal_got.transpose(1, 0, 2).reshape(4, n_nb), nb_slots.reshape(1, n_nb), qe, ge,
            dq_got, dst_slots.reshape(1, n_dst), side_slots.reshape(n_side, 1), fcol, fetched,
            got_feats, code, pre, mean, div, upd, rst, cand, rstate, w_in, u_h, w_key, w_value,
        ),
        "back",
        scratch=[pltpu.VMEM((n_side, 3 * m), BF16), pltpu.VMEM((n_side, width), BF16)],
    )[0]
    grads = jnp.concatenate([late, g_qkv], axis=0)
    rows = grads.shape[0] // devices
    shares = exchange(grads.reshape(devices, rows, m))
    mine = jnp.sum(shares.astype(F32), axis=0).astype(BF16)
    whole = exchange(jnp.broadcast_to(mine[None], (devices, rows, m)))
    g_msg, g_in, g_zr, g_h, g_q, g_k, g_v = call(
        unpack_body,
        [
            ((w_msg.shape[0], width), F32), ((width, 3 * m), F32), ((m, 2 * m), F32),
            ((m, m), F32), ((m, m), F32), ((m, m), F32), ((m, m), F32),
        ],
        (whole.reshape(devices * rows, m),),
        "unpack",
    )
    return (new_memory, embedding, g_msg, g_in, g_zr, g_h, g_q, g_k, g_v)


def solution(mesh):
    split = P(AXES)
    return jax.shard_map(
        body,
        mesh=mesh,
        in_specs=(split,) * 9 + (P(),) * 7 + (split,),
        out_specs=(split, split) + (P(),) * 7,
        check_vma=False,
    )
```

```python
import functools
import math

import jax
import jax.numpy as jnp
from jax import lax
from jax.experimental import pallas as pl
from jax.experimental.pallas import tpu as pltpu
from jax.sharding import PartitionSpec as P

HEADS = 2
AXES = ("acct", "rep")
CAP_VALUE = 10.0
F32 = jnp.float32
BF16 = jnp.bfloat16
I32 = jnp.int32
EXACT = lax.Precision.HIGHEST
VMEM_LIMIT = 56 * 1024 * 1024


def dot(a, b, **kw):
    return jnp.dot(a, b, preferred_element_type=F32, **kw)


def dot_nt(a, b, **kw):
    return lax.dot_general(a, b, (((1,), (1,)), ((), ())), preferred_element_type=F32, **kw)


def dot_tn(a, b, **kw):
    return lax.dot_general(a, b, (((0,), (0,)), ((), ())), preferred_element_type=F32, **kw)


def iota(shape, axis):
    return lax.broadcasted_iota(I32, shape, axis)


def to_col(table, n, per, lane0, base=0):
    devices, lanes = table.shape
    pick = ((iota((n, devices), 0) + base) // per == iota((n, devices), 1)).astype(F32)
    spread = dot(pick, table, precision=EXACT)
    r = iota((n, lanes), 0) + base
    at = iota((n, lanes), 1) == lane0 + r - r // per * per
    return jnp.sum(jnp.where(at, spread, 0.0), axis=1, keepdims=True)


def to_row(table, n, per, lane0):
    devices, lanes = table.shape
    c = iota((lanes, n), 1)
    pick = (iota((lanes, n), 0) == lane0 + c - c // per * per).astype(F32)
    spread = dot(table, pick, precision=EXACT)
    mine = iota((devices, n), 0) == iota((devices, n), 1) // per
    return jnp.sum(jnp.where(mine, spread, 0.0), axis=0, keepdims=True)


def sigmoid(v):
    return 1.0 / (1.0 + jnp.exp(-v))


def call(body, outs, args, name, scratch=(), cost=None):
    vm = pl.BlockSpec(memory_space=pltpu.VMEM)
    return pl.pallas_call(
        body,
        out_shape=[jax.ShapeDtypeStruct(s, d) for s, d in outs],
        in_specs=[vm] * len(args),
        out_specs=[vm] * len(outs),
        scratch_shapes=list(scratch),
        compiler_params=pltpu.CompilerParams(vmem_limit_bytes=VMEM_LIMIT),
        cost_estimate=cost,
        name=name,
    )(*args)


def place_body(ce, cn, devices, so, ss, do, ds, no, ns, bk, feat, req, feats, dplace, nrank):
    events = so.shape[1]
    neighbours = no.shape[0]
    upper = (iota((events, events), 0) < iota((events, events), 1)).astype(BF16)
    own = iota((devices, events), 0)
    rows = iota((2 * devices * ce, events), 0)

    def fill(onehot, rank, value, cap):
        hits = (iota((cap, events), 0) == rank).astype(F32)
        return dot_nt(onehot, hits * value.astype(F32), precision=EXACT)

    chosen = jnp.zeros((2 * devices * ce, events), F32)
    for side, (o_ref, s_ref) in enumerate(((so, ss), (do, ds))):
        owner = o_ref[...]
        onehot = (own == owner).astype(F32)
        before = dot(onehot.astype(BF16), upper)
        rank = jnp.sum(onehot * before, axis=0, keepdims=True).astype(I32)
        req[:, side * ce : (side + 1) * ce] = (
            fill(onehot, rank, s_ref[...] + 1, ce).astype(I32) - 1
        )
        req[:, (2 + side) * ce : (3 + side) * ce] = fill(onehot, rank, bk[...], ce).astype(I32)
        chosen = chosen + (rows == owner * (2 * ce) + (side * ce + rank)).astype(F32)
        if side == 1:
            dplace[...] = owner * ce + rank
    feats[...] = dot(chosen.astype(BF16), feat[...]).astype(BF16)
    base = jnp.zeros((devices, 1), F32)
    total = jnp.zeros((devices, cn), F32)
    event = iota((1, events), 1)
    for k in range(neighbours):
        onehot = (own == no[k : k + 1, :]).astype(F32)
        before = dot(onehot.astype(BF16), upper) + base
        rank = jnp.sum(onehot * before, axis=0, keepdims=True).astype(I32)
        nrank[k : k + 1, :] = rank
        base = base + jnp.sum(onehot, axis=1, keepdims=True)
        total = total + fill(onehot, rank, ns[k : k + 1, :] * events + event + 1, cn)
    req[:, 4 * ce : 4 * ce + cn] = total.astype(I32) - 1


def owner_body(
    ce, rows, feats, got, w_msg, w_in, u_zr, u_h,
    new, dst_new, sfirst, scol, fcol, code, pre, mean, div, upd, rst, cand, rstate, msg, bcol,
):
    n, f = feats.shape
    m = rows.shape[1]
    t = w_msg.shape[0] - m - f
    step = 128
    frequency = jnp.exp(iota((1, t), 1).astype(F32) * (-11.5 / t))
    table = got[:, : 4 * ce].astype(F32)
    scol[...] = to_col(table, n, 2 * ce, 0).astype(I32)
    bcol[...] = to_col(table, n, 2 * ce, 2 * ce)
    slots = to_row(table, n, 2 * ce, 0).astype(I32)

    def messages(i, carry):
        b = pl.ds(pl.multiple_of(i * step, step), step)
        enc = jnp.cos(bcol[b, :] * frequency).astype(BF16)
        code[b, :] = enc
        act = (
            dot(rows[b, :], w_msg[:m, :]) + dot(feats[b, :], w_msg[m : m + f, :])
        ) + dot(enc, w_msg[m + f :, :])
        pre[b, :] = act
        msg[b, :] = (act * sigmoid(act)).astype(BF16)
        return carry

    lax.fori_loop(0, n // step, messages, 0)
    def gru(i, early):
        b = pl.ds(pl.multiple_of(i * step, step), step)
        mine = scol[b, :]
        same = (mine == slots) & (mine >= 0)
        eq = same.astype(F32)
        eq_b = eq.astype(BF16)
        counts = dot(eq_b, jnp.ones((n, msg.shape[1]), BF16))
        divisor = jnp.maximum(counts, 1.0)
        div[b, :] = divisor
        earlier = jnp.where(iota((step, n), 1) < iota((step, n), 0) + i * step, eq, 0.0)
        fcol[b, :] = (jnp.sum(earlier, axis=1, keepdims=True) < 0.5).astype(F32)
        later = jnp.where(iota((step, n), 1) > iota((step, n), 0) + i * step, eq, 0.0)
        early = early + jnp.sum(later, axis=0, keepdims=True)
        mean_b = (dot(eq_b, msg[...]) / divisor).astype(BF16)
        mean[b, :] = mean_b
        state = rows[b, :]
        state_wide = state.astype(F32)
        from_input = dot(mean_b, w_in[...])
        from_state = dot(state, u_zr[...])
        update = sigmoid(from_input[:, :m] + from_state[:, :m])
        reset = sigmoid(from_input[:, m : 2 * m] + from_state[:, m:])
        reset_state = (reset * state_wide).astype(BF16)
        candidate = jnp.tanh(from_input[:, 2 * m :] + dot(reset_state, u_h[...]))
        upd[b, :] = update
        rst[b, :] = reset
        cand[b, :] = candidate
        rstate[b, :] = reset_state
        new[b, :] = ((1.0 - update) * state_wide + update * candidate).astype(BF16)
        return early

    early = lax.fori_loop(0, n // step, gru, jnp.zeros((1, n), F32))
    sfirst[...] = jnp.where((early < 0.5) & (slots >= 0), slots, -2)
    half = n // 2
    r = iota((half, n), 0)
    pick = (iota((half, n), 1) == r + (r // ce + 1) * ce).astype(F32).astype(BF16)
    dst_new[...] = dot(pick, new[...]).astype(BF16)


def patch_body(events, ce, cn, block, old, got, sfirst, new, out):
    table = got[:, 4 * ce :].astype(F32)
    code = to_col(table, block, cn, 0, pl.program_id(0) * block).astype(I32)
    hit = (code // events == sfirst[...]).astype(F32).astype(BF16)
    rows = dot(hit, new[...])
    found = dot(hit, jnp.ones((new.shape[0], 128), BF16)) > 0.5
    for h in range(rows.shape[1] // 128):
        c = slice(h * 128, (h + 1) * 128)
        out[:, c] = jnp.where(found, rows[:, c], old[:, c].astype(F32)).astype(BF16)


def patch(events, ce, cn, fetched, got, sfirst, new):
    s, m = new.shape
    n = fetched.shape[0] - s
    block = 512
    skip = s // block
    return pl.pallas_call(
        functools.partial(patch_body, events, ce, cn, block),
        grid=(n // block,),
        out_shape=jax.ShapeDtypeStruct((n, m), BF16),
        in_specs=[
            pl.BlockSpec((block, m), lambda i: (i + skip, 0)),
            pl.BlockSpec(got.shape, lambda i: (0, 0)),
            pl.BlockSpec((1, s), lambda i: (0, 0)),
            pl.BlockSpec((s, m), lambda i: (0, 0)),
        ],
        out_specs=pl.BlockSpec((block, m), lambda i: (i, 0)),
        name="patch",
    )(fetched, got, sfirst, new)


def hot_body(events, ce, cn, block, got, out):
    table = got[:, 4 * ce :].astype(F32)
    code = to_col(table, block, cn, 0, pl.program_id(0) * block).astype(I32)
    event = jnp.where(code >= 0, code % events, -1)
    out[...] = (iota((block, events), 1) == event).astype(F32).astype(BF16)


def hot(events, ce, cn, got, n):
    block = 512
    return pl.pallas_call(
        functools.partial(hot_body, events, ce, cn, block),
        grid=(n // block,),
        out_shape=jax.ShapeDtypeStruct((n, events), BF16),
        in_specs=[pl.BlockSpec(got.shape, lambda i: (0, 0))],
        out_specs=pl.BlockSpec((block, events), lambda i: (i, 0)),
        name="hot",
    )(got)


def query_body(back, dplace, w_query, q_rows, q_proj):
    n = back.shape[0]
    events = dplace.shape[1]
    pick = (iota((n, events), 0) == dplace[...]).astype(F32).astype(BF16)
    q = dot_tn(pick, back[...]).astype(BF16)
    q_rows[...] = q
    q_proj[...] = dot(q, w_query[...]).astype(BF16)


def attend_body(
    cn, devices, each, keys, q_rows, q_proj, grad, w_query, w_key, w_value, dback, no, nrank,
    emb, reply, g_qkv, kp, vp, dk, dv,
):
    events, m = q_rows.shape
    neighbours = no.shape[0]
    hs = m // HEADS
    scaling = 1.0 / math.sqrt(hs)
    qf = q_proj[...].astype(F32)
    gf = grad[...].astype(F32)
    lane = iota((events, 128), 1)
    raw = jnp.zeros((events, 128), F32)
    probs = jnp.zeros((events, 128), F32)
    for k in range(neighbours):
        b = slice(k * events, (k + 1) * events)
        rows = keys[b, :]
        kpk = dot(rows, w_key[...]).astype(BF16)
        vpk = dot(rows, w_value[...]).astype(BF16)
        kp[b, :] = kpk
        vp[b, :] = vpk
        pk = qf * kpk.astype(F32)
        pv = gf * vpk.astype(F32)
        for h in range(HEADS):
            c = slice(h * hs, (h + 1) * hs)
            at = lane == h * 64 + k
            raw = jnp.where(at, jnp.sum(pk[:, c], axis=1, keepdims=True), raw)
            probs = jnp.where(at, jnp.sum(pv[:, c], axis=1, keepdims=True), probs)
    raw = raw * scaling
    capped = jnp.tanh(raw / CAP_VALUE)
    first = lane < 64
    live = jnp.where(first, lane, lane - 64) < neighbours
    weights = jnp.where(live, jnp.exp(CAP_VALUE * capped), 0.0)

    def per_head(v):
        a = jnp.sum(jnp.where(first, v, 0.0), axis=1, keepdims=True)
        b = jnp.sum(jnp.where(first, 0.0, v), axis=1, keepdims=True)
        return jnp.where(first, a, b)

    attention = weights / per_head(weights)
    att_b = attention.astype(BF16).astype(F32)
    d_scores = attention * (probs - per_head(attention * probs))
    d_raw = d_scores * (1.0 - capped * capped) * scaling
    mix = [jnp.zeros((events, hs), F32) for _ in range(HEADS)]
    dq = [jnp.zeros((events, hs), F32) for _ in range(HEADS)]
    for k in range(neighbours):
        b = slice(k * events, (k + 1) * events)
        for h in range(HEADS):
            c = slice(h * hs, (h + 1) * hs)
            i = h * 64 + k
            a = att_b[:, i : i + 1]
            d = d_raw[:, i : i + 1]
            mix[h] = mix[h] + a * vp[b, c].astype(F32)
            dq[h] = dq[h] + d * kp[b, c].astype(F32)
            dk[b, c] = (d * qf[:, c]).astype(BF16)
            dv[b, c] = (a * gf[:, c]).astype(BF16)
    q = q_rows[...]
    dq_b = jnp.concatenate(dq, axis=1).astype(BF16)
    emb[...] = (q.astype(F32) + jnp.concatenate(mix, axis=1)).astype(BF16)
    g_qkv[0:m, :] = dot_tn(q, dq_b).astype(BF16)
    g_qkv[m : 2 * m, :] = dot_tn(keys[...], dk[...]).astype(BF16)
    g_qkv[2 * m : 3 * m, :] = dot_tn(keys[...], dv[...]).astype(BF16)
    d_rows = (gf + dot_nt(dq_b, w_query[...])).astype(BF16)
    n = devices * each
    spots = (iota((n, events), 0) == dback[...]).astype(F32).astype(BF16)
    sent = dot(spots, d_rows)
    att_t = att_b.T
    raw_t = d_raw.T
    own = iota((devices, events), 0)
    totals = [jnp.zeros((devices, m), F32) for _ in range(4)]
    for k in range(neighbours):
        onehot = (own == no[k : k + 1, :]).astype(F32).astype(BF16)
        hits = (iota((m, events), 0) == nrank[k : k + 1, :]).astype(F32)
        for j, v in enumerate((raw_t, raw_t, att_t, att_t)):
            i = (j % 2) * 64 + k
            values = (hits * v[i : i + 1, :]).astype(BF16)
            totals[j] = totals[j] + dot_nt(onehot, values)
    for j in range(4):
        spot = iota((n, devices), 0) == iota((n, devices), 1) * each + j
        sent = sent + dot(spot.astype(F32).astype(BF16), totals[j].astype(BF16))
    reply[...] = sent.astype(BF16)


def back_body(
    direct, scal, nrow, qsrc, hots, ge, dq, drow, scol, fcol, rows, feats, code, pre, mean, div,
    upd, rst, cand, rstate, w_in, u_h, w_key, w_value, g_qkv, parity, out, gates, dpre, qe,
):
    n, m = mean.shape[0], rows.shape[1]
    f = feats.shape[1]
    hs = m // HEADS
    step = 256
    s = mean.shape[1]
    if direct:
        qe = qsrc
    else:
        events = hots.shape[1]
        devices = qsrc.shape[0] // events
        cn = hots.shape[0] // devices

        def expand(d, carry):
            b = pl.ds(pl.multiple_of(d * cn, cn), cn)
            e = pl.ds(pl.multiple_of(d * events, events), events)
            qe[b, :] = dot(hots[b, :], qsrc[e, :]).astype(BF16)
            return carry

        lax.fori_loop(0, devices, expand, 0)

    def block(i, carry):
        b = pl.ds(pl.multiple_of(i * step, step), step)
        mine = scol[b, :]
        mine = jnp.where(mine >= 0, mine, -7)
        hit = mine == nrow[...]
        parts = []
        for j in range(4):
            src = qe if j < 2 else ge
            h = j % 2
            a = jnp.where(hit, scal[j : j + 1, :].astype(F32), 0.0).astype(BF16)
            parts.append(dot(a, src[:, h * hs : (h + 1) * hs]).astype(BF16))
        dkey = jnp.concatenate(parts[:2], axis=1)
        dval = jnp.concatenate(parts[2:], axis=1)
        here = (mine == drow[...]).astype(F32).astype(BF16)
        du = dot(here, dq[...]) + dot_nt(dkey, w_key[...]) + dot_nt(dval, w_value[...])
        state = rows[b, :].astype(F32)
        update = upd[b, :]
        reset = rst[b, :]
        candidate = cand[b, :]
        d_cand = (du * update * (1.0 - candidate * candidate)).astype(BF16)
        d_reset = dot_nt(d_cand, u_h[...]) * state * reset * (1.0 - reset)
        d_update = du * (candidate - state) * update * (1.0 - update)
        d_gates = jnp.concatenate([d_update.astype(BF16), d_reset.astype(BF16), d_cand], axis=1)
        d_mean = dot_nt(d_gates, w_in[...]) / div[b, :]
        act = pre[b, :]
        sg = sigmoid(act)
        dpre[b, :] = (d_mean * sg * (1.0 + act * (1.0 - sg))).astype(BF16)
        gates[b, :] = jnp.where(fcol[b, :] > 0.5, d_gates.astype(F32), 0.0).astype(BF16)
        return carry

    lax.fori_loop(0, n // step, block, 0)
    half = out.shape[1]
    me = parity[0, 0]
    at = [0]

    def put(value):
        start, size = at[0], value.shape[0]
        low = max(0, min(size, half - start))
        if low:
            out[me, start : start + low, :] = value[:low, :].astype(BF16)
        if low < size:
            out[1 - me, start + low - half : start + size - half, :] = value[low:, :].astype(BF16)
        at[0] = start + size

    def put_cols(value):
        for j in range(value.shape[1] // 128):
            put(value[:, j * 128 : (j + 1) * 128])

    state_rows = rows[:n, :]
    put_cols(dot_tn(mean[...], gates[...]))
    put_cols(dot_tn(state_rows, gates[:, : 2 * m]))
    put_cols(dot_tn(rstate[...], gates[:, 2 * m :]))
    put_cols(dot_tn(state_rows, dpre[...]))
    put_cols(dot_tn(feats[...], dpre[...]))
    put_cols(dot_tn(code[...], dpre[...]))
    for j in range(3):
        put_cols(g_qkv[j * m : (j + 1) * m, :].astype(F32))


def spread_body(x, out):
    total = x[0].astype(F32)
    for i in range(1, x.shape[0]):
        total = total + x[i].astype(F32)
    total = total.astype(BF16)
    for i in range(x.shape[0]):
        out[i] = total


def unpack_body(mine, other, parity, g_in, g_zr, g_h, g_msg, g_q, g_k, g_v):
    half = mine.shape[0]
    even = parity[0, 0] == 0
    at = [0]

    def take(ref, r, c, size):
        start = at[0]
        low = max(0, min(size, half - start))
        if low:
            b = slice(start, start + low)
            ref[r : r + low, c : c + 128] = jnp.where(even, mine[b, :], other[b, :]).astype(F32)
        if low < size:
            b = slice(start + low - half, start + size - half)
            ref[r + low : r + size, c : c + 128] = jnp.where(
                even, other[b, :], mine[b, :]
            ).astype(F32)
        at[0] = start + size

    for ref in (g_in, g_zr, g_h, g_msg, g_q, g_k, g_v):
        for c in range(0, ref.shape[1], 128):
            take(ref, 0, c, ref.shape[0])


def exchange(x):
    return lax.all_to_all(x, AXES, split_axis=0, concat_axis=0, tiled=True)


def body(
    memory, features, buckets, src_owner, src_slot, dst_owner, dst_slot, nb_owner, nb_slot,
    w_msg, w_in, u_zr, u_h, w_query, w_key, w_value, emb_grad,
):
    devices = lax.axis_size(AXES)
    events, m = emb_grad.shape
    acc_rows = memory.shape[0]
    neighbours = nb_slot.shape[1]
    feat = features.shape[1]
    width = w_msg.shape[1]
    ce = 2 * events // devices
    cn = 2 * events * neighbours // devices
    n_dst = devices * ce
    n_side = 2 * n_dst
    n_nb = devices * cn
    grad_all = lax.all_gather(emb_grad, AXES, axis=0, tiled=True)
    no = nb_owner.reshape(events, neighbours).T
    req, side_feats, dplace, nrank = call(
        functools.partial(place_body, ce, cn, devices),
        [
            ((devices, 4 * ce + cn), I32),
            ((n_side, feat), BF16),
            ((1, events), I32),
            ((neighbours, events), I32),
        ],
        (
            src_owner.reshape(1, events), src_slot.reshape(1, events),
            dst_owner.reshape(1, events), dst_slot.reshape(1, events),
            no, nb_slot.T, buckets.reshape(1, events), features,
        ),
        "place",
    )
    got = exchange(req.reshape(devices, 1, 4 * ce + cn)).reshape(devices, 4 * ce + cn)
    got_feats = exchange(side_feats.reshape(devices, 2 * ce, feat)).reshape(n_side, feat)
    side_slots = got[:, : 2 * ce].reshape(n_side)
    nb_code = got[:, 4 * ce :].reshape(n_nb)
    wanted = jnp.concatenate([side_slots, nb_code // events])
    fetched = memory[jnp.maximum(wanted, 0)]
    (
        new_side, dst_new, sfirst, scol, fcol, code, pre, mean, div, upd, rst, cand, rstate,
    ) = call(
        functools.partial(owner_body, ce),
        [
            ((n_side, m), BF16), ((n_dst, m), BF16), ((1, n_side), I32), ((n_side, 1), I32),
            ((n_side, 1), F32), ((n_side, w_msg.shape[0] - m - feat), BF16),
            ((n_side, width), F32), ((n_side, width), BF16), ((n_side, width), F32),
            ((n_side, m), F32), ((n_side, m), F32), ((n_side, m), F32), ((n_side, m), BF16),
        ],
        (fetched, got_feats, got, w_msg, w_in, u_zr, u_h),
        "owner",
        scratch=[pltpu.VMEM((n_side, width), BF16), pltpu.VMEM((n_side, 1), F32)],
    )
    back_dst = exchange(dst_new.reshape(devices, ce, m)).reshape(n_dst, m)
    nb_reply = patch(events, ce, cn, fetched, got, sfirst, new_side)
    back_nb = exchange(nb_reply.reshape(devices, cn, m))
    back_dst, nb_reply = lax.optimization_barrier((back_dst, nb_reply))
    q_rows, q_proj = call(
        query_body,
        [((events, m), BF16), ((events, m), BF16)],
        (back_dst, dplace, w_query),
        "query",
    )
    proj_all = lax.all_gather(q_proj, AXES, axis=0, tiled=True)
    each = max(2 * ce, -(-(ce + 4) // 8) * 8)
    late_memory, late_got, _ = lax.optimization_barrier((memory, got, nb_reply))
    late_slots = late_got[:, : 2 * ce].reshape(n_side)
    new_memory = late_memory.at[jnp.where(late_slots >= 0, late_slots, acc_rows)].set(
        new_side, mode="drop"
    )
    late_code = late_got[:, 4 * ce :].reshape(n_nb)
    table = jnp.maximum(late_code, 0) % events + jnp.arange(n_nb, dtype=I32) // cn * events
    ge = grad_all[table]
    nrow = (late_code // events).reshape(1, n_nb)
    drow = jnp.concatenate(
        [jnp.full((devices, each - ce), -1, I32), late_got[:, ce : 2 * ce]], axis=1
    ).reshape(1, devices * each)
    hots = hot(events, ce, cn, late_got, n_nb)
    nb_place = (no * cn + nrank).reshape(-1)
    back_nb, new_memory, ge, nrow, drow, hots, nb_place, q_rows = lax.optimization_barrier(
        (back_nb, new_memory, ge, nrow, drow, hots, nb_place, q_rows)
    )
    keys = back_nb.reshape(n_nb, m)[nb_place]
    dback = dplace // ce * each + (each - ce) + dplace % ce
    embedding, reply, g_qkv = call(
        functools.partial(attend_body, cn, devices, each),
        [((events, m), BF16), ((devices * each, m), BF16), ((3 * m, m), BF16)],
        (keys, q_rows, q_proj, emb_grad, w_query, w_key, w_value, dback, no, nrank),
        "attend",
        scratch=[pltpu.VMEM((events * neighbours, m), BF16)] * 4,
    )
    back = exchange(reply.reshape(devices, each, m))
    scal = back[:, :4, :cn].transpose(1, 0, 2).reshape(4, n_nb)
    direct = cn % 16 != 0
    index = lax.axis_index(AXES)
    parity = (index % 2).astype(I32).reshape(1, 1)
    total_rows = (w_msg.size + w_in.size + u_zr.size + u_h.size + 3 * w_query.size) // 128
    half = total_rows // 2
    args = (
        scal, nrow, proj_all[table] if direct else proj_all, hots, ge,
        back.reshape(devices * each, m), drow, scol, fcol, fetched,
        got_feats, code, pre, mean, div, upd, rst, cand, rstate, w_in, u_h, w_key, w_value,
        g_qkv, parity,
    )
    vm = pl.BlockSpec(memory_space=pltpu.VMEM)
    sm = pl.BlockSpec(memory_space=pltpu.SMEM)
    halves = pl.pallas_call(
        functools.partial(back_body, direct),
        out_shape=jax.ShapeDtypeStruct((2, half, 128), BF16),
        in_specs=[vm] * (len(args) - 1) + [sm],
        out_specs=vm,
        scratch_shapes=[
            pltpu.VMEM((n_side, 3 * m), BF16), pltpu.VMEM((n_side, width), BF16),
            pltpu.VMEM((n_nb, m), BF16),
        ],
        compiler_params=pltpu.CompilerParams(vmem_limit_bytes=VMEM_LIMIT),
        name="back",
    )(*args)
    pairs = [(i, i ^ 1) for i in range(devices)]
    teams = [[i for i in range(devices) if i % 2 == p] for p in range(2)]
    size = devices // 2
    keep, send = halves[0], halves[1]
    half_sum = (
        keep.astype(F32) + lax.ppermute(send, AXES, pairs).astype(F32)
    ).astype(BF16).reshape(size, half // size, 128)
    shares = lax.all_to_all(
        half_sum, AXES, split_axis=0, concat_axis=0, tiled=True, axis_index_groups=teams
    )
    spread = call(spread_body, [(shares.shape, BF16)], (shares,), "spread")[0]
    mine = lax.all_to_all(
        spread, AXES, split_axis=0, concat_axis=0, tiled=True, axis_index_groups=teams
    ).reshape(half, 128)
    other = lax.ppermute(mine, AXES, pairs)
    outs = [
        ((width, 3 * m), F32), ((m, 2 * m), F32), ((m, m), F32),
        ((w_msg.shape[0], width), F32), ((m, m), F32), ((m, m), F32), ((m, m), F32),
    ]
    g_in, g_zr, g_h, g_msg, g_q, g_k, g_v = pl.pallas_call(
        unpack_body,
        out_shape=[jax.ShapeDtypeStruct(a, d) for a, d in outs],
        in_specs=[vm, vm, sm],
        out_specs=[vm] * len(outs),
        name="unpack",
    )(mine, other, parity)
    return (new_memory, embedding, g_msg, g_in, g_zr, g_h, g_q, g_k, g_v)


def solution(mesh):
    split = P(AXES)
    return jax.shard_map(
        body,
        mesh=mesh,
        in_specs=(split,) * 9 + (P(),) * 7 + (split,),
        out_specs=(split, split) + (P(),) * 7,
        check_vma=False,
    )
```

```python
import functools
import math

import jax
import jax.numpy as jnp
from jax import lax
from jax.experimental import pallas as pl
from jax.experimental.pallas import tpu as pltpu
from jax.sharding import PartitionSpec as P

HEADS = 2
AXES = ("acct", "rep")
CAP_VALUE = 10.0
F32 = jnp.float32
BF16 = jnp.bfloat16
I32 = jnp.int32
EXACT = lax.Precision.HIGHEST
VMEM_LIMIT = 56 * 1024 * 1024


def dot(a, b, **kw):
    return jnp.dot(a, b, preferred_element_type=F32, **kw)


def dot_nt(a, b, **kw):
    return lax.dot_general(a, b, (((1,), (1,)), ((), ())), preferred_element_type=F32, **kw)


def dot_tn(a, b, **kw):
    return lax.dot_general(a, b, (((0,), (0,)), ((), ())), preferred_element_type=F32, **kw)


def iota(shape, axis):
    return lax.broadcasted_iota(I32, shape, axis)


def to_col(table, n, per, lane0, base=0):
    devices, lanes = table.shape
    pick = ((iota((n, devices), 0) + base) // per == iota((n, devices), 1)).astype(F32)
    spread = dot(pick, table, precision=EXACT)
    r = iota((n, lanes), 0) + base
    at = iota((n, lanes), 1) == lane0 + r - r // per * per
    return jnp.sum(jnp.where(at, spread, 0.0), axis=1, keepdims=True)


def to_row(table, n, per, lane0):
    devices, lanes = table.shape
    c = iota((lanes, n), 1)
    pick = (iota((lanes, n), 0) == lane0 + c - c // per * per).astype(F32)
    spread = dot(table, pick, precision=EXACT)
    mine = iota((devices, n), 0) == iota((devices, n), 1) // per
    return jnp.sum(jnp.where(mine, spread, 0.0), axis=0, keepdims=True)


def sigmoid(v):
    return 1.0 / (1.0 + jnp.exp(-v))


def call(body, outs, args, name, scratch=(), cost=None):
    vm = pl.BlockSpec(memory_space=pltpu.VMEM)
    return pl.pallas_call(
        body,
        out_shape=[jax.ShapeDtypeStruct(s, d) for s, d in outs],
        in_specs=[vm] * len(args),
        out_specs=[vm] * len(outs),
        scratch_shapes=list(scratch),
        compiler_params=pltpu.CompilerParams(vmem_limit_bytes=VMEM_LIMIT),
        cost_estimate=cost,
        name=name,
    )(*args)


def place_body(ce, cn, devices, so, ss, do, ds, no, ns, bk, feat, req, feats, dplace, nrank):
    events = so.shape[1]
    neighbours = no.shape[0]
    upper = (iota((events, events), 0) < iota((events, events), 1)).astype(BF16)
    own = iota((devices, events), 0)
    rows = iota((2 * devices * ce, events), 0)

    def fill(onehot, rank, value, cap):
        hits = (iota((cap, events), 0) == rank).astype(F32)
        return dot_nt(onehot, hits * value.astype(F32), precision=EXACT)

    chosen = jnp.zeros((2 * devices * ce, events), F32)
    for side, (o_ref, s_ref) in enumerate(((so, ss), (do, ds))):
        owner = o_ref[...]
        onehot = (own == owner).astype(F32)
        before = dot(onehot.astype(BF16), upper)
        rank = jnp.sum(onehot * before, axis=0, keepdims=True).astype(I32)
        req[:, side * ce : (side + 1) * ce] = (
            fill(onehot, rank, s_ref[...] + 1, ce).astype(I32) - 1
        )
        req[:, (2 + side) * ce : (3 + side) * ce] = fill(onehot, rank, bk[...], ce).astype(I32)
        chosen = chosen + (rows == owner * (2 * ce) + (side * ce + rank)).astype(F32)
        if side == 1:
            dplace[...] = owner * ce + rank
    feats[...] = dot(chosen.astype(BF16), feat[...]).astype(BF16)
    base = jnp.zeros((devices, 1), F32)
    total = jnp.zeros((devices, cn), F32)
    event = iota((1, events), 1)
    for k in range(neighbours):
        onehot = (own == no[k : k + 1, :]).astype(F32)
        before = dot(onehot.astype(BF16), upper) + base
        rank = jnp.sum(onehot * before, axis=0, keepdims=True).astype(I32)
        nrank[k : k + 1, :] = rank
        base = base + jnp.sum(onehot, axis=1, keepdims=True)
        total = total + fill(onehot, rank, ns[k : k + 1, :] * events + event + 1, cn)
    req[:, 4 * ce : 4 * ce + cn] = total.astype(I32) - 1


def widen_rows(source, target):
    step = 256

    def run(i, carry):
        b = pl.ds(pl.multiple_of(i * step, step), step)
        target[b, :] = source[b, :].astype(F32)
        return carry

    lax.fori_loop(0, source.shape[0] // step, run, 0)


def owner_body(
    ce, cn, shift, memory, feats, got, slots_s, w_msg, w_in, u_zr, u_h,
    new, dst_new, reply, rows, sfirst, scol, fcol, code, pre, mean, div, upd, rst, cand, rstate,
    msg, bcol, table, wide, copied,
):
    n, f = feats.shape
    acc_rows, m = memory.shape
    devices = got.shape[0]
    t = w_msg.shape[0] - m - f
    step = 128
    widen_rows(memory, table)
    group = math.gcd(ce, 8)

    def side_rows(i, carry):
        d, g = i // (2 * ce // group), i % (2 * ce // group)
        base = pl.multiple_of(i * group, group)
        for p in range(group):
            slot = jnp.maximum(slots_s[d, g * group + p], 0)
            wide[pl.ds(base + p, 1), :] = table[pl.ds(slot, 1), :]
        return carry

    lax.fori_loop(0, n // group, side_rows, 0, unroll=2)
    frequency = jnp.exp(iota((1, t), 1).astype(F32) * (-11.5 / t))
    numbers = got[:, : 4 * ce].astype(F32)
    scol[...] = to_col(numbers, n, 2 * ce, 0).astype(I32)
    bcol[...] = to_col(numbers, n, 2 * ce, 2 * ce)
    slots = to_row(numbers, n, 2 * ce, 0).astype(I32)
    rows[...] = jnp.where(scol[...] >= 0, wide[...], 0.0).astype(BF16)

    def messages(i, carry):
        b = pl.ds(pl.multiple_of(i * step, step), step)
        enc = jnp.cos(bcol[b, :] * frequency).astype(BF16)
        code[b, :] = enc
        act = (
            dot(rows[b, :], w_msg[:m, :]) + dot(feats[b, :], w_msg[m : m + f, :])
        ) + dot(enc, w_msg[m + f :, :])
        pre[b, :] = act
        msg[b, :] = (act * sigmoid(act)).astype(BF16)
        return carry

    lax.fori_loop(0, n // step, messages, 0)
    def gru(i, early):
        b = pl.ds(pl.multiple_of(i * step, step), step)
        mine = scol[b, :]
        same = (mine == slots) & (mine >= 0)
        eq = same.astype(F32)
        eq_b = eq.astype(BF16)
        counts = dot(eq_b, jnp.ones((n, msg.shape[1]), BF16))
        divisor = jnp.maximum(counts, 1.0)
        div[b, :] = divisor
        earlier = jnp.where(iota((step, n), 1) < iota((step, n), 0) + i * step, eq, 0.0)
        fcol[b, :] = (jnp.sum(earlier, axis=1, keepdims=True) < 0.5).astype(F32)
        later = jnp.where(iota((step, n), 1) > iota((step, n), 0) + i * step, eq, 0.0)
        early = early + jnp.sum(later, axis=0, keepdims=True)
        mean_b = (dot(eq_b, msg[...]) / divisor).astype(BF16)
        mean[b, :] = mean_b
        state = rows[b, :]
        state_wide = state.astype(F32)
        from_input = dot(mean_b, w_in[...])
        from_state = dot(state, u_zr[...])
        update = sigmoid(from_input[:, :m] + from_state[:, :m])
        reset = sigmoid(from_input[:, m : 2 * m] + from_state[:, m:])
        reset_state = (reset * state_wide).astype(BF16)
        candidate = jnp.tanh(from_input[:, 2 * m :] + dot(reset_state, u_h[...]))
        upd[b, :] = update
        rst[b, :] = reset
        cand[b, :] = candidate
        rstate[b, :] = reset_state
        fresh = ((1.0 - update) * state_wide + update * candidate).astype(BF16)
        new[b, :] = fresh
        wide[b, :] = fresh.astype(F32)
        return early

    early = lax.fori_loop(0, n // step, gru, jnp.zeros((1, n), F32))
    sfirst[...] = jnp.where((early < 0.5) & (slots >= 0), slots, -2)
    half = n // 2
    r = iota((half, n), 0)
    pick = (iota((half, n), 1) == r + (r // ce + 1) * ce).astype(F32).astype(BF16)
    dst_new[...] = dot(pick, new[...]).astype(BF16)

    def store_rows(i, carry):
        d, g = i // (2 * ce // group), i % (2 * ce // group)
        base = pl.multiple_of(i * group, group)
        for p in range(group):
            slot = slots_s[d, g * group + p]
            slot = jnp.where(slot >= 0, slot, acc_rows)
            table[pl.ds(slot, 1), :] = wide[pl.ds(base + p, 1), :]
        return carry

    lax.fori_loop(0, n // group, store_rows, 0, unroll=2)
    bunch = math.gcd(cn, 8)

    def nb_rows(i, carry):
        d, g = i // (cn // bunch), i % (cn // bunch)
        lane = 4 * ce + g * bunch

        @pl.when(slots_s[d, lane] >= 0)
        def _():
            base = pl.multiple_of(i * bunch, bunch)
            for p in range(bunch):
                slot = jnp.maximum(slots_s[d, lane + p], 0) >> shift
                copied[pl.ds(base + p, 1), :] = table[pl.ds(slot, 1), :]

        return carry

    lax.fori_loop(0, devices * cn // bunch, nb_rows, 0)
    reply[...] = copied[...].astype(BF16)


def refresh_body(block, old, sfirst, new, out):
    row = iota((block, 1), 0) + pl.program_id(0) * block
    hit = (row == sfirst[...]).astype(F32).astype(BF16)
    rows = dot(hit, new[...])
    found = dot(hit, jnp.ones((new.shape[0], 128), BF16)) > 0.5
    for h in range(rows.shape[1] // 128):
        c = slice(h * 128, (h + 1) * 128)
        out[:, c] = jnp.where(found, rows[:, c], old[:, c].astype(F32)).astype(BF16)


def refresh(memory, sfirst, new):
    n, m = memory.shape
    s = new.shape[0]
    block = 512
    return pl.pallas_call(
        functools.partial(refresh_body, block),
        grid=(n // block,),
        out_shape=jax.ShapeDtypeStruct((n, m), BF16),
        in_specs=[
            pl.BlockSpec((block, m), lambda i: (i, 0)),
            pl.BlockSpec((1, s), lambda i: (0, 0)),
            pl.BlockSpec((s, m), lambda i: (0, 0)),
        ],
        out_specs=pl.BlockSpec((block, m), lambda i: (i, 0)),
        name="refresh",
    )(memory, sfirst, new)


def hot_body(events, ce, cn, block, got, out):
    table = got[:, 4 * ce :].astype(F32)
    code = to_col(table, block, cn, 0, pl.program_id(0) * block).astype(I32)
    event = jnp.where(code >= 0, code % events, -1)
    out[...] = (iota((block, events), 1) == event).astype(F32).astype(BF16)


def hot(events, ce, cn, got, n):
    block = 512
    return pl.pallas_call(
        functools.partial(hot_body, events, ce, cn, block),
        grid=(n // block,),
        out_shape=jax.ShapeDtypeStruct((n, events), BF16),
        in_specs=[pl.BlockSpec(got.shape, lambda i: (0, 0))],
        out_specs=pl.BlockSpec((block, events), lambda i: (i, 0)),
        name="hot",
    )(got)


def query_body(back, dplace, w_query, q_rows, q_proj):
    n = back.shape[0]
    events = dplace.shape[1]
    pick = (iota((n, events), 0) == dplace[...]).astype(F32).astype(BF16)
    q = dot_tn(pick, back[...]).astype(BF16)
    q_rows[...] = q
    q_proj[...] = dot(q, w_query[...]).astype(BF16)


def attend_body(
    cn, devices, each, keys, q_rows, q_proj, grad, w_query, w_key, w_value, dback, no, nrank,
    emb, reply, g_qkv, kp, vp, dk, dv,
):
    events, m = q_rows.shape
    neighbours = no.shape[0]
    hs = m // HEADS
    scaling = 1.0 / math.sqrt(hs)
    qf = q_proj[...].astype(F32)
    gf = grad[...].astype(F32)
    lane = iota((events, 128), 1)
    raw = jnp.zeros((events, 128), F32)
    probs = jnp.zeros((events, 128), F32)
    for k in range(neighbours):
        b = slice(k * events, (k + 1) * events)
        rows = keys[b, :]
        kpk = dot(rows, w_key[...]).astype(BF16)
        vpk = dot(rows, w_value[...]).astype(BF16)
        kp[b, :] = kpk
        vp[b, :] = vpk
        pk = qf * kpk.astype(F32)
        pv = gf * vpk.astype(F32)
        for h in range(HEADS):
            c = slice(h * hs, (h + 1) * hs)
            at = lane == h * 64 + k
            raw = jnp.where(at, jnp.sum(pk[:, c], axis=1, keepdims=True), raw)
            probs = jnp.where(at, jnp.sum(pv[:, c], axis=1, keepdims=True), probs)
    raw = raw * scaling
    capped = jnp.tanh(raw / CAP_VALUE)
    first = lane < 64
    live = jnp.where(first, lane, lane - 64) < neighbours
    weights = jnp.where(live, jnp.exp(CAP_VALUE * capped), 0.0)

    def per_head(v):
        a = jnp.sum(jnp.where(first, v, 0.0), axis=1, keepdims=True)
        b = jnp.sum(jnp.where(first, 0.0, v), axis=1, keepdims=True)
        return jnp.where(first, a, b)

    attention = weights / per_head(weights)
    att_b = attention.astype(BF16).astype(F32)
    d_scores = attention * (probs - per_head(attention * probs))
    d_raw = d_scores * (1.0 - capped * capped) * scaling
    mix = [jnp.zeros((events, hs), F32) for _ in range(HEADS)]
    dq = [jnp.zeros((events, hs), F32) for _ in range(HEADS)]
    for k in range(neighbours):
        b = slice(k * events, (k + 1) * events)
        for h in range(HEADS):
            c = slice(h * hs, (h + 1) * hs)
            i = h * 64 + k
            a = att_b[:, i : i + 1]
            d = d_raw[:, i : i + 1]
            mix[h] = mix[h] + a * vp[b, c].astype(F32)
            dq[h] = dq[h] + d * kp[b, c].astype(F32)
            dk[b, c] = (d * qf[:, c]).astype(BF16)
            dv[b, c] = (a * gf[:, c]).astype(BF16)
    q = q_rows[...]
    dq_b = jnp.concatenate(dq, axis=1).astype(BF16)
    emb[...] = (q.astype(F32) + jnp.concatenate(mix, axis=1)).astype(BF16)
    g_qkv[0:m, :] = dot_tn(q, dq_b).astype(BF16)
    g_qkv[m : 2 * m, :] = dot_tn(keys[...], dk[...]).astype(BF16)
    g_qkv[2 * m : 3 * m, :] = dot_tn(keys[...], dv[...]).astype(BF16)
    d_rows = (gf + dot_nt(dq_b, w_query[...])).astype(BF16)
    n = devices * each
    spots = (iota((n, events), 0) == dback[...]).astype(F32).astype(BF16)
    sent = dot(spots, d_rows)
    att_t = att_b.T
    raw_t = d_raw.T
    own = iota((devices, events), 0)
    totals = [jnp.zeros((devices, m), F32) for _ in range(4)]
    for k in range(neighbours):
        onehot = (own == no[k : k + 1, :]).astype(F32).astype(BF16)
        hits = (iota((m, events), 0) == nrank[k : k + 1, :]).astype(F32)
        for j, v in enumerate((raw_t, raw_t, att_t, att_t)):
            i = (j % 2) * 64 + k
            values = (hits * v[i : i + 1, :]).astype(BF16)
            totals[j] = totals[j] + dot_nt(onehot, values)
    for j in range(4):
        spot = iota((n, devices), 0) == iota((n, devices), 1) * each + j
        sent = sent + dot(spot.astype(F32).astype(BF16), totals[j].astype(BF16))
    reply[...] = sent.astype(BF16)


def back_body(
    direct, scal, nrow, qsrc, hots, ge, dq, drow, scol, fcol, rows, feats, code, pre, mean, div,
    upd, rst, cand, rstate, w_in, u_h, w_key, w_value, g_qkv, parity, out, gates, dpre, qe,
):
    n, m = mean.shape[0], rows.shape[1]
    f = feats.shape[1]
    hs = m // HEADS
    step = 256
    s = mean.shape[1]
    if direct:
        qe = qsrc
    else:
        events = hots.shape[1]
        devices = qsrc.shape[0] // events
        cn = hots.shape[0] // devices

        def expand(d, carry):
            b = pl.ds(pl.multiple_of(d * cn, cn), cn)
            e = pl.ds(pl.multiple_of(d * events, events), events)
            qe[b, :] = dot(hots[b, :], qsrc[e, :]).astype(BF16)
            return carry

        lax.fori_loop(0, devices, expand, 0)

    def block(i, carry):
        b = pl.ds(pl.multiple_of(i * step, step), step)
        mine = scol[b, :]
        mine = jnp.where(mine >= 0, mine, -7)
        hit = mine == nrow[...]
        parts = []
        for j in range(4):
            src = qe if j < 2 else ge
            h = j % 2
            a = jnp.where(hit, scal[j : j + 1, :].astype(F32), 0.0).astype(BF16)
            parts.append(dot(a, src[:, h * hs : (h + 1) * hs]).astype(BF16))
        dkey = jnp.concatenate(parts[:2], axis=1)
        dval = jnp.concatenate(parts[2:], axis=1)
        here = (mine == drow[...]).astype(F32).astype(BF16)
        du = dot(here, dq[...]) + dot_nt(dkey, w_key[...]) + dot_nt(dval, w_value[...])
        state = rows[b, :].astype(F32)
        update = upd[b, :]
        reset = rst[b, :]
        candidate = cand[b, :]
        d_cand = (du * update * (1.0 - candidate * candidate)).astype(BF16)
        d_reset = dot_nt(d_cand, u_h[...]) * state * reset * (1.0 - reset)
        d_update = du * (candidate - state) * update * (1.0 - update)
        d_gates = jnp.concatenate([d_update.astype(BF16), d_reset.astype(BF16), d_cand], axis=1)
        d_mean = dot_nt(d_gates, w_in[...]) / div[b, :]
        act = pre[b, :]
        sg = sigmoid(act)
        dpre[b, :] = (d_mean * sg * (1.0 + act * (1.0 - sg))).astype(BF16)
        gates[b, :] = jnp.where(fcol[b, :] > 0.5, d_gates.astype(F32), 0.0).astype(BF16)
        return carry

    lax.fori_loop(0, n // step, block, 0)
    half = out.shape[1]
    me = parity[0, 0]
    at = [0]

    def put(value):
        start, size = at[0], value.shape[0]
        low = max(0, min(size, half - start))
        if low:
            out[me, start : start + low, :] = value[:low, :].astype(BF16)
        if low < size:
            out[1 - me, start + low - half : start + size - half, :] = value[low:, :].astype(BF16)
        at[0] = start + size

    def put_cols(value):
        for j in range(value.shape[1] // 128):
            put(value[:, j * 128 : (j + 1) * 128])

    state_rows = rows[:n, :]
    put_cols(dot_tn(mean[...], gates[...]))
    put_cols(dot_tn(state_rows, gates[:, : 2 * m]))
    put_cols(dot_tn(rstate[...], gates[:, 2 * m :]))
    put_cols(dot_tn(state_rows, dpre[...]))
    put_cols(dot_tn(feats[...], dpre[...]))
    put_cols(dot_tn(code[...], dpre[...]))
    for j in range(3):
        put_cols(g_qkv[j * m : (j + 1) * m, :].astype(F32))


def spread_body(x, out):
    total = x[0].astype(F32)
    for i in range(1, x.shape[0]):
        total = total + x[i].astype(F32)
    total = total.astype(BF16)
    for i in range(x.shape[0]):
        out[i] = total


def unpack_body(mine, other, parity, g_in, g_zr, g_h, g_msg, g_q, g_k, g_v):
    half = mine.shape[0]
    even = parity[0, 0] == 0
    at = [0]

    def take(ref, r, c, size):
        start = at[0]
        low = max(0, min(size, half - start))
        if low:
            b = slice(start, start + low)
            ref[r : r + low, c : c + 128] = jnp.where(even, mine[b, :], other[b, :]).astype(F32)
        if low < size:
            b = slice(start + low - half, start + size - half)
            ref[r + low : r + size, c : c + 128] = jnp.where(
                even, other[b, :], mine[b, :]
            ).astype(F32)
        at[0] = start + size

    for ref in (g_in, g_zr, g_h, g_msg, g_q, g_k, g_v):
        for c in range(0, ref.shape[1], 128):
            take(ref, 0, c, ref.shape[0])


def exchange(x):
    return lax.all_to_all(x, AXES, split_axis=0, concat_axis=0, tiled=True)


def body(
    memory, features, buckets, src_owner, src_slot, dst_owner, dst_slot, nb_owner, nb_slot,
    w_msg, w_in, u_zr, u_h, w_query, w_key, w_value, emb_grad,
):
    devices = lax.axis_size(AXES)
    events, m = emb_grad.shape
    acc_rows = memory.shape[0]
    neighbours = nb_slot.shape[1]
    feat = features.shape[1]
    width = w_msg.shape[1]
    ce = 2 * events // devices
    cn = 2 * events * neighbours // devices
    n_dst = devices * ce
    n_side = 2 * n_dst
    n_nb = devices * cn
    grad_all = lax.all_gather(emb_grad, AXES, axis=0, tiled=True)
    no = nb_owner.reshape(events, neighbours).T
    req, side_feats, dplace, nrank = call(
        functools.partial(place_body, ce, cn, devices),
        [
            ((devices, 4 * ce + cn), I32),
            ((n_side, feat), BF16),
            ((1, events), I32),
            ((neighbours, events), I32),
        ],
        (
            src_owner.reshape(1, events), src_slot.reshape(1, events),
            dst_owner.reshape(1, events), dst_slot.reshape(1, events),
            no, nb_slot.T, buckets.reshape(1, events), features,
        ),
        "place",
    )
    got = exchange(req.reshape(devices, 1, 4 * ce + cn)).reshape(devices, 4 * ce + cn)
    got_feats = exchange(side_feats.reshape(devices, 2 * ce, feat)).reshape(n_side, feat)
    vm = pl.BlockSpec(memory_space=pltpu.VMEM)
    sm = pl.BlockSpec(memory_space=pltpu.SMEM)
    shift = events.bit_length() - 1
    assert 1 << shift == events
    owner_outs = [
        ((n_side, m), BF16), ((n_dst, m), BF16), ((n_nb, m), BF16), ((n_side, m), BF16),
        ((1, n_side), I32), ((n_side, 1), I32), ((n_side, 1), F32),
        ((n_side, w_msg.shape[0] - m - feat), BF16),
        ((n_side, width), F32), ((n_side, width), BF16), ((n_side, width), F32),
        ((n_side, m), F32), ((n_side, m), F32), ((n_side, m), F32), ((n_side, m), BF16),
    ]
    (
        new_side, dst_new, nb_reply, fetched, sfirst, scol, fcol, code, pre, mean, div,
        upd, rst, cand, rstate,
    ) = pl.pallas_call(
        functools.partial(owner_body, ce, cn, shift),
        out_shape=[jax.ShapeDtypeStruct(a, d) for a, d in owner_outs],
        in_specs=[vm, vm, vm, sm, vm, vm, vm, vm],
        out_specs=[vm] * len(owner_outs),
        scratch_shapes=[
            pltpu.VMEM((n_side, width), BF16), pltpu.VMEM((n_side, 1), F32),
            pltpu.VMEM((acc_rows + 8, m), F32), pltpu.VMEM((n_side, m), F32),
            pltpu.VMEM((n_nb, m), F32),
        ],
        compiler_params=pltpu.CompilerParams(vmem_limit_bytes=VMEM_LIMIT),
        name="owner",
    )(memory, got_feats, got, got, w_msg, w_in, u_zr, u_h)
    back_dst = exchange(dst_new.reshape(devices, ce, m)).reshape(n_dst, m)
    back_nb = exchange(nb_reply.reshape(devices, cn, m))
    q_rows, q_proj = call(
        query_body,
        [((events, m), BF16), ((events, m), BF16)],
        (back_dst, dplace, w_query),
        "query",
    )
    proj_all = lax.all_gather(q_proj, AXES, axis=0, tiled=True)
    each = max(2 * ce, -(-(ce + 4) // 8) * 8)
    late_got, _ = lax.optimization_barrier((got, nb_reply))
    new_memory = refresh(memory, sfirst, new_side)
    late_code = late_got[:, 4 * ce :].reshape(n_nb)
    table = jnp.maximum(late_code, 0) % events + jnp.arange(n_nb, dtype=I32) // cn * events
    ge = grad_all[table]
    nrow = (late_code // events).reshape(1, n_nb)
    drow = jnp.concatenate(
        [jnp.full((devices, each - ce), -1, I32), late_got[:, ce : 2 * ce]], axis=1
    ).reshape(1, devices * each)
    hots = hot(events, ce, cn, late_got, n_nb)
    nb_place = (no * cn + nrank).reshape(-1)
    back_nb, new_memory, ge, nrow, drow, hots, nb_place, q_rows = lax.optimization_barrier(
        (back_nb, new_memory, ge, nrow, drow, hots, nb_place, q_rows)
    )
    keys = back_nb.reshape(n_nb, m)[nb_place]
    dback = dplace // ce * each + (each - ce) + dplace % ce
    embedding, reply, g_qkv = call(
        functools.partial(attend_body, cn, devices, each),
        [((events, m), BF16), ((devices * each, m), BF16), ((3 * m, m), BF16)],
        (keys, q_rows, q_proj, emb_grad, w_query, w_key, w_value, dback, no, nrank),
        "attend",
        scratch=[pltpu.VMEM((events * neighbours, m), BF16)] * 4,
    )
    back = exchange(reply.reshape(devices, each, m))
    scal = back[:, :4, :cn].transpose(1, 0, 2).reshape(4, n_nb)
    direct = cn % 16 != 0
    index = lax.axis_index(AXES)
    parity = (index % 2).astype(I32).reshape(1, 1)
    total_rows = (w_msg.size + w_in.size + u_zr.size + u_h.size + 3 * w_query.size) // 128
    half = total_rows // 2
    args = (
        scal, nrow, proj_all[table] if direct else proj_all, hots, ge,
        back.reshape(devices * each, m), drow, scol, fcol, fetched,
        got_feats, code, pre, mean, div, upd, rst, cand, rstate, w_in, u_h, w_key, w_value,
        g_qkv, parity,
    )
    halves = pl.pallas_call(
        functools.partial(back_body, direct),
        out_shape=jax.ShapeDtypeStruct((2, half, 128), BF16),
        in_specs=[vm] * (len(args) - 1) + [sm],
        out_specs=vm,
        scratch_shapes=[
            pltpu.VMEM((n_side, 3 * m), BF16), pltpu.VMEM((n_side, width), BF16),
            pltpu.VMEM((n_nb, m), BF16),
        ],
        compiler_params=pltpu.CompilerParams(vmem_limit_bytes=VMEM_LIMIT),
        name="back",
    )(*args)
    pairs = [(i, i ^ 1) for i in range(devices)]
    teams = [[i for i in range(devices) if i % 2 == p] for p in range(2)]
    size = devices // 2
    keep, send = halves[0], halves[1]
    half_sum = (
        keep.astype(F32) + lax.ppermute(send, AXES, pairs).astype(F32)
    ).astype(BF16).reshape(size, half // size, 128)
    shares = lax.all_to_all(
        half_sum, AXES, split_axis=0, concat_axis=0, tiled=True, axis_index_groups=teams
    )
    spread = call(spread_body, [(shares.shape, BF16)], (shares,), "spread")[0]
    mine = lax.all_to_all(
        spread, AXES, split_axis=0, concat_axis=0, tiled=True, axis_index_groups=teams
    ).reshape(half, 128)
    other = lax.ppermute(mine, AXES, pairs)
    outs = [
        ((width, 3 * m), F32), ((m, 2 * m), F32), ((m, m), F32),
        ((w_msg.shape[0], width), F32), ((m, m), F32), ((m, m), F32), ((m, m), F32),
    ]
    g_in, g_zr, g_h, g_msg, g_q, g_k, g_v = pl.pallas_call(
        unpack_body,
        out_shape=[jax.ShapeDtypeStruct(a, d) for a, d in outs],
        in_specs=[vm, vm, sm],
        out_specs=[vm] * len(outs),
        name="unpack",
    )(mine, other, parity)
    return (new_memory, embedding, g_msg, g_in, g_zr, g_h, g_q, g_k, g_v)


def solution(mesh):
    split = P(AXES)
    return jax.shard_map(
        body,
        mesh=mesh,
        in_specs=(split,) * 9 + (P(),) * 7 + (split,),
        out_specs=(split, split) + (P(),) * 7,
        check_vma=False,
    )
```

```python
import functools
import math

import jax
import jax.numpy as jnp
from jax import lax
from jax.experimental import pallas as pl
from jax.experimental.pallas import tpu as pltpu
from jax.sharding import PartitionSpec as P

HEADS = 2
AXES = ("acct", "rep")
CAP_VALUE = 10.0
F32 = jnp.float32
BF16 = jnp.bfloat16
I32 = jnp.int32
EXACT = lax.Precision.HIGHEST

def room(mib):
    return pltpu.CompilerParams(vmem_limit_bytes=mib * 1024 * 1024)


def dot(a, b, **kw):
    return jnp.dot(a, b, preferred_element_type=F32, **kw)


def dot_nt(a, b, **kw):
    return lax.dot_general(a, b, (((1,), (1,)), ((), ())), preferred_element_type=F32, **kw)


def dot_tn(a, b, **kw):
    return lax.dot_general(a, b, (((0,), (0,)), ((), ())), preferred_element_type=F32, **kw)


def iota(shape, axis):
    return lax.broadcasted_iota(I32, shape, axis)


def to_col(table, n, per, lane0, base=0):
    devices, lanes = table.shape
    pick = ((iota((n, devices), 0) + base) // per == iota((n, devices), 1)).astype(F32)
    spread = dot(pick, table, precision=EXACT)
    r = iota((n, lanes), 0) + base
    at = iota((n, lanes), 1) == lane0 + r - r // per * per
    return jnp.sum(jnp.where(at, spread, 0.0), axis=1, keepdims=True)


def to_row(table, n, per, lane0):
    devices, lanes = table.shape
    c = iota((lanes, n), 1)
    pick = (iota((lanes, n), 0) == lane0 + c - c // per * per).astype(F32)
    spread = dot(table, pick, precision=EXACT)
    mine = iota((devices, n), 0) == iota((devices, n), 1) // per
    return jnp.sum(jnp.where(mine, spread, 0.0), axis=0, keepdims=True)


def sigmoid(v):
    return 1.0 / (1.0 + jnp.exp(-v))


def call(body, outs, args, name, mib, scratch=()):
    vm = pl.BlockSpec(memory_space=pltpu.VMEM)
    return pl.pallas_call(
        body,
        out_shape=[jax.ShapeDtypeStruct(s, d) for s, d in outs],
        in_specs=[vm] * len(args),
        out_specs=[vm] * len(outs),
        scratch_shapes=list(scratch),
        compiler_params=room(mib),
        name=name,
    )(*args)


def place_body(ce, cn, devices, so, ss, do, ds, no, ns, bk, feat, req, feats, dplace, nrank):
    events = so.shape[1]
    neighbours = no.shape[0]
    upper = (iota((events, events), 0) < iota((events, events), 1)).astype(BF16)
    own = iota((devices, events), 0)
    rows = iota((2 * devices * ce, events), 0)

    def fill(onehot, rank, value, cap):
        hits = (iota((cap, events), 0) == rank).astype(F32)
        return dot_nt(onehot, hits * value.astype(F32), precision=EXACT)

    chosen = jnp.zeros((2 * devices * ce, events), F32)
    for side, (o_ref, s_ref) in enumerate(((so, ss), (do, ds))):
        owner = o_ref[...]
        onehot = (own == owner).astype(F32)
        before = dot(onehot.astype(BF16), upper)
        rank = jnp.sum(onehot * before, axis=0, keepdims=True).astype(I32)
        req[:, side * ce : (side + 1) * ce] = (
            fill(onehot, rank, s_ref[...] + 1, ce).astype(I32) - 1
        )
        req[:, (2 + side) * ce : (3 + side) * ce] = fill(onehot, rank, bk[...], ce).astype(I32)
        chosen = chosen + (rows == owner * (2 * ce) + (side * ce + rank)).astype(F32)
        if side == 1:
            dplace[...] = owner * ce + rank
    feats[...] = dot(chosen.astype(BF16), feat[...]).astype(BF16)
    base = jnp.zeros((devices, 1), F32)
    total = jnp.zeros((devices, cn), F32)
    event = iota((1, events), 1)
    for k in range(neighbours):
        onehot = (own == no[k : k + 1, :]).astype(F32)
        before = dot(onehot.astype(BF16), upper) + base
        rank = jnp.sum(onehot * before, axis=0, keepdims=True).astype(I32)
        nrank[k : k + 1, :] = rank
        base = base + jnp.sum(onehot, axis=1, keepdims=True)
        total = total + fill(onehot, rank, ns[k : k + 1, :] * events + event + 1, cn)
    req[:, 4 * ce : 4 * ce + cn] = total.astype(I32) - 1


def widen_rows(source, target):
    step = 256

    def run(i, carry):
        b = pl.ds(pl.multiple_of(i * step, step), step)
        target[b, :] = source[b, :].astype(F32)
        return carry

    lax.fori_loop(0, source.shape[0] // step, run, 0)


def pick_rows(table, target, slots_s, first, count, read):
    rows = math.lcm(count, 8)
    sources = rows // count

    def block(i, carry):
        for g in range(rows // 8):
            found = []
            for r in range(g * 8, g * 8 + 8):
                where = read(slots_s[i * sources + r // count, first + r % count])
                found.append(table[pl.ds(where, 1), :])
            base = pl.multiple_of(i * rows + g * 8, 8)
            target[pl.ds(base, 8), :] = jnp.concatenate(found, axis=0)
        return carry

    lax.fori_loop(0, slots_s.shape[0] // sources, block, 0)


def sides_body(ce, memory, slots_s, rows, table, wide):
    widen_rows(memory, table)
    pick_rows(table, wide, slots_s, 0, 2 * ce, lambda v: jnp.maximum(v, 0))
    rows[...] = wide[...].astype(BF16)


def answer_body(ce, cn, shift, memory, new, slots_s, reply, table, wide, copied):
    acc_rows = memory.shape[0]
    widen_rows(memory, table)
    wide[...] = new[...].astype(F32)

    each = 2 * ce
    rows = math.lcm(each, 8)
    sources = rows // each

    def store(i, carry):
        fresh = wide[pl.ds(pl.multiple_of(i * rows, rows), rows), :]
        for r in range(rows):
            slot = slots_s[i * sources + r // each, r % each]
            slot = jnp.where(slot >= 0, slot, acc_rows)
            table[pl.ds(slot, 1), :] = fresh[r : r + 1, :]
        return carry

    lax.fori_loop(0, slots_s.shape[0] // sources, store, 0)
    pick_rows(
        table, copied, slots_s, 4 * ce, cn,
        lambda v: lax.shift_right_logical(jnp.maximum(v, 0), shift),
    )
    reply[...] = copied[...].astype(BF16)


def owner_body(
    ce, rows, feats, got, w_msg, w_in, u_zr, u_h,
    new, dst_new, sfirst, scol, fcol, code, pre, mean, div, upd, rst, cand, rstate, msg, bcol,
):
    n, f = feats.shape
    m = rows.shape[1]
    t = w_msg.shape[0] - m - f
    step = 128
    frequency = jnp.exp(iota((1, t), 1).astype(F32) * (-11.5 / t))
    numbers = got[:, : 4 * ce].astype(F32)
    scol[...] = to_col(numbers, n, 2 * ce, 0).astype(I32)
    bcol[...] = to_col(numbers, n, 2 * ce, 2 * ce)
    slots = to_row(numbers, n, 2 * ce, 0).astype(I32)

    def messages(i, carry):
        b = pl.ds(pl.multiple_of(i * step, step), step)
        enc = jnp.cos(bcol[b, :] * frequency).astype(BF16)
        code[b, :] = enc
        act = (
            dot(rows[b, :], w_msg[:m, :]) + dot(feats[b, :], w_msg[m : m + f, :])
        ) + dot(enc, w_msg[m + f :, :])
        pre[b, :] = act
        msg[b, :] = (act * sigmoid(act)).astype(BF16)
        return carry

    lax.fori_loop(0, n // step, messages, 0)
    def gru(i, early):
        b = pl.ds(pl.multiple_of(i * step, step), step)
        mine = scol[b, :]
        same = (mine == slots) & (mine >= 0)
        eq = same.astype(F32)
        eq_b = eq.astype(BF16)
        counts = dot(eq_b, jnp.ones((n, msg.shape[1]), BF16))
        divisor = jnp.maximum(counts, 1.0)
        div[b, :] = divisor
        earlier = jnp.where(iota((step, n), 1) < iota((step, n), 0) + i * step, eq, 0.0)
        fcol[b, :] = (jnp.sum(earlier, axis=1, keepdims=True) < 0.5).astype(F32)
        later = jnp.where(iota((step, n), 1) > iota((step, n), 0) + i * step, eq, 0.0)
        early = early + jnp.sum(later, axis=0, keepdims=True)
        mean_b = (dot(eq_b, msg[...]) / divisor).astype(BF16)
        mean[b, :] = mean_b
        state = rows[b, :]
        state_wide = state.astype(F32)
        from_input = dot(mean_b, w_in[...])
        from_state = dot(state, u_zr[...])
        update = sigmoid(from_input[:, :m] + from_state[:, :m])
        reset = sigmoid(from_input[:, m : 2 * m] + from_state[:, m:])
        reset_state = (reset * state_wide).astype(BF16)
        candidate = jnp.tanh(from_input[:, 2 * m :] + dot(reset_state, u_h[...]))
        upd[b, :] = update
        rst[b, :] = reset
        cand[b, :] = candidate
        rstate[b, :] = reset_state
        new[b, :] = ((1.0 - update) * state_wide + update * candidate).astype(BF16)
        return early

    early = lax.fori_loop(0, n // step, gru, jnp.zeros((1, n), F32))
    sfirst[...] = jnp.where((early < 0.5) & (slots >= 0), slots, -2)
    half = n // 2
    r = iota((half, n), 0)
    pick = (iota((half, n), 1) == r + (r // ce + 1) * ce).astype(F32).astype(BF16)
    dst_new[...] = dot(pick, new[...]).astype(BF16)


def refresh_body(block, old, sfirst, new, out):
    row = iota((block, 1), 0) + pl.program_id(0) * block
    hit = (row == sfirst[...]).astype(F32).astype(BF16)
    rows = dot(hit, new[...])
    found = dot(hit, jnp.ones((new.shape[0], 128), BF16)) > 0.5
    for h in range(rows.shape[1] // 128):
        c = slice(h * 128, (h + 1) * 128)
        out[:, c] = jnp.where(found, rows[:, c], old[:, c].astype(F32)).astype(BF16)


def refresh(memory, sfirst, new):
    n, m = memory.shape
    s = new.shape[0]
    block = 512
    return pl.pallas_call(
        functools.partial(refresh_body, block),
        grid=(n // block,),
        out_shape=jax.ShapeDtypeStruct((n, m), BF16),
        in_specs=[
            pl.BlockSpec((block, m), lambda i: (i, 0)),
            pl.BlockSpec((1, s), lambda i: (0, 0)),
            pl.BlockSpec((s, m), lambda i: (0, 0)),
        ],
        out_specs=pl.BlockSpec((block, m), lambda i: (i, 0)),
        compiler_params=room(8),
        name="refresh",
    )(memory, sfirst, new)


def hot_body(events, ce, cn, block, got, out):
    table = got[:, 4 * ce :].astype(F32)
    code = to_col(table, block, cn, 0, pl.program_id(0) * block).astype(I32)
    event = jnp.where(code >= 0, code % events, -1)
    out[...] = (iota((block, events), 1) == event).astype(F32).astype(BF16)


def hot(events, ce, cn, got, n):
    block = 512
    return pl.pallas_call(
        functools.partial(hot_body, events, ce, cn, block),
        grid=(n // block,),
        out_shape=jax.ShapeDtypeStruct((n, events), BF16),
        in_specs=[pl.BlockSpec(got.shape, lambda i: (0, 0))],
        out_specs=pl.BlockSpec((block, events), lambda i: (i, 0)),
        compiler_params=room(6),
        name="hot",
    )(got)


def query_body(back, dplace, w_query, q_rows, q_proj):
    n = back.shape[0]
    events = dplace.shape[1]
    pick = (iota((n, events), 0) == dplace[...]).astype(F32).astype(BF16)
    q = dot_tn(pick, back[...]).astype(BF16)
    q_rows[...] = q
    q_proj[...] = dot(q, w_query[...]).astype(BF16)


def attend_body(
    cn, devices, each, keys, q_rows, q_proj, grad, w_query, w_key, w_value, dback, no, nrank,
    emb, reply, g_qkv, kp, vp, dk, dv,
):
    events, m = q_rows.shape
    neighbours = no.shape[0]
    hs = m // HEADS
    scaling = 1.0 / math.sqrt(hs)
    qf = q_proj[...].astype(F32)
    gf = grad[...].astype(F32)
    lane = iota((events, 128), 1)
    raw = jnp.zeros((events, 128), F32)
    probs = jnp.zeros((events, 128), F32)
    for k in range(neighbours):
        b = slice(k * events, (k + 1) * events)
        rows = keys[b, :]
        kpk = dot(rows, w_key[...]).astype(BF16)
        vpk = dot(rows, w_value[...]).astype(BF16)
        kp[b, :] = kpk
        vp[b, :] = vpk
        pk = qf * kpk.astype(F32)
        pv = gf * vpk.astype(F32)
        for h in range(HEADS):
            c = slice(h * hs, (h + 1) * hs)
            at = lane == h * 64 + k
            raw = jnp.where(at, jnp.sum(pk[:, c], axis=1, keepdims=True), raw)
            probs = jnp.where(at, jnp.sum(pv[:, c], axis=1, keepdims=True), probs)
    raw = raw * scaling
    capped = jnp.tanh(raw / CAP_VALUE)
    first = lane < 64
    live = jnp.where(first, lane, lane - 64) < neighbours
    weights = jnp.where(live, jnp.exp(CAP_VALUE * capped), 0.0)

    def per_head(v):
        a = jnp.sum(jnp.where(first, v, 0.0), axis=1, keepdims=True)
        b = jnp.sum(jnp.where(first, 0.0, v), axis=1, keepdims=True)
        return jnp.where(first, a, b)

    attention = weights / per_head(weights)
    att_b = attention.astype(BF16).astype(F32)
    d_scores = attention * (probs - per_head(attention * probs))
    d_raw = d_scores * (1.0 - capped * capped) * scaling
    mix = [jnp.zeros((events, hs), F32) for _ in range(HEADS)]
    dq = [jnp.zeros((events, hs), F32) for _ in range(HEADS)]
    for k in range(neighbours):
        b = slice(k * events, (k + 1) * events)
        for h in range(HEADS):
            c = slice(h * hs, (h + 1) * hs)
            i = h * 64 + k
            a = att_b[:, i : i + 1]
            d = d_raw[:, i : i + 1]
            mix[h] = mix[h] + a * vp[b, c].astype(F32)
            dq[h] = dq[h] + d * kp[b, c].astype(F32)
            dk[b, c] = (d * qf[:, c]).astype(BF16)
            dv[b, c] = (a * gf[:, c]).astype(BF16)
    q = q_rows[...]
    dq_b = jnp.concatenate(dq, axis=1).astype(BF16)
    emb[...] = (q.astype(F32) + jnp.concatenate(mix, axis=1)).astype(BF16)
    g_qkv[0:m, :] = dot_tn(q, dq_b).astype(BF16)
    g_qkv[m : 2 * m, :] = dot_tn(keys[...], dk[...]).astype(BF16)
    g_qkv[2 * m : 3 * m, :] = dot_tn(keys[...], dv[...]).astype(BF16)
    d_rows = (gf + dot_nt(dq_b, w_query[...])).astype(BF16)
    n = devices * each
    spots = (iota((n, events), 0) == dback[...]).astype(F32).astype(BF16)
    sent = dot(spots, d_rows)
    att_t = att_b.T
    raw_t = d_raw.T
    own = iota((devices, events), 0)
    totals = [jnp.zeros((devices, m), F32) for _ in range(4)]
    for k in range(neighbours):
        onehot = (own == no[k : k + 1, :]).astype(F32).astype(BF16)
        hits = (iota((m, events), 0) == nrank[k : k + 1, :]).astype(F32)
        for j, v in enumerate((raw_t, raw_t, att_t, att_t)):
            i = (j % 2) * 64 + k
            values = (hits * v[i : i + 1, :]).astype(BF16)
            totals[j] = totals[j] + dot_nt(onehot, values)
    for j in range(4):
        spot = iota((n, devices), 0) == iota((n, devices), 1) * each + j
        sent = sent + dot(spot.astype(F32).astype(BF16), totals[j].astype(BF16))
    reply[...] = sent.astype(BF16)


def expand_body(cn, source, hots, out):
    events = hots.shape[1]

    def run(d, carry):
        b = pl.ds(pl.multiple_of(d * cn, cn), cn)
        e = pl.ds(pl.multiple_of(d * events, events), events)
        out[b, :] = dot(hots[b, :], source[e, :]).astype(BF16)
        return carry

    lax.fori_loop(0, hots.shape[0] // cn, run, 0, unroll=4)


def back_body(
    scal, nrow, qe, ge, dq, drow, scol, fcol, rows, feats, code, pre, mean, div,
    upd, rst, cand, rstate, w_in, u_h, w_key, w_value, g_qkv, parity, keep, send, gates, dpre,
):
    n, m = mean.shape[0], rows.shape[1]
    f = feats.shape[1]
    hs = m // HEADS
    step = 256
    s = mean.shape[1]
    def block(i, carry):
        b = pl.ds(pl.multiple_of(i * step, step), step)
        mine = scol[b, :]
        mine = jnp.where(mine >= 0, mine, -7)
        hit = mine == nrow[...]
        parts = []
        for j in range(4):
            src = qe if j < 2 else ge
            h = j % 2
            a = jnp.where(hit, scal[j : j + 1, :].astype(F32), 0.0).astype(BF16)
            parts.append(dot(a, src[:, h * hs : (h + 1) * hs]).astype(BF16))
        dkey = jnp.concatenate(parts[:2], axis=1)
        dval = jnp.concatenate(parts[2:], axis=1)
        here = (mine == drow[...]).astype(F32).astype(BF16)
        du = dot(here, dq[...]) + dot_nt(dkey, w_key[...]) + dot_nt(dval, w_value[...])
        state = rows[b, :].astype(F32)
        update = upd[b, :]
        reset = rst[b, :]
        candidate = cand[b, :]
        d_cand = (du * update * (1.0 - candidate * candidate)).astype(BF16)
        d_reset = dot_nt(d_cand, u_h[...]) * state * reset * (1.0 - reset)
        d_update = du * (candidate - state) * update * (1.0 - update)
        d_gates = jnp.concatenate([d_update.astype(BF16), d_reset.astype(BF16), d_cand], axis=1)
        d_mean = dot_nt(d_gates, w_in[...]) / div[b, :]
        act = pre[b, :]
        sg = sigmoid(act)
        dpre[b, :] = (d_mean * sg * (1.0 + act * (1.0 - sg))).astype(BF16)
        gates[b, :] = jnp.where(fcol[b, :] > 0.5, d_gates.astype(F32), 0.0).astype(BF16)
        return carry

    lax.fori_loop(0, n // step, block, 0)
    half = keep.shape[0]
    even = parity[0, 0] == 0
    at = [0]

    def put(value):
        start, size = at[0], value.shape[0]
        low = max(0, min(size, half - start))
        pieces = ((value[:low, :], True, start), (value[low:, :], False, start + low - half))
        for part, first, r in pieces:
            if part.shape[0]:
                part = part.astype(BF16)
                b = slice(r, r + part.shape[0])

                @pl.when(even == first)
                def _():
                    keep[b, :] = part

                @pl.when(even != first)
                def _():
                    send[b, :] = part

        at[0] = start + size

    def put_cols(value):
        for j in range(value.shape[1] // 128):
            put(value[:, j * 128 : (j + 1) * 128])

    state_rows = rows[:n, :]
    put_cols(dot_tn(mean[...], gates[...]))
    put_cols(dot_tn(state_rows, gates[:, : 2 * m]))
    put_cols(dot_tn(rstate[...], gates[:, 2 * m :]))
    put_cols(dot_tn(state_rows, dpre[...]))
    put_cols(dot_tn(feats[...], dpre[...]))
    put_cols(dot_tn(code[...], dpre[...]))
    for j in range(3):
        put_cols(g_qkv[j * m : (j + 1) * m, :].astype(F32))


def spread_body(x, out):
    total = x[0].astype(F32)
    for i in range(1, x.shape[0]):
        total = total + x[i].astype(F32)
    total = total.astype(BF16)
    for i in range(x.shape[0]):
        out[i] = total


def unpack_body(mine, other, parity, g_in, g_zr, g_h, g_msg, g_q, g_k, g_v):
    half = mine.shape[0]
    even = parity[0, 0] == 0
    at = [0]

    def take(ref, r, c, size):
        start = at[0]
        low = max(0, min(size, half - start))
        if low:
            b = slice(start, start + low)
            ref[r : r + low, c : c + 128] = jnp.where(even, mine[b, :], other[b, :]).astype(F32)
        if low < size:
            b = slice(start + low - half, start + size - half)
            ref[r + low : r + size, c : c + 128] = jnp.where(
                even, other[b, :], mine[b, :]
            ).astype(F32)
        at[0] = start + size

    for ref in (g_in, g_zr, g_h, g_msg, g_q, g_k, g_v):
        for c in range(0, ref.shape[1], 128):
            take(ref, 0, c, ref.shape[0])


def exchange(x):
    return lax.all_to_all(x, AXES, split_axis=0, concat_axis=0, tiled=True)


def body(
    memory, features, buckets, src_owner, src_slot, dst_owner, dst_slot, nb_owner, nb_slot,
    w_msg, w_in, u_zr, u_h, w_query, w_key, w_value, emb_grad,
):
    devices = lax.axis_size(AXES)
    events, m = emb_grad.shape
    acc_rows = memory.shape[0]
    neighbours = nb_slot.shape[1]
    feat = features.shape[1]
    width = w_msg.shape[1]
    ce = 2 * events // devices
    cn = 2 * events * neighbours // devices
    n_dst = devices * ce
    n_side = 2 * n_dst
    n_nb = devices * cn
    grad_all = lax.all_gather(emb_grad, AXES, axis=0, tiled=True)
    no = nb_owner.reshape(events, neighbours).T
    req, side_feats, dplace, nrank = call(
        functools.partial(place_body, ce, cn, devices),
        [
            ((devices, 4 * ce + cn), I32),
            ((n_side, feat), BF16),
            ((1, events), I32),
            ((neighbours, events), I32),
        ],
        (
            src_owner.reshape(1, events), src_slot.reshape(1, events),
            dst_owner.reshape(1, events), dst_slot.reshape(1, events),
            no, nb_slot.T, buckets.reshape(1, events), features,
        ),
        "place",
        56,
    )
    got = exchange(req.reshape(devices, 1, 4 * ce + cn)).reshape(devices, 4 * ce + cn)
    got_feats = exchange(side_feats.reshape(devices, 2 * ce, feat)).reshape(n_side, feat)
    vm = pl.BlockSpec(memory_space=pltpu.VMEM)
    sm = pl.BlockSpec(memory_space=pltpu.SMEM)
    shift = events.bit_length() - 1
    assert 1 << shift == events
    owner_outs = [
        ((n_side, m), BF16), ((n_dst, m), BF16),
        ((1, n_side), I32), ((n_side, 1), I32), ((n_side, 1), F32),
        ((n_side, w_msg.shape[0] - m - feat), BF16),
        ((n_side, width), F32), ((n_side, width), BF16), ((n_side, width), F32),
        ((n_side, m), F32), ((n_side, m), F32), ((n_side, m), F32), ((n_side, m), BF16),
    ]
    fetched = pl.pallas_call(
        functools.partial(sides_body, ce),
        out_shape=jax.ShapeDtypeStruct((n_side, m), BF16),
        in_specs=[vm, sm],
        out_specs=vm,
        scratch_shapes=[pltpu.VMEM((acc_rows, m), F32), pltpu.VMEM((n_side, m), F32)],
        compiler_params=room(56),
        name="sides",
    )(memory, got)
    (
        new_side, dst_new, sfirst, scol, fcol, code, pre, mean, div, upd, rst, cand, rstate,
    ) = call(
        functools.partial(owner_body, ce),
        owner_outs,
        (fetched, got_feats, got, w_msg, w_in, u_zr, u_h),
        "owner",
        56,
        scratch=[pltpu.VMEM((n_side, width), BF16), pltpu.VMEM((n_side, 1), F32)],
    )
    nb_reply = pl.pallas_call(
        functools.partial(answer_body, ce, cn, shift),
        out_shape=jax.ShapeDtypeStruct((n_nb, m), BF16),
        in_specs=[vm, vm, sm],
        out_specs=vm,
        scratch_shapes=[
            pltpu.VMEM((acc_rows + 8, m), F32), pltpu.VMEM((n_side, m), F32),
            pltpu.VMEM((n_nb, m), F32),
        ],
        compiler_params=room(56),
        name="answer",
    )(memory, new_side, got)
    back_dst = exchange(dst_new.reshape(devices, ce, m)).reshape(n_dst, m)
    back_nb = exchange(nb_reply.reshape(devices, cn, m))
    back_dst, nb_reply = lax.optimization_barrier((back_dst, nb_reply))
    q_rows, q_proj = call(
        query_body,
        [((events, m), BF16), ((events, m), BF16)],
        (back_dst, dplace, w_query),
        "query",
        4,
    )
    proj_all = lax.all_gather(q_proj, AXES, axis=0, tiled=True)
    each = max(2 * ce, -(-(ce + 4) // 8) * 8)
    late_got, _ = lax.optimization_barrier((got, nb_reply))
    new_memory = refresh(memory, sfirst, new_side)
    late_code = late_got[:, 4 * ce :].reshape(n_nb)
    table = jnp.maximum(late_code, 0) % events + jnp.arange(n_nb, dtype=I32) // cn * events
    ge = grad_all[table]
    nrow = (late_code // events).reshape(1, n_nb)
    drow = jnp.concatenate(
        [jnp.full((devices, each - ce), -1, I32), late_got[:, ce : 2 * ce]], axis=1
    ).reshape(1, devices * each)
    hots = hot(events, ce, cn, late_got, n_nb)
    nb_place = (no * cn + nrank).reshape(-1)
    back_nb, new_memory, ge, nrow, drow, hots, nb_place, q_rows = lax.optimization_barrier(
        (back_nb, new_memory, ge, nrow, drow, hots, nb_place, q_rows)
    )
    keys = back_nb.reshape(n_nb, m)[nb_place]
    dback = dplace // ce * each + (each - ce) + dplace % ce
    embedding, reply, g_qkv = call(
        functools.partial(attend_body, cn, devices, each),
        [((events, m), BF16), ((devices * each, m), BF16), ((3 * m, m), BF16)],
        (keys, q_rows, q_proj, emb_grad, w_query, w_key, w_value, dback, no, nrank),
        "attend",
        14,
        scratch=[pltpu.VMEM((events * neighbours, m), BF16)] * 4,
    )
    back = exchange(reply.reshape(devices, each, m))
    if cn % 16:
        qe = proj_all[table]
    else:
        qe = pl.pallas_call(
            functools.partial(expand_body, cn),
            out_shape=jax.ShapeDtypeStruct((n_nb, m), BF16),
            in_specs=[vm, vm],
            out_specs=vm,
            compiler_params=room(8),
            name="expand",
        )(proj_all, hots)
    back, qe = lax.optimization_barrier((back, qe))
    scal = back[:, :4, :cn].transpose(1, 0, 2).reshape(4, n_nb)
    index = lax.axis_index(AXES)
    parity = (index % 2).astype(I32).reshape(1, 1)
    total_rows = (w_msg.size + w_in.size + u_zr.size + u_h.size + 3 * w_query.size) // 128
    half = total_rows // 2
    args = (
        scal, nrow, qe, ge, back.reshape(devices * each, m), drow, scol, fcol, fetched,
        got_feats, code, pre, mean, div, upd, rst, cand, rstate, w_in, u_h, w_key, w_value,
        g_qkv, parity,
    )
    keep, send = pl.pallas_call(
        back_body,
        out_shape=[jax.ShapeDtypeStruct((half, 128), BF16)] * 2,
        in_specs=[vm] * (len(args) - 1) + [sm],
        out_specs=[vm] * 2,
        scratch_shapes=[pltpu.VMEM((n_side, 3 * m), BF16), pltpu.VMEM((n_side, width), BF16)],
        compiler_params=room(56),
        name="back",
    )(*args)
    pairs = [(i, i ^ 1) for i in range(devices)]
    teams = [[i for i in range(devices) if i % 2 == p] for p in range(2)]
    size = devices // 2
    half_sum = (
        keep.astype(F32) + lax.ppermute(send, AXES, pairs).astype(F32)
    ).astype(BF16).reshape(size, half // size, 128)
    shares = lax.all_to_all(
        half_sum, AXES, split_axis=0, concat_axis=0, tiled=True, axis_index_groups=teams
    )
    spread = call(spread_body, [(shares.shape, BF16)], (shares,), "spread", 6)[0]
    mine = lax.all_to_all(
        spread, AXES, split_axis=0, concat_axis=0, tiled=True, axis_index_groups=teams
    ).reshape(half, 128)
    other = lax.ppermute(mine, AXES, pairs)
    outs = [
        ((width, 3 * m), F32), ((m, 2 * m), F32), ((m, m), F32),
        ((w_msg.shape[0], width), F32), ((m, m), F32), ((m, m), F32), ((m, m), F32),
    ]
    g_in, g_zr, g_h, g_msg, g_q, g_k, g_v = pl.pallas_call(
        unpack_body,
        out_shape=[jax.ShapeDtypeStruct(a, d) for a, d in outs],
        in_specs=[vm, vm, sm],
        out_specs=[vm] * len(outs),
        compiler_params=room(8),
        name="unpack",
    )(mine, other, parity)
    return (new_memory, embedding, g_msg, g_in, g_zr, g_h, g_q, g_k, g_v)


def solution(mesh):
    split = P(AXES)
    return jax.shard_map(
        body,
        mesh=mesh,
        in_specs=(split,) * 9 + (P(),) * 7 + (split,),
        out_specs=(split, split) + (P(),) * 7,
        check_vma=False,
    )
```

```python
import functools
import math

import jax
import jax.numpy as jnp
from jax import lax
from jax.experimental import pallas as pl
from jax.experimental.pallas import tpu as pltpu
from jax.sharding import PartitionSpec as P

HEADS = 2
AXES = ("acct", "rep")
CAP_VALUE = 10.0
F32 = jnp.float32
BF16 = jnp.bfloat16
I32 = jnp.int32
EXACT = lax.Precision.HIGHEST

def room(mib):
    return pltpu.CompilerParams(vmem_limit_bytes=mib * 1024 * 1024)


def dot(a, b, **kw):
    return jnp.dot(a, b, preferred_element_type=F32, **kw)


def dot_nt(a, b, **kw):
    return lax.dot_general(a, b, (((1,), (1,)), ((), ())), preferred_element_type=F32, **kw)


def dot_tn(a, b, **kw):
    return lax.dot_general(a, b, (((0,), (0,)), ((), ())), preferred_element_type=F32, **kw)


def iota(shape, axis):
    return lax.broadcasted_iota(I32, shape, axis)


def to_col(table, n, per, lane0, base=0):
    devices, lanes = table.shape
    pick = ((iota((n, devices), 0) + base) // per == iota((n, devices), 1)).astype(F32)
    spread = dot(pick, table, precision=EXACT)
    r = iota((n, lanes), 0) + base
    at = iota((n, lanes), 1) == lane0 + r - r // per * per
    return jnp.sum(jnp.where(at, spread, 0.0), axis=1, keepdims=True)


def to_row(table, n, per, lane0):
    devices, lanes = table.shape
    c = iota((lanes, n), 1)
    pick = (iota((lanes, n), 0) == lane0 + c - c // per * per).astype(F32)
    spread = dot(table, pick, precision=EXACT)
    mine = iota((devices, n), 0) == iota((devices, n), 1) // per
    return jnp.sum(jnp.where(mine, spread, 0.0), axis=0, keepdims=True)


def sigmoid(v):
    return 1.0 / (1.0 + jnp.exp(-v))


def call(body, outs, args, name, mib, scratch=(), scalars=0):
    vm = pl.BlockSpec(memory_space=pltpu.VMEM)
    sm = pl.BlockSpec(memory_space=pltpu.SMEM)
    return pl.pallas_call(
        body,
        out_shape=[jax.ShapeDtypeStruct(s, d) for s, d in outs],
        in_specs=[vm] * (len(args) - scalars) + [sm] * scalars,
        out_specs=[vm] * len(outs),
        scratch_shapes=list(scratch),
        compiler_params=room(mib),
        name=name,
    )(*args)


def place_body(ce, cn, devices, so, ss, do, ds, no, ns, bk, feat, req, feats, dplace, nrank):
    events = so.shape[1]
    neighbours = no.shape[0]
    upper = (iota((events, events), 0) < iota((events, events), 1)).astype(BF16)
    own = iota((devices, events), 0)
    rows = iota((2 * devices * ce, events), 0)

    def fill(onehot, rank, value, cap):
        hits = (iota((cap, events), 0) == rank).astype(F32)
        owner_b = onehot.astype(BF16)
        high = dot_nt(owner_b, (hits * (value >> 7).astype(F32)).astype(BF16))
        low = dot_nt(owner_b, (hits * (value & 127).astype(F32)).astype(BF16))
        return high * 128.0 + low

    chosen = jnp.zeros((2 * devices * ce, events), F32)
    for side, (o_ref, s_ref) in enumerate(((so, ss), (do, ds))):
        owner = o_ref[...]
        onehot = (own == owner).astype(F32)
        before = dot(onehot.astype(BF16), upper)
        rank = jnp.sum(onehot * before, axis=0, keepdims=True).astype(I32)
        req[:, side * ce : (side + 1) * ce] = (
            fill(onehot, rank, s_ref[...] + 1, ce).astype(I32) - 1
        )
        req[:, (2 + side) * ce : (3 + side) * ce] = fill(onehot, rank, bk[...], ce).astype(I32)
        chosen = chosen + (rows == owner * (2 * ce) + (side * ce + rank)).astype(F32)
        if side == 1:
            dplace[...] = owner * ce + rank
    feats[...] = dot(chosen.astype(BF16), feat[...]).astype(BF16)
    base = jnp.zeros((devices, 1), F32)
    slots = jnp.zeros((devices, cn), F32)
    which = jnp.zeros((devices, cn), F32)
    event = iota((1, events), 1)
    for k in range(neighbours):
        onehot = (own == no[k : k + 1, :]).astype(F32)
        before = dot(onehot.astype(BF16), upper) + base
        rank = jnp.sum(onehot * before, axis=0, keepdims=True).astype(I32)
        nrank[k : k + 1, :] = rank
        base = base + jnp.sum(onehot, axis=1, keepdims=True)
        slots = slots + fill(onehot, rank, ns[k : k + 1, :], cn)
        which = which + fill(onehot, rank, event + 1, cn)
    req[:, 4 * ce : 4 * ce + cn] = slots.astype(I32)
    req[:, 4 * ce + cn :] = which.astype(I32) - 1


def widen_rows(source, target):
    step = 256

    def run(i, carry):
        b = pl.ds(pl.multiple_of(i * step, step), step)
        for h in range(target.shape[0]):
            target[h, b, :] = source[b, h * 128 : (h + 1) * 128].astype(F32)
        return carry

    lax.fori_loop(0, source.shape[0] // step, run, 0)


def narrow_rows(source, target):
    for h in range(source.shape[0]):
        target[:, h * 128 : (h + 1) * 128] = source[h].astype(BF16)


def pick_rows(table, target, slots_s, first, count, read):
    rows = math.lcm(count, 8)
    sources = rows // count

    def block(i, carry):
        for g in range(rows // 8):
            where = [
                read(slots_s[i * sources + r // count, first + r % count])
                for r in range(g * 8, g * 8 + 8)
            ]
            base = pl.multiple_of(i * rows + g * 8, 8)
            for h in range(table.shape[0]):
                found = [table[h, pl.ds(w, 1), :] for w in where]
                target[h, pl.ds(base, 8), :] = jnp.concatenate(found, axis=0)
        return carry

    lax.fori_loop(0, slots_s.shape[0] // sources, block, 0)


def sides_body(ce, memory, slots_s, rows, table, wide):
    widen_rows(memory, table)
    pick_rows(table, wide, slots_s, 0, 2 * ce, lambda v: jnp.maximum(v, 0))
    narrow_rows(wide, rows)


def answer_body(ce, cn, memory, new, slots_s, reply, table, wide, copied):
    acc_rows = memory.shape[0]
    widen_rows(memory, table)
    widen_rows(new, wide)

    each = 2 * ce
    rows = math.lcm(each, 8)
    sources = rows // each

    def store(i, carry):
        fresh = [
            wide[h, pl.ds(pl.multiple_of(i * rows, rows), rows), :] for h in range(wide.shape[0])
        ]
        for r in range(rows):
            slot = slots_s[i * sources + r // each, r % each]
            slot = jnp.where(slot >= 0, slot, acc_rows)
            for h in range(wide.shape[0]):
                table[h, pl.ds(slot, 1), :] = fresh[h][r : r + 1, :]
        return carry

    lax.fori_loop(0, slots_s.shape[0] // sources, store, 0)
    pick_rows(table, copied, slots_s, 4 * ce, cn, lambda v: v)
    narrow_rows(copied, reply)


def owner_body(
    ce, rows, feats, got, w_msg, w_in, u_zr, u_h,
    new, dst_new, sfirst, scol, fcol, code, pre, mean, div, upd, rst, cand, rstate, msg, bcol,
):
    n, f = feats.shape
    m = rows.shape[1]
    t = w_msg.shape[0] - m - f
    step = 128
    frequency = jnp.exp(iota((1, t), 1).astype(F32) * (-11.5 / t))
    numbers = got[:, : 4 * ce].astype(F32)
    scol[...] = to_col(numbers, n, 2 * ce, 0).astype(I32)
    bcol[...] = to_col(numbers, n, 2 * ce, 2 * ce)
    slots = to_row(numbers, n, 2 * ce, 0).astype(I32)

    def messages(i, carry):
        b = pl.ds(pl.multiple_of(i * step, step), step)
        enc = jnp.cos(bcol[b, :] * frequency).astype(BF16)
        code[b, :] = enc
        act = (
            dot(rows[b, :], w_msg[:m, :]) + dot(feats[b, :], w_msg[m : m + f, :])
        ) + dot(enc, w_msg[m + f :, :])
        pre[b, :] = act
        msg[b, :] = (act * sigmoid(act)).astype(BF16)
        return carry

    lax.fori_loop(0, n // step, messages, 0)
    def gru(i, early):
        b = pl.ds(pl.multiple_of(i * step, step), step)
        mine = scol[b, :]
        same = (mine == slots) & (mine >= 0)
        eq = same.astype(F32)
        eq_b = eq.astype(BF16)
        counts = dot(eq_b, jnp.ones((n, msg.shape[1]), BF16))
        divisor = jnp.maximum(counts, 1.0)
        div[b, :] = divisor
        earlier = jnp.where(iota((step, n), 1) < iota((step, n), 0) + i * step, eq, 0.0)
        fcol[b, :] = (jnp.sum(earlier, axis=1, keepdims=True) < 0.5).astype(F32)
        later = jnp.where(iota((step, n), 1) > iota((step, n), 0) + i * step, eq, 0.0)
        early = early + jnp.sum(later, axis=0, keepdims=True)
        mean_b = (dot(eq_b, msg[...]) / divisor).astype(BF16)
        mean[b, :] = mean_b
        state = rows[b, :]
        state_wide = state.astype(F32)
        from_input = dot(mean_b, w_in[...])
        from_state = dot(state, u_zr[...])
        update = sigmoid(from_input[:, :m] + from_state[:, :m])
        reset = sigmoid(from_input[:, m : 2 * m] + from_state[:, m:])
        reset_state = (reset * state_wide).astype(BF16)
        candidate = jnp.tanh(from_input[:, 2 * m :] + dot(reset_state, u_h[...]))
        upd[b, :] = update
        rst[b, :] = reset
        cand[b, :] = candidate
        rstate[b, :] = reset_state
        new[b, :] = ((1.0 - update) * state_wide + update * candidate).astype(BF16)
        return early

    early = lax.fori_loop(0, n // step, gru, jnp.zeros((1, n), F32))
    sfirst[...] = jnp.where((early < 0.5) & (slots >= 0), slots, -2)
    half = n // 2
    r = iota((half, n), 0)
    pick = (iota((half, n), 1) == r + (r // ce + 1) * ce).astype(F32).astype(BF16)
    dst_new[...] = dot(pick, new[...]).astype(BF16)


def refresh_body(block, old, sfirst, new, out):
    row = iota((block, 1), 0) + pl.program_id(0) * block
    hit = (row == sfirst[...]).astype(F32).astype(BF16)
    rows = dot(hit, new[...])
    found = dot(hit, jnp.ones((new.shape[0], 128), BF16)) > 0.5
    for h in range(rows.shape[1] // 128):
        c = slice(h * 128, (h + 1) * 128)
        out[:, c] = jnp.where(found, rows[:, c], old[:, c].astype(F32)).astype(BF16)


def refresh(memory, sfirst, new):
    n, m = memory.shape
    s = new.shape[0]
    block = 512
    return pl.pallas_call(
        functools.partial(refresh_body, block),
        grid=(n // block,),
        out_shape=jax.ShapeDtypeStruct((n, m), BF16),
        in_specs=[
            pl.BlockSpec((block, m), lambda i: (i, 0)),
            pl.BlockSpec((1, s), lambda i: (0, 0)),
            pl.BlockSpec((s, m), lambda i: (0, 0)),
        ],
        out_specs=pl.BlockSpec((block, m), lambda i: (i, 0)),
        compiler_params=room(8),
        name="refresh",
    )(memory, sfirst, new)


def hot_body(events, ce, cn, block, got, out):
    table = got[:, 4 * ce + cn :].astype(F32)
    event = to_col(table, block, cn, 0, pl.program_id(0) * block).astype(I32)
    out[...] = (iota((block, events), 1) == event).astype(F32).astype(BF16)


def hot(events, ce, cn, got, n):
    block = 512
    return pl.pallas_call(
        functools.partial(hot_body, events, ce, cn, block),
        grid=(n // block,),
        out_shape=jax.ShapeDtypeStruct((n, events), BF16),
        in_specs=[pl.BlockSpec(got.shape, lambda i: (0, 0))],
        out_specs=pl.BlockSpec((block, events), lambda i: (i, 0)),
        compiler_params=room(6),
        name="hot",
    )(got)


def query_body(back, dplace, w_query, q_rows, q_proj):
    n = back.shape[0]
    events = dplace.shape[1]
    pick = (iota((n, events), 0) == dplace[...]).astype(F32).astype(BF16)
    q = dot_tn(pick, back[...]).astype(BF16)
    q_rows[...] = q
    q_proj[...] = dot(q, w_query[...]).astype(BF16)


def attend_body(
    cn, devices, each, back, q_rows, q_proj, grad, w_query, w_key, w_value, dback, no, nrank, places,
    emb, reply, g_qkv, kp, vp, dk, dv, keys, wide, picked,
):
    events, m = q_rows.shape
    neighbours = no.shape[0]
    hs = m // HEADS
    scaling = 1.0 / math.sqrt(hs)
    widen_rows(back, wide)
    pick_rows(wide, picked, places, 0, events, lambda v: v)
    narrow_rows(picked, keys)
    qf = q_proj[...].astype(F32)
    gf = grad[...].astype(F32)
    lane = iota((events, 128), 1)
    raw = jnp.zeros((events, 128), F32)
    probs = jnp.zeros((events, 128), F32)
    for k in range(neighbours):
        b = slice(k * events, (k + 1) * events)
        rows = keys[b, :]
        kpk = dot(rows, w_key[...]).astype(BF16)
        vpk = dot(rows, w_value[...]).astype(BF16)
        kp[b, :] = kpk
        vp[b, :] = vpk
        pk = qf * kpk.astype(F32)
        pv = gf * vpk.astype(F32)
        for h in range(HEADS):
            c = slice(h * hs, (h + 1) * hs)
            at = lane == h * 64 + k
            raw = jnp.where(at, jnp.sum(pk[:, c], axis=1, keepdims=True), raw)
            probs = jnp.where(at, jnp.sum(pv[:, c], axis=1, keepdims=True), probs)
    raw = raw * scaling
    capped = jnp.tanh(raw / CAP_VALUE)
    first = lane < 64
    live = jnp.where(first, lane, lane - 64) < neighbours
    weights = jnp.where(live, jnp.exp(CAP_VALUE * capped), 0.0)

    def per_head(v):
        a = jnp.sum(jnp.where(first, v, 0.0), axis=1, keepdims=True)
        b = jnp.sum(jnp.where(first, 0.0, v), axis=1, keepdims=True)
        return jnp.where(first, a, b)

    attention = weights / per_head(weights)
    att_b = attention.astype(BF16).astype(F32)
    d_scores = attention * (probs - per_head(attention * probs))
    d_raw = d_scores * (1.0 - capped * capped) * scaling
    mix = [jnp.zeros((events, hs), F32) for _ in range(HEADS)]
    dq = [jnp.zeros((events, hs), F32) for _ in range(HEADS)]
    for k in range(neighbours):
        b = slice(k * events, (k + 1) * events)
        for h in range(HEADS):
            c = slice(h * hs, (h + 1) * hs)
            i = h * 64 + k
            a = att_b[:, i : i + 1]
            d = d_raw[:, i : i + 1]
            mix[h] = mix[h] + a * vp[b, c].astype(F32)
            dq[h] = dq[h] + d * kp[b, c].astype(F32)
            dk[b, c] = (d * qf[:, c]).astype(BF16)
            dv[b, c] = (a * gf[:, c]).astype(BF16)
    q = q_rows[...]
    dq_b = jnp.concatenate(dq, axis=1).astype(BF16)
    emb[...] = (q.astype(F32) + jnp.concatenate(mix, axis=1)).astype(BF16)
    g_qkv[0:m, :] = dot_tn(q, dq_b).astype(BF16)
    g_qkv[m : 2 * m, :] = dot_tn(keys[...], dk[...]).astype(BF16)
    g_qkv[2 * m : 3 * m, :] = dot_tn(keys[...], dv[...]).astype(BF16)
    d_rows = (gf + dot_nt(dq_b, w_query[...])).astype(BF16)
    n = devices * each
    spots = (iota((n, events), 0) == dback[...]).astype(F32).astype(BF16)
    sent = dot(spots, d_rows)
    att_t = att_b.T
    raw_t = d_raw.T
    own = iota((devices, events), 0)
    totals = [jnp.zeros((devices, m), F32) for _ in range(4)]
    for k in range(neighbours):
        onehot = (own == no[k : k + 1, :]).astype(F32).astype(BF16)
        hits = (iota((m, events), 0) == nrank[k : k + 1, :]).astype(F32)
        for j, v in enumerate((raw_t, raw_t, att_t, att_t)):
            i = (j % 2) * 64 + k
            values = (hits * v[i : i + 1, :]).astype(BF16)
            totals[j] = totals[j] + dot_nt(onehot, values)
    for j in range(4):
        spot = iota((n, devices), 0) == iota((n, devices), 1) * each + j
        sent = sent + dot(spot.astype(F32).astype(BF16), totals[j].astype(BF16))
    reply[...] = sent.astype(BF16)


def expand_body(cn, source, hots, out):
    events = hots.shape[1]

    def run(d, carry):
        b = pl.ds(pl.multiple_of(d * cn, cn), cn)
        e = pl.ds(pl.multiple_of(d * events, events), events)
        out[b, :] = dot(hots[b, :], source[e, :]).astype(BF16)
        return carry

    lax.fori_loop(0, hots.shape[0] // cn, run, 0, unroll=4)


def back_body(
    scal, nrow, qe, ge, dq, drow, scol, fcol, rows, feats, code, pre, mean, div,
    upd, rst, cand, rstate, w_in, u_h, w_key, w_value, g_qkv, parity, keep, send, gates, dpre,
):
    n, m = mean.shape[0], rows.shape[1]
    f = feats.shape[1]
    hs = m // HEADS
    step = 256
    s = mean.shape[1]
    def block(i, carry):
        b = pl.ds(pl.multiple_of(i * step, step), step)
        mine = scol[b, :]
        mine = jnp.where(mine >= 0, mine, -7)
        hit = mine == nrow[...]
        parts = []
        for j in range(4):
            src = qe if j < 2 else ge
            h = j % 2
            a = jnp.where(hit, scal[j : j + 1, :].astype(F32), 0.0).astype(BF16)
            parts.append(dot(a, src[:, h * hs : (h + 1) * hs]).astype(BF16))
        dkey = jnp.concatenate(parts[:2], axis=1)
        dval = jnp.concatenate(parts[2:], axis=1)
        here = (mine == drow[...]).astype(F32).astype(BF16)
        du = dot(here, dq[...]) + dot_nt(dkey, w_key[...]) + dot_nt(dval, w_value[...])
        state = rows[b, :].astype(F32)
        update = upd[b, :]
        reset = rst[b, :]
        candidate = cand[b, :]
        d_cand = (du * update * (1.0 - candidate * candidate)).astype(BF16)
        d_reset = dot_nt(d_cand, u_h[...]) * state * reset * (1.0 - reset)
        d_update = du * (candidate - state) * update * (1.0 - update)
        d_gates = jnp.concatenate([d_update.astype(BF16), d_reset.astype(BF16), d_cand], axis=1)
        d_mean = dot_nt(d_gates, w_in[...]) / div[b, :]
        act = pre[b, :]
        sg = sigmoid(act)
        dpre[b, :] = (d_mean * sg * (1.0 + act * (1.0 - sg))).astype(BF16)
        gates[b, :] = jnp.where(fcol[b, :] > 0.5, d_gates.astype(F32), 0.0).astype(BF16)
        return carry

    lax.fori_loop(0, n // step, block, 0)
    half = keep.shape[0]
    even = parity[0, 0] == 0
    at = [0]

    def put(value):
        start, size = at[0], value.shape[0]
        low = max(0, min(size, half - start))
        pieces = ((value[:low, :], True, start), (value[low:, :], False, start + low - half))
        for part, first, r in pieces:
            if part.shape[0]:
                part = part.astype(BF16)
                b = slice(r, r + part.shape[0])

                @pl.when(even == first)
                def _():
                    keep[b, :] = part

                @pl.when(even != first)
                def _():
                    send[b, :] = part

        at[0] = start + size

    def put_cols(value):
        for j in range(value.shape[1] // 128):
            put(value[:, j * 128 : (j + 1) * 128])

    state_rows = rows[:n, :]
    put_cols(dot_tn(mean[...], gates[...]))
    put_cols(dot_tn(state_rows, gates[:, : 2 * m]))
    put_cols(dot_tn(rstate[...], gates[:, 2 * m :]))
    put_cols(dot_tn(state_rows, dpre[...]))
    put_cols(dot_tn(feats[...], dpre[...]))
    put_cols(dot_tn(code[...], dpre[...]))
    for j in range(3):
        put_cols(g_qkv[j * m : (j + 1) * m, :].astype(F32))


def spread_body(x, out):
    total = x[0].astype(F32)
    for i in range(1, x.shape[0]):
        total = total + x[i].astype(F32)
    total = total.astype(BF16)
    for i in range(x.shape[0]):
        out[i] = total


def unpack_body(mine, other, parity, g_in, g_zr, g_h, g_msg, g_q, g_k, g_v):
    half = mine.shape[0]
    even = parity[0, 0] == 0
    at = [0]

    def take(ref, r, c, size):
        start = at[0]
        low = max(0, min(size, half - start))
        if low:
            b = slice(start, start + low)
            ref[r : r + low, c : c + 128] = jnp.where(even, mine[b, :], other[b, :]).astype(F32)
        if low < size:
            b = slice(start + low - half, start + size - half)
            ref[r + low : r + size, c : c + 128] = jnp.where(
                even, other[b, :], mine[b, :]
            ).astype(F32)
        at[0] = start + size

    for ref in (g_in, g_zr, g_h, g_msg, g_q, g_k, g_v):
        for c in range(0, ref.shape[1], 128):
            take(ref, 0, c, ref.shape[0])


def exchange(x):
    return lax.all_to_all(x, AXES, split_axis=0, concat_axis=0, tiled=True)


def body(
    memory, features, buckets, src_owner, src_slot, dst_owner, dst_slot, nb_owner, nb_slot,
    w_msg, w_in, u_zr, u_h, w_query, w_key, w_value, emb_grad,
):
    devices = lax.axis_size(AXES)
    events, m = emb_grad.shape
    acc_rows = memory.shape[0]
    neighbours = nb_slot.shape[1]
    feat = features.shape[1]
    width = w_msg.shape[1]
    ce = 2 * events // devices
    cn = 2 * events * neighbours // devices
    n_dst = devices * ce
    n_side = 2 * n_dst
    n_nb = devices * cn
    lanes = 4 * ce + 2 * cn
    grad_all = lax.all_gather(emb_grad, AXES, axis=0, tiled=True)
    no = nb_owner.reshape(events, neighbours).T
    req, side_feats, dplace, nrank = call(
        functools.partial(place_body, ce, cn, devices),
        [
            ((devices, lanes), I32),
            ((n_side, feat), BF16),
            ((1, events), I32),
            ((neighbours, events), I32),
        ],
        (
            src_owner.reshape(1, events), src_slot.reshape(1, events),
            dst_owner.reshape(1, events), dst_slot.reshape(1, events),
            no, nb_slot.T, buckets.reshape(1, events), features,
        ),
        "place",
        56,
    )
    got = exchange(req.reshape(devices, 1, lanes)).reshape(devices, lanes)
    got_feats = exchange(side_feats.reshape(devices, 2 * ce, feat)).reshape(n_side, feat)
    vm = pl.BlockSpec(memory_space=pltpu.VMEM)
    sm = pl.BlockSpec(memory_space=pltpu.SMEM)
    owner_outs = [
        ((n_side, m), BF16), ((n_dst, m), BF16),
        ((1, n_side), I32), ((n_side, 1), I32), ((n_side, 1), F32),
        ((n_side, w_msg.shape[0] - m - feat), BF16),
        ((n_side, width), F32), ((n_side, width), BF16), ((n_side, width), F32),
        ((n_side, m), F32), ((n_side, m), F32), ((n_side, m), F32), ((n_side, m), BF16),
    ]
    fetched = pl.pallas_call(
        functools.partial(sides_body, ce),
        out_shape=jax.ShapeDtypeStruct((n_side, m), BF16),
        in_specs=[vm, sm],
        out_specs=vm,
        scratch_shapes=[
            pltpu.VMEM((m // 128, acc_rows, 128), F32), pltpu.VMEM((m // 128, n_side, 128), F32),
        ],
        compiler_params=room(56),
        name="sides",
    )(memory, got)
    (
        new_side, dst_new, sfirst, scol, fcol, code, pre, mean, div, upd, rst, cand, rstate,
    ) = call(
        functools.partial(owner_body, ce),
        owner_outs,
        (fetched, got_feats, got, w_msg, w_in, u_zr, u_h),
        "owner",
        56,
        scratch=[pltpu.VMEM((n_side, width), BF16), pltpu.VMEM((n_side, 1), F32)],
    )
    nb_reply = pl.pallas_call(
        functools.partial(answer_body, ce, cn),
        out_shape=jax.ShapeDtypeStruct((n_nb, m), BF16),
        in_specs=[vm, vm, sm],
        out_specs=vm,
        scratch_shapes=[
            pltpu.VMEM((m // 128, acc_rows + 8, 128), F32),
            pltpu.VMEM((m // 128, n_side, 128), F32), pltpu.VMEM((m // 128, n_nb, 128), F32),
        ],
        compiler_params=room(56),
        name="answer",
    )(memory, new_side, got)
    back_dst = exchange(dst_new.reshape(devices, ce, m)).reshape(n_dst, m)
    back_nb = exchange(nb_reply.reshape(devices, cn, m))
    back_dst, nb_reply = lax.optimization_barrier((back_dst, nb_reply))
    q_rows, q_proj = call(
        query_body,
        [((events, m), BF16), ((events, m), BF16)],
        (back_dst, dplace, w_query),
        "query",
        4,
    )
    proj_all = lax.all_gather(q_proj, AXES, axis=0, tiled=True)
    each = max(2 * ce, -(-(ce + 4) // 8) * 8)
    late_got, _ = lax.optimization_barrier((got, nb_reply))
    new_memory = refresh(memory, sfirst, new_side)
    late_event = late_got[:, 4 * ce + cn :].reshape(n_nb)
    table = jnp.maximum(late_event, 0) + jnp.arange(n_nb, dtype=I32) // cn * events
    ge = grad_all[table]
    late_slots = late_got[:, 4 * ce : 4 * ce + cn].reshape(n_nb)
    nrow = jnp.where(late_event >= 0, late_slots, -1).reshape(1, n_nb)
    drow = jnp.concatenate(
        [jnp.full((devices, each - ce), -1, I32), late_got[:, ce : 2 * ce]], axis=1
    ).reshape(1, devices * each)
    hots = hot(events, ce, cn, late_got, n_nb)
    nb_place = no * cn + nrank
    back_nb, new_memory, ge, nrow, drow, hots, nb_place, q_rows = lax.optimization_barrier(
        (back_nb, new_memory, ge, nrow, drow, hots, nb_place, q_rows)
    )
    dback = dplace // ce * each + (each - ce) + dplace % ce
    embedding, reply, g_qkv = call(
        functools.partial(attend_body, cn, devices, each),
        [((events, m), BF16), ((devices * each, m), BF16), ((3 * m, m), BF16)],
        (
            back_nb.reshape(n_nb, m), q_rows, q_proj, emb_grad, w_query, w_key, w_value, dback, no,
            nrank, nb_place,
        ),
        "attend",
        20,
        scratch=[pltpu.VMEM((events * neighbours, m), BF16)] * 5
        + [
            pltpu.VMEM((m // 128, n_nb, 128), F32),
            pltpu.VMEM((m // 128, events * neighbours, 128), F32),
        ],
        scalars=1,
    )
    back = exchange(reply.reshape(devices, each, m))
    if cn % 16:
        qe = proj_all[table]
    else:
        qe = pl.pallas_call(
            functools.partial(expand_body, cn),
            out_shape=jax.ShapeDtypeStruct((n_nb, m), BF16),
            in_specs=[vm, vm],
            out_specs=vm,
            compiler_params=room(8),
            name="expand",
        )(proj_all, hots)
    back, qe = lax.optimization_barrier((back, qe))
    scal = back[:, :4, :cn].transpose(1, 0, 2).reshape(4, n_nb)
    index = lax.axis_index(AXES)
    parity = (index % 2).astype(I32).reshape(1, 1)
    total_rows = (w_msg.size + w_in.size + u_zr.size + u_h.size + 3 * w_query.size) // 128
    half = total_rows // 2
    args = (
        scal, nrow, qe, ge, back.reshape(devices * each, m), drow, scol, fcol, fetched,
        got_feats, code, pre, mean, div, upd, rst, cand, rstate, w_in, u_h, w_key, w_value,
        g_qkv, parity,
    )
    keep, send = pl.pallas_call(
        back_body,
        out_shape=[jax.ShapeDtypeStruct((half, 128), BF16)] * 2,
        in_specs=[vm] * (len(args) - 1) + [sm],
        out_specs=[vm] * 2,
        scratch_shapes=[pltpu.VMEM((n_side, 3 * m), BF16), pltpu.VMEM((n_side, width), BF16)],
        compiler_params=room(56),
        name="back",
    )(*args)
    pairs = [(i, i ^ 1) for i in range(devices)]
    teams = [[i for i in range(devices) if i % 2 == p] for p in range(2)]
    size = devices // 2
    half_sum = (
        keep.astype(F32) + lax.ppermute(send, AXES, pairs).astype(F32)
    ).astype(BF16).reshape(size, half // size, 128)
    shares = lax.all_to_all(
        half_sum, AXES, split_axis=0, concat_axis=0, tiled=True, axis_index_groups=teams
    )
    spread = call(spread_body, [(shares.shape, BF16)], (shares,), "spread", 6)[0]
    mine = lax.all_to_all(
        spread, AXES, split_axis=0, concat_axis=0, tiled=True, axis_index_groups=teams
    ).reshape(half, 128)
    other = lax.ppermute(mine, AXES, pairs)
    outs = [
        ((width, 3 * m), F32), ((m, 2 * m), F32), ((m, m), F32),
        ((w_msg.shape[0], width), F32), ((m, m), F32), ((m, m), F32), ((m, m), F32),
    ]
    g_in, g_zr, g_h, g_msg, g_q, g_k, g_v = pl.pallas_call(
        unpack_body,
        out_shape=[jax.ShapeDtypeStruct(a, d) for a, d in outs],
        in_specs=[vm, vm, sm],
        out_specs=[vm] * len(outs),
        compiler_params=room(8),
        name="unpack",
    )(mine, other, parity)
    return (new_memory, embedding, g_msg, g_in, g_zr, g_h, g_q, g_k, g_v)


def solution(mesh):
    split = P(AXES)
    return jax.shard_map(
        body,
        mesh=mesh,
        in_specs=(split,) * 9 + (P(),) * 7 + (split,),
        out_specs=(split, split) + (P(),) * 7,
        check_vma=False,
    )
```

```python
import functools
import math

import jax
import jax.numpy as jnp
from jax import lax
from jax.experimental import pallas as pl
from jax.experimental.pallas import tpu as pltpu
from jax.sharding import PartitionSpec as P

HEADS = 2
AXES = ("acct", "rep")
CAP_VALUE = 10.0
F32 = jnp.float32
BF16 = jnp.bfloat16
I32 = jnp.int32
EXACT = lax.Precision.HIGHEST

def room(mib):
    return pltpu.CompilerParams(vmem_limit_bytes=mib * 1024 * 1024)


def dot(a, b, **kw):
    return jnp.dot(a, b, preferred_element_type=F32, **kw)


def dot_nt(a, b, **kw):
    return lax.dot_general(a, b, (((1,), (1,)), ((), ())), preferred_element_type=F32, **kw)


def dot_tn(a, b, **kw):
    return lax.dot_general(a, b, (((0,), (0,)), ((), ())), preferred_element_type=F32, **kw)


def iota(shape, axis):
    return lax.broadcasted_iota(I32, shape, axis)


def to_col(table, n, per, lane0, base=0):
    devices, lanes = table.shape
    pick = ((iota((n, devices), 0) + base) // per == iota((n, devices), 1)).astype(F32)
    spread = dot(pick, table, precision=EXACT)
    r = iota((n, lanes), 0) + base
    at = iota((n, lanes), 1) == lane0 + r - r // per * per
    return jnp.sum(jnp.where(at, spread, 0.0), axis=1, keepdims=True)


def to_row(table, n, per, lane0):
    devices, lanes = table.shape
    c = iota((lanes, n), 1)
    pick = (iota((lanes, n), 0) == lane0 + c - c // per * per).astype(F32)
    spread = dot(table, pick, precision=EXACT)
    mine = iota((devices, n), 0) == iota((devices, n), 1) // per
    return jnp.sum(jnp.where(mine, spread, 0.0), axis=0, keepdims=True)


def sigmoid(v):
    return 1.0 / (1.0 + jnp.exp(-v))


def call(body, outs, args, name, mib, scratch=(), scalars=0):
    vm = pl.BlockSpec(memory_space=pltpu.VMEM)
    sm = pl.BlockSpec(memory_space=pltpu.SMEM)
    return pl.pallas_call(
        body,
        out_shape=[jax.ShapeDtypeStruct(s, d) for s, d in outs],
        in_specs=[vm] * (len(args) - scalars) + [sm] * scalars,
        out_specs=[vm] * len(outs),
        scratch_shapes=list(scratch),
        compiler_params=room(mib),
        name=name,
    )(*args)


def place_body(ce, cn, devices, so, ss, do, ds, no, ns, bk, feat, req, feats, dplace, nrank):
    events = so.shape[1]
    neighbours = no.shape[0]
    upper = (iota((events, events), 0) < iota((events, events), 1)).astype(BF16)
    own = iota((devices, events), 0)
    rows = iota((2 * devices * ce, events), 0)

    def fill(onehot, rank, value, cap):
        hits = (iota((cap, events), 0) == rank).astype(F32)
        owner_b = onehot.astype(BF16)
        high = dot_nt(owner_b, (hits * (value >> 7).astype(F32)).astype(BF16))
        low = dot_nt(owner_b, (hits * (value & 127).astype(F32)).astype(BF16))
        return high * 128.0 + low

    chosen = jnp.zeros((2 * devices * ce, events), F32)
    for side, (o_ref, s_ref) in enumerate(((so, ss), (do, ds))):
        owner = o_ref[...]
        onehot = (own == owner).astype(F32)
        before = dot(onehot.astype(BF16), upper)
        rank = jnp.sum(onehot * before, axis=0, keepdims=True).astype(I32)
        req[:, side * ce : (side + 1) * ce] = (
            fill(onehot, rank, s_ref[...] + 1, ce).astype(I32) - 1
        )
        req[:, (2 + side) * ce : (3 + side) * ce] = fill(onehot, rank, bk[...], ce).astype(I32)
        chosen = chosen + (rows == owner * (2 * ce) + (side * ce + rank)).astype(F32)
        if side == 1:
            dplace[...] = owner * ce + rank
    feats[...] = dot(chosen.astype(BF16), feat[...]).astype(BF16)
    base = jnp.zeros((devices, 1), F32)
    slots = jnp.zeros((devices, cn), F32)
    which = jnp.zeros((devices, cn), F32)
    event = iota((1, events), 1)
    for k in range(neighbours):
        onehot = (own == no[k : k + 1, :]).astype(F32)
        before = dot(onehot.astype(BF16), upper) + base
        rank = jnp.sum(onehot * before, axis=0, keepdims=True).astype(I32)
        nrank[k : k + 1, :] = rank
        base = base + jnp.sum(onehot, axis=1, keepdims=True)
        slots = slots + fill(onehot, rank, ns[k : k + 1, :], cn)
        which = which + fill(onehot, rank, event + 1, cn)
    req[:, 4 * ce : 4 * ce + cn] = slots.astype(I32)
    req[:, 4 * ce + cn :] = which.astype(I32) - 1


def widen_rows(source, target):
    step = 256

    def run(i, carry):
        b = pl.ds(pl.multiple_of(i * step, step), step)
        for h in range(target.shape[0]):
            target[h, b, :] = source[b, h * 128 : (h + 1) * 128].astype(F32)
        return carry

    lax.fori_loop(0, source.shape[0] // step, run, 0)


def narrow_rows(source, target):
    for h in range(source.shape[0]):
        target[:, h * 128 : (h + 1) * 128] = source[h].astype(BF16)


def pick_rows(table, target, slots_s, first, count, read):
    rows = math.lcm(count, 8)
    sources = rows // count

    def block(i, carry):
        for g in range(rows // 8):
            where = [
                read(slots_s[i * sources + r // count, first + r % count])
                for r in range(g * 8, g * 8 + 8)
            ]
            base = pl.multiple_of(i * rows + g * 8, 8)
            for h in range(table.shape[0]):
                found = [table[h, pl.ds(w, 1), :] for w in where]
                target[h, pl.ds(base, 8), :] = jnp.concatenate(found, axis=0)
        return carry

    lax.fori_loop(0, slots_s.shape[0] // sources, block, 0)


def sides_body(ce, memory, slots_s, rows, table, wide):
    widen_rows(memory, table)
    pick_rows(table, wide, slots_s, 0, 2 * ce, lambda v: jnp.maximum(v, 0))
    narrow_rows(wide, rows)


def answer_body(ce, cn, memory, new, slots_s, reply, table, wide, copied):
    acc_rows = memory.shape[0]
    widen_rows(memory, table)
    widen_rows(new, wide)

    each = 2 * ce
    rows = math.lcm(each, 8)
    sources = rows // each

    def store(i, carry):
        fresh = [
            wide[h, pl.ds(pl.multiple_of(i * rows, rows), rows), :] for h in range(wide.shape[0])
        ]
        for r in range(rows):
            slot = slots_s[i * sources + r // each, r % each]
            slot = jnp.where(slot >= 0, slot, acc_rows)
            for h in range(wide.shape[0]):
                table[h, pl.ds(slot, 1), :] = fresh[h][r : r + 1, :]
        return carry

    lax.fori_loop(0, slots_s.shape[0] // sources, store, 0)
    pick_rows(table, copied, slots_s, 4 * ce, cn, lambda v: v)
    narrow_rows(copied, reply)


def owner_body(
    ce, rows, feats, got, w_msg, w_in, u_zr, u_h,
    new, dst_new, sfirst, scol, fcol, code, pre, mean, div, upd, rst, cand, rstate, msg, bcol,
):
    n, f = feats.shape
    m = rows.shape[1]
    t = w_msg.shape[0] - m - f
    step = 128
    frequency = jnp.exp(iota((1, t), 1).astype(F32) * (-11.5 / t))
    numbers = got[:, : 4 * ce].astype(F32)
    scol[...] = to_col(numbers, n, 2 * ce, 0).astype(I32)
    bcol[...] = to_col(numbers, n, 2 * ce, 2 * ce)
    slots = to_row(numbers, n, 2 * ce, 0).astype(I32)

    def messages(i, carry):
        b = pl.ds(pl.multiple_of(i * step, step), step)
        enc = jnp.cos(bcol[b, :] * frequency).astype(BF16)
        code[b, :] = enc
        act = (
            dot(rows[b, :], w_msg[:m, :]) + dot(feats[b, :], w_msg[m : m + f, :])
        ) + dot(enc, w_msg[m + f :, :])
        pre[b, :] = act
        msg[b, :] = (act * sigmoid(act)).astype(BF16)
        return carry

    lax.fori_loop(0, n // step, messages, 0)
    def gru(i, early):
        b = pl.ds(pl.multiple_of(i * step, step), step)
        mine = scol[b, :]
        same = (mine == slots) & (mine >= 0)
        eq = same.astype(F32)
        eq_b = eq.astype(BF16)
        counts = dot(eq_b, jnp.ones((n, msg.shape[1]), BF16))
        divisor = jnp.maximum(counts, 1.0)
        div[b, :] = divisor
        earlier = jnp.where(iota((step, n), 1) < iota((step, n), 0) + i * step, eq, 0.0)
        fcol[b, :] = (jnp.sum(earlier, axis=1, keepdims=True) < 0.5).astype(F32)
        later = jnp.where(iota((step, n), 1) > iota((step, n), 0) + i * step, eq, 0.0)
        early = early + jnp.sum(later, axis=0, keepdims=True)
        mean_b = (dot(eq_b, msg[...]) / divisor).astype(BF16)
        mean[b, :] = mean_b
        state = rows[b, :]
        state_wide = state.astype(F32)
        from_input = dot(mean_b, w_in[...])
        from_state = dot(state, u_zr[...])
        update = sigmoid(from_input[:, :m] + from_state[:, :m])
        reset = sigmoid(from_input[:, m : 2 * m] + from_state[:, m:])
        reset_state = (reset * state_wide).astype(BF16)
        candidate = jnp.tanh(from_input[:, 2 * m :] + dot(reset_state, u_h[...]))
        upd[b, :] = update
        rst[b, :] = reset
        cand[b, :] = candidate
        rstate[b, :] = reset_state
        new[b, :] = ((1.0 - update) * state_wide + update * candidate).astype(BF16)
        return early

    early = lax.fori_loop(0, n // step, gru, jnp.zeros((1, n), F32))
    sfirst[...] = jnp.where((early < 0.5) & (slots >= 0), slots, -2)
    half = n // 2
    r = iota((half, n), 0)
    pick = (iota((half, n), 1) == r + (r // ce + 1) * ce).astype(F32).astype(BF16)
    dst_new[...] = dot(pick, new[...]).astype(BF16)


def refresh_body(block, old, sfirst, new, out):
    row = iota((block, 1), 0) + pl.program_id(0) * block
    hit = (row == sfirst[...]).astype(F32).astype(BF16)
    rows = dot(hit, new[...])
    found = dot(hit, jnp.ones((new.shape[0], 128), BF16)) > 0.5
    for h in range(rows.shape[1] // 128):
        c = slice(h * 128, (h + 1) * 128)
        out[:, c] = jnp.where(found, rows[:, c], old[:, c].astype(F32)).astype(BF16)


def refresh(memory, sfirst, new):
    n, m = memory.shape
    s = new.shape[0]
    block = 512
    return pl.pallas_call(
        functools.partial(refresh_body, block),
        grid=(n // block,),
        out_shape=jax.ShapeDtypeStruct((n, m), BF16),
        in_specs=[
            pl.BlockSpec((block, m), lambda i: (i, 0)),
            pl.BlockSpec((1, s), lambda i: (0, 0)),
            pl.BlockSpec((s, m), lambda i: (0, 0)),
        ],
        out_specs=pl.BlockSpec((block, m), lambda i: (i, 0)),
        compiler_params=room(8),
        name="refresh",
    )(memory, sfirst, new)


def hot_body(events, ce, cn, block, got, out):
    table = got[:, 4 * ce + cn :].astype(F32)
    event = to_col(table, block, cn, 0, pl.program_id(0) * block).astype(I32)
    out[...] = (iota((block, events), 1) == event).astype(F32).astype(BF16)


def hot(events, ce, cn, got, n):
    block = 512
    return pl.pallas_call(
        functools.partial(hot_body, events, ce, cn, block),
        grid=(n // block,),
        out_shape=jax.ShapeDtypeStruct((n, events), BF16),
        in_specs=[pl.BlockSpec(got.shape, lambda i: (0, 0))],
        out_specs=pl.BlockSpec((block, events), lambda i: (i, 0)),
        compiler_params=room(6),
        name="hot",
    )(got)


def query_body(back, dplace, w_query, q_rows, q_proj):
    n = back.shape[0]
    events = dplace.shape[1]
    pick = (iota((n, events), 0) == dplace[...]).astype(F32).astype(BF16)
    q = dot_tn(pick, back[...]).astype(BF16)
    q_rows[...] = q
    q_proj[...] = dot(q, w_query[...]).astype(BF16)


def attend_body(
    cn, devices, each, back, q_rows, q_proj, grad, w_query, w_key, w_value, dback, no, nrank, places,
    emb, reply, g_qkv, kp, vp, dk, dv, keys, wide, picked,
):
    events, m = q_rows.shape
    neighbours = no.shape[0]
    hs = m // HEADS
    scaling = 1.0 / math.sqrt(hs)
    widen_rows(back, wide)
    pick_rows(wide, picked, places, 0, events, lambda v: v)
    narrow_rows(picked, keys)
    qf = q_proj[...].astype(F32)
    gf = grad[...].astype(F32)
    lane = iota((events, 128), 1)
    raw = jnp.zeros((events, 128), F32)
    probs = jnp.zeros((events, 128), F32)
    for k in range(neighbours):
        b = slice(k * events, (k + 1) * events)
        rows = keys[b, :]
        kpk = dot(rows, w_key[...]).astype(BF16)
        vpk = dot(rows, w_value[...]).astype(BF16)
        kp[b, :] = kpk
        vp[b, :] = vpk
        pk = qf * kpk.astype(F32)
        pv = gf * vpk.astype(F32)
        for h in range(HEADS):
            c = slice(h * hs, (h + 1) * hs)
            at = lane == h * 64 + k
            raw = jnp.where(at, jnp.sum(pk[:, c], axis=1, keepdims=True), raw)
            probs = jnp.where(at, jnp.sum(pv[:, c], axis=1, keepdims=True), probs)
    raw = raw * scaling
    capped = jnp.tanh(raw / CAP_VALUE)
    first = lane < 64
    live = jnp.where(first, lane, lane - 64) < neighbours
    weights = jnp.where(live, jnp.exp(CAP_VALUE * capped), 0.0)

    def per_head(v):
        a = jnp.sum(jnp.where(first, v, 0.0), axis=1, keepdims=True)
        b = jnp.sum(jnp.where(first, 0.0, v), axis=1, keepdims=True)
        return jnp.where(first, a, b)

    attention = weights / per_head(weights)
    att_b = attention.astype(BF16).astype(F32)
    d_scores = attention * (probs - per_head(attention * probs))
    d_raw = d_scores * (1.0 - capped * capped) * scaling
    mix = [jnp.zeros((events, hs), F32) for _ in range(HEADS)]
    dq = [jnp.zeros((events, hs), F32) for _ in range(HEADS)]
    for k in range(neighbours):
        b = slice(k * events, (k + 1) * events)
        for h in range(HEADS):
            c = slice(h * hs, (h + 1) * hs)
            i = h * 64 + k
            a = att_b[:, i : i + 1]
            d = d_raw[:, i : i + 1]
            mix[h] = mix[h] + a * vp[b, c].astype(F32)
            dq[h] = dq[h] + d * kp[b, c].astype(F32)
            dk[b, c] = (d * qf[:, c]).astype(BF16)
            dv[b, c] = (a * gf[:, c]).astype(BF16)
    q = q_rows[...]
    dq_b = jnp.concatenate(dq, axis=1).astype(BF16)
    emb[...] = (q.astype(F32) + jnp.concatenate(mix, axis=1)).astype(BF16)
    g_qkv[0:m, :] = dot_tn(q, dq_b).astype(BF16)
    g_qkv[m : 2 * m, :] = dot_tn(keys[...], dk[...]).astype(BF16)
    g_qkv[2 * m : 3 * m, :] = dot_tn(keys[...], dv[...]).astype(BF16)
    d_rows = (gf + dot_nt(dq_b, w_query[...])).astype(BF16)
    n = devices * each
    spots = (iota((n, events), 0) == dback[...]).astype(F32).astype(BF16)
    sent = dot(spots, d_rows)
    att_t = att_b.T
    raw_t = d_raw.T
    own = iota((devices, events), 0)
    totals = [jnp.zeros((devices, m), F32) for _ in range(4)]
    for k in range(neighbours):
        onehot = (own == no[k : k + 1, :]).astype(F32).astype(BF16)
        hits = (iota((m, events), 0) == nrank[k : k + 1, :]).astype(F32)
        for j, v in enumerate((raw_t, raw_t, att_t, att_t)):
            i = (j % 2) * 64 + k
            values = (hits * v[i : i + 1, :]).astype(BF16)
            totals[j] = totals[j] + dot_nt(onehot, values)
    for j in range(4):
        spot = iota((n, devices), 0) == iota((n, devices), 1) * each + j
        sent = sent + dot(spot.astype(F32).astype(BF16), totals[j].astype(BF16))
    reply[...] = sent.astype(BF16)


def expand_body(cn, source, hots, out):
    events = hots.shape[1]

    def run(d, carry):
        b = pl.ds(pl.multiple_of(d * cn, cn), cn)
        e = pl.ds(pl.multiple_of(d * events, events), events)
        out[b, :] = dot(hots[b, :], source[e, :]).astype(BF16)
        return carry

    lax.fori_loop(0, hots.shape[0] // cn, run, 0, unroll=4)


def early_body(scal, nrow, ge, dq, drow, scol, w_value, out):
    n, m = out.shape
    hs = m // HEADS
    step = 256

    def block(i, carry):
        b = pl.ds(pl.multiple_of(i * step, step), step)
        mine = scol[b, :]
        mine = jnp.where(mine >= 0, mine, -7)
        hit = mine == nrow[...]
        parts = []
        for h in range(HEADS):
            a = jnp.where(hit, scal[2 + h : 3 + h, :].astype(F32), 0.0).astype(BF16)
            parts.append(dot(a, ge[:, h * hs : (h + 1) * hs]).astype(BF16))
        here = (mine == drow[...]).astype(F32).astype(BF16)
        dval = jnp.concatenate(parts, axis=1)
        out[b, :] = dot(here, dq[...]) + dot_nt(dval, w_value[...])
        return carry

    lax.fori_loop(0, n // step, block, 0)


def back_body(
    scal, nrow, qe, partial, scol, fcol, rows, feats, code, pre, mean, div,
    upd, rst, cand, rstate, w_in, u_h, w_key, g_qkv, parity, keep, send, gates, dpre,
):
    n, m = mean.shape[0], rows.shape[1]
    f = feats.shape[1]
    hs = m // HEADS
    step = 256
    s = mean.shape[1]
    def block(i, carry):
        b = pl.ds(pl.multiple_of(i * step, step), step)
        mine = scol[b, :]
        mine = jnp.where(mine >= 0, mine, -7)
        hit = mine == nrow[...]
        parts = []
        for h in range(HEADS):
            a = jnp.where(hit, scal[h : h + 1, :].astype(F32), 0.0).astype(BF16)
            parts.append(dot(a, qe[:, h * hs : (h + 1) * hs]).astype(BF16))
        du = partial[b, :] + dot_nt(jnp.concatenate(parts, axis=1), w_key[...])
        state = rows[b, :].astype(F32)
        update = upd[b, :]
        reset = rst[b, :]
        candidate = cand[b, :]
        d_cand = (du * update * (1.0 - candidate * candidate)).astype(BF16)
        d_reset = dot_nt(d_cand, u_h[...]) * state * reset * (1.0 - reset)
        d_update = du * (candidate - state) * update * (1.0 - update)
        d_gates = jnp.concatenate([d_update.astype(BF16), d_reset.astype(BF16), d_cand], axis=1)
        d_mean = dot_nt(d_gates, w_in[...]) / div[b, :]
        act = pre[b, :]
        sg = sigmoid(act)
        dpre[b, :] = (d_mean * sg * (1.0 + act * (1.0 - sg))).astype(BF16)
        gates[b, :] = jnp.where(fcol[b, :] > 0.5, d_gates.astype(F32), 0.0).astype(BF16)
        return carry

    lax.fori_loop(0, n // step, block, 0)
    half = keep.shape[0]
    even = parity[0, 0] == 0
    at = [0]

    def put(value):
        start, size = at[0], value.shape[0]
        low = max(0, min(size, half - start))
        pieces = ((value[:low, :], True, start), (value[low:, :], False, start + low - half))
        for part, first, r in pieces:
            if part.shape[0]:
                part = part.astype(BF16)
                b = slice(r, r + part.shape[0])

                @pl.when(even == first)
                def _():
                    keep[b, :] = part

                @pl.when(even != first)
                def _():
                    send[b, :] = part

        at[0] = start + size

    def put_cols(value):
        for j in range(value.shape[1] // 128):
            put(value[:, j * 128 : (j + 1) * 128])

    state_rows = rows[:n, :]
    put_cols(dot_tn(mean[...], gates[...]))
    put_cols(dot_tn(state_rows, gates[:, : 2 * m]))
    put_cols(dot_tn(rstate[...], gates[:, 2 * m :]))
    put_cols(dot_tn(state_rows, dpre[...]))
    put_cols(dot_tn(feats[...], dpre[...]))
    put_cols(dot_tn(code[...], dpre[...]))
    for j in range(3):
        put_cols(g_qkv[j * m : (j + 1) * m, :].astype(F32))


def spread_body(x, out):
    total = x[0].astype(F32)
    for i in range(1, x.shape[0]):
        total = total + x[i].astype(F32)
    total = total.astype(BF16)
    for i in range(x.shape[0]):
        out[i] = total


def unpack_body(mine, other, parity, g_in, g_zr, g_h, g_msg, g_q, g_k, g_v):
    half = mine.shape[0]
    even = parity[0, 0] == 0
    at = [0]

    def take(ref, r, c, size):
        start = at[0]
        low = max(0, min(size, half - start))
        if low:
            b = slice(start, start + low)
            ref[r : r + low, c : c + 128] = jnp.where(even, mine[b, :], other[b, :]).astype(F32)
        if low < size:
            b = slice(start + low - half, start + size - half)
            ref[r + low : r + size, c : c + 128] = jnp.where(
                even, other[b, :], mine[b, :]
            ).astype(F32)
        at[0] = start + size

    for ref in (g_in, g_zr, g_h, g_msg, g_q, g_k, g_v):
        for c in range(0, ref.shape[1], 128):
            take(ref, 0, c, ref.shape[0])


def exchange(x):
    return lax.all_to_all(x, AXES, split_axis=0, concat_axis=0, tiled=True)


def body(
    memory, features, buckets, src_owner, src_slot, dst_owner, dst_slot, nb_owner, nb_slot,
    w_msg, w_in, u_zr, u_h, w_query, w_key, w_value, emb_grad,
):
    devices = lax.axis_size(AXES)
    events, m = emb_grad.shape
    acc_rows = memory.shape[0]
    neighbours = nb_slot.shape[1]
    feat = features.shape[1]
    width = w_msg.shape[1]
    ce = 2 * events // devices
    cn = 2 * events * neighbours // devices
    n_dst = devices * ce
    n_side = 2 * n_dst
    n_nb = devices * cn
    lanes = 4 * ce + 2 * cn
    grad_all = lax.all_gather(emb_grad, AXES, axis=0, tiled=True)
    no = nb_owner.reshape(events, neighbours).T
    req, side_feats, dplace, nrank = call(
        functools.partial(place_body, ce, cn, devices),
        [
            ((devices, lanes), I32),
            ((n_side, feat), BF16),
            ((1, events), I32),
            ((neighbours, events), I32),
        ],
        (
            src_owner.reshape(1, events), src_slot.reshape(1, events),
            dst_owner.reshape(1, events), dst_slot.reshape(1, events),
            no, nb_slot.T, buckets.reshape(1, events), features,
        ),
        "place",
        56,
    )
    got = exchange(req.reshape(devices, 1, lanes)).reshape(devices, lanes)
    got_feats = exchange(side_feats.reshape(devices, 2 * ce, feat)).reshape(n_side, feat)
    vm = pl.BlockSpec(memory_space=pltpu.VMEM)
    sm = pl.BlockSpec(memory_space=pltpu.SMEM)
    owner_outs = [
        ((n_side, m), BF16), ((n_dst, m), BF16),
        ((1, n_side), I32), ((n_side, 1), I32), ((n_side, 1), F32),
        ((n_side, w_msg.shape[0] - m - feat), BF16),
        ((n_side, width), F32), ((n_side, width), BF16), ((n_side, width), F32),
        ((n_side, m), F32), ((n_side, m), F32), ((n_side, m), F32), ((n_side, m), BF16),
    ]
    fetched = pl.pallas_call(
        functools.partial(sides_body, ce),
        out_shape=jax.ShapeDtypeStruct((n_side, m), BF16),
        in_specs=[vm, sm],
        out_specs=vm,
        scratch_shapes=[
            pltpu.VMEM((m // 128, acc_rows, 128), F32), pltpu.VMEM((m // 128, n_side, 128), F32),
        ],
        compiler_params=room(56),
        name="sides",
    )(memory, got)
    (
        new_side, dst_new, sfirst, scol, fcol, code, pre, mean, div, upd, rst, cand, rstate,
    ) = call(
        functools.partial(owner_body, ce),
        owner_outs,
        (fetched, got_feats, got, w_msg, w_in, u_zr, u_h),
        "owner",
        56,
        scratch=[pltpu.VMEM((n_side, width), BF16), pltpu.VMEM((n_side, 1), F32)],
    )
    nb_reply = pl.pallas_call(
        functools.partial(answer_body, ce, cn),
        out_shape=jax.ShapeDtypeStruct((n_nb, m), BF16),
        in_specs=[vm, vm, sm],
        out_specs=vm,
        scratch_shapes=[
            pltpu.VMEM((m // 128, acc_rows + 8, 128), F32),
            pltpu.VMEM((m // 128, n_side, 128), F32), pltpu.VMEM((m // 128, n_nb, 128), F32),
        ],
        compiler_params=room(56),
        name="answer",
    )(memory, new_side, got)
    back_dst = exchange(dst_new.reshape(devices, ce, m)).reshape(n_dst, m)
    back_nb = exchange(nb_reply.reshape(devices, cn, m))
    back_dst, nb_reply = lax.optimization_barrier((back_dst, nb_reply))
    q_rows, q_proj = call(
        query_body,
        [((events, m), BF16), ((events, m), BF16)],
        (back_dst, dplace, w_query),
        "query",
        4,
    )
    proj_all = lax.all_gather(q_proj, AXES, axis=0, tiled=True)
    each = max(2 * ce, -(-(ce + 4) // 8) * 8)
    late_got, _ = lax.optimization_barrier((got, nb_reply))
    new_memory = refresh(memory, sfirst, new_side)
    late_event = late_got[:, 4 * ce + cn :].reshape(n_nb)
    table = jnp.maximum(late_event, 0) + jnp.arange(n_nb, dtype=I32) // cn * events
    ge = grad_all[table]
    late_slots = late_got[:, 4 * ce : 4 * ce + cn].reshape(n_nb)
    nrow = jnp.where(late_event >= 0, late_slots, -1).reshape(1, n_nb)
    drow = jnp.concatenate(
        [jnp.full((devices, each - ce), -1, I32), late_got[:, ce : 2 * ce]], axis=1
    ).reshape(1, devices * each)
    hots = hot(events, ce, cn, late_got, n_nb)
    nb_place = no * cn + nrank
    back_nb, new_memory, ge, nrow, drow, hots, nb_place, q_rows = lax.optimization_barrier(
        (back_nb, new_memory, ge, nrow, drow, hots, nb_place, q_rows)
    )
    dback = dplace // ce * each + (each - ce) + dplace % ce
    embedding, reply, g_qkv = call(
        functools.partial(attend_body, cn, devices, each),
        [((events, m), BF16), ((devices * each, m), BF16), ((3 * m, m), BF16)],
        (
            back_nb.reshape(n_nb, m), q_rows, q_proj, emb_grad, w_query, w_key, w_value, dback, no,
            nrank, nb_place,
        ),
        "attend",
        20,
        scratch=[pltpu.VMEM((events * neighbours, m), BF16)] * 5
        + [
            pltpu.VMEM((m // 128, n_nb, 128), F32),
            pltpu.VMEM((m // 128, events * neighbours, 128), F32),
        ],
        scalars=1,
    )
    back = exchange(reply.reshape(devices, each, m))
    if cn % 16:
        qe = proj_all[table]
    else:
        qe = pl.pallas_call(
            functools.partial(expand_body, cn),
            out_shape=jax.ShapeDtypeStruct((n_nb, m), BF16),
            in_specs=[vm, vm],
            out_specs=vm,
            compiler_params=room(8),
            name="expand",
        )(proj_all, hots)
    scal = back[:, :4, :cn].transpose(1, 0, 2).reshape(4, n_nb)
    partial = call(
        early_body,
        [((n_side, m), F32)],
        (scal, nrow, ge, back.reshape(devices * each, m), drow, scol, w_value),
        "early",
        56,
    )[0]
    qe, partial = lax.optimization_barrier((qe, partial))
    index = lax.axis_index(AXES)
    parity = (index % 2).astype(I32).reshape(1, 1)
    total_rows = (w_msg.size + w_in.size + u_zr.size + u_h.size + 3 * w_query.size) // 128
    half = total_rows // 2
    args = (
        scal, nrow, qe, partial, scol, fcol, fetched,
        got_feats, code, pre, mean, div, upd, rst, cand, rstate, w_in, u_h, w_key,
        g_qkv, parity,
    )
    keep, send = pl.pallas_call(
        back_body,
        out_shape=[jax.ShapeDtypeStruct((half, 128), BF16)] * 2,
        in_specs=[vm] * (len(args) - 1) + [sm],
        out_specs=[vm] * 2,
        scratch_shapes=[pltpu.VMEM((n_side, 3 * m), BF16), pltpu.VMEM((n_side, width), BF16)],
        compiler_params=room(56),
        name="back",
    )(*args)
    pairs = [(i, i ^ 1) for i in range(devices)]
    teams = [[i for i in range(devices) if i % 2 == p] for p in range(2)]
    size = devices // 2
    half_sum = (
        keep.astype(F32) + lax.ppermute(send, AXES, pairs).astype(F32)
    ).astype(BF16).reshape(size, half // size, 128)
    shares = lax.all_to_all(
        half_sum, AXES, split_axis=0, concat_axis=0, tiled=True, axis_index_groups=teams
    )
    spread = call(spread_body, [(shares.shape, BF16)], (shares,), "spread", 6)[0]
    mine = lax.all_to_all(
        spread, AXES, split_axis=0, concat_axis=0, tiled=True, axis_index_groups=teams
    ).reshape(half, 128)
    other = lax.ppermute(mine, AXES, pairs)
    outs = [
        ((width, 3 * m), F32), ((m, 2 * m), F32), ((m, m), F32),
        ((w_msg.shape[0], width), F32), ((m, m), F32), ((m, m), F32), ((m, m), F32),
    ]
    g_in, g_zr, g_h, g_msg, g_q, g_k, g_v = pl.pallas_call(
        unpack_body,
        out_shape=[jax.ShapeDtypeStruct(a, d) for a, d in outs],
        in_specs=[vm, vm, sm],
        out_specs=[vm] * len(outs),
        compiler_params=room(8),
        name="unpack",
    )(mine, other, parity)
    return (new_memory, embedding, g_msg, g_in, g_zr, g_h, g_q, g_k, g_v)


def solution(mesh):
    split = P(AXES)
    return jax.shard_map(
        body,
        mesh=mesh,
        in_specs=(split,) * 9 + (P(),) * 7 + (split,),
        out_specs=(split, split) + (P(),) * 7,
        check_vma=False,
    )
```

```python
import functools
import math

import jax
import jax.numpy as jnp
from jax import lax
from jax.experimental import pallas as pl
from jax.experimental.pallas import tpu as pltpu
from jax.sharding import PartitionSpec as P

HEADS = 2
AXES = ("acct", "rep")
CAP_VALUE = 10.0
F32 = jnp.float32
BF16 = jnp.bfloat16
I32 = jnp.int32
EXACT = lax.Precision.HIGHEST

def room(mib):
    return pltpu.CompilerParams(vmem_limit_bytes=mib * 1024 * 1024)


def dot(a, b, **kw):
    return jnp.dot(a, b, preferred_element_type=F32, **kw)


def dot_nt(a, b, **kw):
    return lax.dot_general(a, b, (((1,), (1,)), ((), ())), preferred_element_type=F32, **kw)


def dot_tn(a, b, **kw):
    return lax.dot_general(a, b, (((0,), (0,)), ((), ())), preferred_element_type=F32, **kw)


def iota(shape, axis):
    return lax.broadcasted_iota(I32, shape, axis)


def to_col(table, n, per, lane0, base=0):
    devices, lanes = table.shape
    pick = ((iota((n, devices), 0) + base) // per == iota((n, devices), 1)).astype(F32)
    spread = dot(pick, table, precision=EXACT)
    r = iota((n, lanes), 0) + base
    at = iota((n, lanes), 1) == lane0 + r - r // per * per
    return jnp.sum(jnp.where(at, spread, 0.0), axis=1, keepdims=True)


def to_row(table, n, per, lane0):
    devices, lanes = table.shape
    c = iota((lanes, n), 1)
    pick = (iota((lanes, n), 0) == lane0 + c - c // per * per).astype(F32)
    spread = dot(table, pick, precision=EXACT)
    mine = iota((devices, n), 0) == iota((devices, n), 1) // per
    return jnp.sum(jnp.where(mine, spread, 0.0), axis=0, keepdims=True)


def sigmoid(v):
    return 1.0 / (1.0 + jnp.exp(-v))


def call(body, outs, args, name, mib, scratch=(), scalars=0):
    vm = pl.BlockSpec(memory_space=pltpu.VMEM)
    sm = pl.BlockSpec(memory_space=pltpu.SMEM)
    return pl.pallas_call(
        body,
        out_shape=[jax.ShapeDtypeStruct(s, d) for s, d in outs],
        in_specs=[vm] * (len(args) - scalars) + [sm] * scalars,
        out_specs=[vm] * len(outs),
        scratch_shapes=list(scratch),
        compiler_params=room(mib),
        name=name,
    )(*args)


def place_body(ce, cn, devices, so, ss, do, ds, no, ns, bk, feat, req, feats, dplace, nrank):
    events = so.shape[1]
    neighbours = no.shape[0]
    upper = (iota((events, events), 0) < iota((events, events), 1)).astype(BF16)
    own = iota((devices, events), 0)
    rows = iota((2 * devices * ce, events), 0)

    def fill(onehot, rank, value, cap):
        hits = (iota((cap, events), 0) == rank).astype(F32)
        owner_b = onehot.astype(BF16)
        high = dot_nt(owner_b, (hits * (value >> 7).astype(F32)).astype(BF16))
        low = dot_nt(owner_b, (hits * (value & 127).astype(F32)).astype(BF16))
        return high * 128.0 + low

    chosen = jnp.zeros((2 * devices * ce, events), F32)
    for side, (o_ref, s_ref) in enumerate(((so, ss), (do, ds))):
        owner = o_ref[...]
        onehot = (own == owner).astype(F32)
        before = dot(onehot.astype(BF16), upper)
        rank = jnp.sum(onehot * before, axis=0, keepdims=True).astype(I32)
        req[:, side * ce : (side + 1) * ce] = (
            fill(onehot, rank, s_ref[...] + 1, ce).astype(I32) - 1
        )
        req[:, (2 + side) * ce : (3 + side) * ce] = fill(onehot, rank, bk[...], ce).astype(I32)
        chosen = chosen + (rows == owner * (2 * ce) + (side * ce + rank)).astype(F32)
        if side == 1:
            dplace[...] = owner * ce + rank
    feats[...] = dot(chosen.astype(BF16), feat[...]).astype(BF16)
    base = jnp.zeros((devices, 1), F32)
    slots = jnp.zeros((devices, cn), F32)
    which = jnp.zeros((devices, cn), F32)
    event = iota((1, events), 1)
    for k in range(neighbours):
        onehot = (own == no[k : k + 1, :]).astype(F32)
        before = dot(onehot.astype(BF16), upper) + base
        rank = jnp.sum(onehot * before, axis=0, keepdims=True).astype(I32)
        nrank[k : k + 1, :] = rank
        base = base + jnp.sum(onehot, axis=1, keepdims=True)
        slots = slots + fill(onehot, rank, ns[k : k + 1, :], cn)
        which = which + fill(onehot, rank, event + 1, cn)
    req[:, 4 * ce : 4 * ce + cn] = slots.astype(I32)
    req[:, 4 * ce + cn :] = which.astype(I32) - 1


def widen_rows(source, target):
    step = 256

    def run(i, carry):
        b = pl.ds(pl.multiple_of(i * step, step), step)
        for h in range(target.shape[0]):
            target[h, b, :] = source[b, h * 128 : (h + 1) * 128].astype(F32)
        return carry

    lax.fori_loop(0, source.shape[0] // step, run, 0)


def narrow_rows(source, target):
    for h in range(source.shape[0]):
        target[:, h * 128 : (h + 1) * 128] = source[h].astype(BF16)


def pick_rows(table, target, slots_s, first, count, read):
    rows = math.lcm(count, 8)
    sources = rows // count

    def block(i, carry):
        for g in range(rows // 8):
            where = [
                read(slots_s[i * sources + r // count, first + r % count])
                for r in range(g * 8, g * 8 + 8)
            ]
            base = pl.multiple_of(i * rows + g * 8, 8)
            for h in range(table.shape[0]):
                found = [table[h, pl.ds(w, 1), :] for w in where]
                target[h, pl.ds(base, 8), :] = jnp.concatenate(found, axis=0)
        return carry

    lax.fori_loop(0, slots_s.shape[0] // sources, block, 0)


def sides_body(ce, memory, slots_s, rows, table, wide):
    widen_rows(memory, table)
    pick_rows(table, wide, slots_s, 0, 2 * ce, lambda v: jnp.maximum(v, 0))
    narrow_rows(wide, rows)


def answer_body(ce, cn, memory, new, slots_s, reply, table, wide, copied):
    acc_rows = memory.shape[0]
    widen_rows(memory, table)
    widen_rows(new, wide)

    each = 2 * ce
    rows = math.lcm(each, 8)
    sources = rows // each

    def store(i, carry):
        fresh = [
            wide[h, pl.ds(pl.multiple_of(i * rows, rows), rows), :] for h in range(wide.shape[0])
        ]
        for r in range(rows):
            slot = slots_s[i * sources + r // each, r % each]
            slot = jnp.where(slot >= 0, slot, acc_rows)
            for h in range(wide.shape[0]):
                table[h, pl.ds(slot, 1), :] = fresh[h][r : r + 1, :]
        return carry

    lax.fori_loop(0, slots_s.shape[0] // sources, store, 0)
    pick_rows(table, copied, slots_s, 4 * ce, cn, lambda v: v)
    narrow_rows(copied, reply)


def owner_body(
    ce, rows, feats, got, w_msg, w_in, u_zr, u_h,
    new, dst_new, sfirst, scol, fcol, code, pre, mean, div, upd, rst, cand, rstate, msg, bcol,
):
    n, f = feats.shape
    m = rows.shape[1]
    t = w_msg.shape[0] - m - f
    step = 128
    frequency = jnp.exp(iota((1, t), 1).astype(F32) * (-11.5 / t))
    numbers = got[:, : 4 * ce].astype(F32)
    scol[...] = to_col(numbers, n, 2 * ce, 0).astype(I32)
    bcol[...] = to_col(numbers, n, 2 * ce, 2 * ce)
    slots = to_row(numbers, n, 2 * ce, 0).astype(I32)

    def messages(i, carry):
        b = pl.ds(pl.multiple_of(i * step, step), step)
        enc = jnp.cos(bcol[b, :] * frequency).astype(BF16)
        code[b, :] = enc
        act = (
            dot(rows[b, :], w_msg[:m, :]) + dot(feats[b, :], w_msg[m : m + f, :])
        ) + dot(enc, w_msg[m + f :, :])
        pre[b, :] = act
        msg[b, :] = (act * sigmoid(act)).astype(BF16)
        return carry

    lax.fori_loop(0, n // step, messages, 0)
    def gru(i, early):
        b = pl.ds(pl.multiple_of(i * step, step), step)
        mine = scol[b, :]
        same = (mine == slots) & (mine >= 0)
        eq = same.astype(F32)
        eq_b = eq.astype(BF16)
        counts = dot(eq_b, jnp.ones((n, msg.shape[1]), BF16))
        divisor = jnp.maximum(counts, 1.0)
        div[b, :] = divisor
        earlier = jnp.where(iota((step, n), 1) < iota((step, n), 0) + i * step, eq, 0.0)
        fcol[b, :] = (jnp.sum(earlier, axis=1, keepdims=True) < 0.5).astype(F32)
        later = jnp.where(iota((step, n), 1) > iota((step, n), 0) + i * step, eq, 0.0)
        early = early + jnp.sum(later, axis=0, keepdims=True)
        mean_b = (dot(eq_b, msg[...]) / divisor).astype(BF16)
        mean[b, :] = mean_b
        state = rows[b, :]
        state_wide = state.astype(F32)
        from_input = dot(mean_b, w_in[...])
        from_state = dot(state, u_zr[...])
        update = sigmoid(from_input[:, :m] + from_state[:, :m])
        reset = sigmoid(from_input[:, m : 2 * m] + from_state[:, m:])
        reset_state = (reset * state_wide).astype(BF16)
        candidate = jnp.tanh(from_input[:, 2 * m :] + dot(reset_state, u_h[...]))
        upd[b, :] = update
        rst[b, :] = reset
        cand[b, :] = candidate
        rstate[b, :] = reset_state
        new[b, :] = ((1.0 - update) * state_wide + update * candidate).astype(BF16)
        return early

    early = lax.fori_loop(0, n // step, gru, jnp.zeros((1, n), F32))
    sfirst[...] = jnp.where((early < 0.5) & (slots >= 0), slots, -2)
    half = n // 2
    r = iota((half, n), 0)
    pick = (iota((half, n), 1) == r + (r // ce + 1) * ce).astype(F32).astype(BF16)
    dst_new[...] = dot(pick, new[...]).astype(BF16)


def refresh_body(block, old, sfirst, new, out):
    row = iota((block, 1), 0) + pl.program_id(0) * block
    hit = (row == sfirst[...]).astype(F32).astype(BF16)
    rows = dot(hit, new[...])
    found = dot(hit, jnp.ones((new.shape[0], 128), BF16)) > 0.5
    for h in range(rows.shape[1] // 128):
        c = slice(h * 128, (h + 1) * 128)
        out[:, c] = jnp.where(found, rows[:, c], old[:, c].astype(F32)).astype(BF16)


def refresh(memory, sfirst, new):
    n, m = memory.shape
    s = new.shape[0]
    block = 512
    return pl.pallas_call(
        functools.partial(refresh_body, block),
        grid=(n // block,),
        out_shape=jax.ShapeDtypeStruct((n, m), BF16),
        in_specs=[
            pl.BlockSpec((block, m), lambda i: (i, 0)),
            pl.BlockSpec((1, s), lambda i: (0, 0)),
            pl.BlockSpec((s, m), lambda i: (0, 0)),
        ],
        out_specs=pl.BlockSpec((block, m), lambda i: (i, 0)),
        compiler_params=room(8),
        name="refresh",
    )(memory, sfirst, new)


def hot_body(events, ce, cn, block, got, out):
    table = got[:, 4 * ce + cn :].astype(F32)
    event = to_col(table, block, cn, 0, pl.program_id(0) * block).astype(I32)
    out[...] = (iota((block, events), 1) == event).astype(F32).astype(BF16)


def hot(events, ce, cn, got, n):
    block = 512
    return pl.pallas_call(
        functools.partial(hot_body, events, ce, cn, block),
        grid=(n // block,),
        out_shape=jax.ShapeDtypeStruct((n, events), BF16),
        in_specs=[pl.BlockSpec(got.shape, lambda i: (0, 0))],
        out_specs=pl.BlockSpec((block, events), lambda i: (i, 0)),
        compiler_params=room(6),
        name="hot",
    )(got)


def query_body(back, dplace, w_query, q_rows, q_proj):
    n = back.shape[0]
    events = dplace.shape[1]
    pick = (iota((n, events), 0) == dplace[...]).astype(F32).astype(BF16)
    q = dot_tn(pick, back[...]).astype(BF16)
    q_rows[...] = q
    q_proj[...] = dot(q, w_query[...]).astype(BF16)


def attend_body(
    cn, devices, each, back, q_rows, q_proj, grad, w_query, w_key, w_value, dback, no, nrank, places,
    emb, reply, g_qkv, kp, vp, dk, dv, keys, wide, picked,
):
    events, m = q_rows.shape
    neighbours = no.shape[0]
    hs = m // HEADS
    scaling = 1.0 / math.sqrt(hs)
    widen_rows(back, wide)
    pick_rows(wide, picked, places, 0, events, lambda v: v)
    narrow_rows(picked, keys)
    qf = q_proj[...].astype(F32)
    gf = grad[...].astype(F32)
    lane = iota((events, 128), 1)
    raw = jnp.zeros((events, 128), F32)
    probs = jnp.zeros((events, 128), F32)
    for k in range(neighbours):
        b = slice(k * events, (k + 1) * events)
        rows = keys[b, :]
        kpk = dot(rows, w_key[...]).astype(BF16)
        vpk = dot(rows, w_value[...]).astype(BF16)
        kp[b, :] = kpk
        vp[b, :] = vpk
        pk = qf * kpk.astype(F32)
        pv = gf * vpk.astype(F32)
        for h in range(HEADS):
            c = slice(h * hs, (h + 1) * hs)
            at = lane == h * 64 + k
            raw = jnp.where(at, jnp.sum(pk[:, c], axis=1, keepdims=True), raw)
            probs = jnp.where(at, jnp.sum(pv[:, c], axis=1, keepdims=True), probs)
    raw = raw * scaling
    capped = jnp.tanh(raw / CAP_VALUE)
    first = lane < 64
    live = jnp.where(first, lane, lane - 64) < neighbours
    weights = jnp.where(live, jnp.exp(CAP_VALUE * capped), 0.0)

    def per_head(v):
        a = jnp.sum(jnp.where(first, v, 0.0), axis=1, keepdims=True)
        b = jnp.sum(jnp.where(first, 0.0, v), axis=1, keepdims=True)
        return jnp.where(first, a, b)

    attention = weights / per_head(weights)
    att_b = attention.astype(BF16).astype(F32)
    d_scores = attention * (probs - per_head(attention * probs))
    d_raw = d_scores * (1.0 - capped * capped) * scaling
    mix = [jnp.zeros((events, hs), F32) for _ in range(HEADS)]
    dq = [jnp.zeros((events, hs), F32) for _ in range(HEADS)]
    for k in range(neighbours):
        b = slice(k * events, (k + 1) * events)
        for h in range(HEADS):
            c = slice(h * hs, (h + 1) * hs)
            i = h * 64 + k
            a = att_b[:, i : i + 1]
            d = d_raw[:, i : i + 1]
            mix[h] = mix[h] + a * vp[b, c].astype(F32)
            dq[h] = dq[h] + d * kp[b, c].astype(F32)
            dk[b, c] = (d * qf[:, c]).astype(BF16)
            dv[b, c] = (a * gf[:, c]).astype(BF16)
    q = q_rows[...]
    dq_b = jnp.concatenate(dq, axis=1).astype(BF16)
    emb[...] = (q.astype(F32) + jnp.concatenate(mix, axis=1)).astype(BF16)
    g_qkv[0:m, :] = dot_tn(q, dq_b).astype(BF16)
    g_qkv[m : 2 * m, :] = dot_tn(keys[...], dk[...]).astype(BF16)
    g_qkv[2 * m : 3 * m, :] = dot_tn(keys[...], dv[...]).astype(BF16)
    d_rows = (gf + dot_nt(dq_b, w_query[...])).astype(BF16)
    n = devices * each
    spots = (iota((n, events), 0) == dback[...]).astype(F32).astype(BF16)
    sent = dot(spots, d_rows)
    att_t = att_b.T
    raw_t = d_raw.T
    own = iota((devices, events), 0)
    totals = [jnp.zeros((devices, m), F32) for _ in range(4)]
    for k in range(neighbours):
        onehot = (own == no[k : k + 1, :]).astype(F32).astype(BF16)
        hits = (iota((m, events), 0) == nrank[k : k + 1, :]).astype(F32)
        for j, v in enumerate((raw_t, raw_t, att_t, att_t)):
            i = (j % 2) * 64 + k
            values = (hits * v[i : i + 1, :]).astype(BF16)
            totals[j] = totals[j] + dot_nt(onehot, values)
    for j in range(4):
        spot = iota((n, devices), 0) == iota((n, devices), 1) * each + j
        sent = sent + dot(spot.astype(F32).astype(BF16), totals[j].astype(BF16))
    reply[...] = sent.astype(BF16)


def expand_body(cn, source, hots, out):
    events = hots.shape[1]

    def run(d, carry):
        b = pl.ds(pl.multiple_of(d * cn, cn), cn)
        e = pl.ds(pl.multiple_of(d * events, events), events)
        out[b, :] = dot(hots[b, :], source[e, :]).astype(BF16)
        return carry

    lax.fori_loop(0, hots.shape[0] // cn, run, 0, unroll=4)


def early_body(scal, nrow, ge, dq, drow, scol, w_value, out):
    n, m = out.shape
    hs = m // HEADS
    step = 256

    def block(i, carry):
        b = pl.ds(pl.multiple_of(i * step, step), step)
        mine = scol[b, :]
        mine = jnp.where(mine >= 0, mine, -7)
        hit = mine == nrow[...]
        parts = []
        for h in range(HEADS):
            a = jnp.where(hit, scal[2 + h : 3 + h, :].astype(F32), 0.0).astype(BF16)
            parts.append(dot(a, ge[:, h * hs : (h + 1) * hs]).astype(BF16))
        here = (mine == drow[...]).astype(F32).astype(BF16)
        dval = jnp.concatenate(parts, axis=1)
        out[b, :] = dot(here, dq[...]) + dot_nt(dval, w_value[...])
        return carry

    lax.fori_loop(0, n // step, block, 0)


def back_body(
    cn, scal, nrow, source, hots, partial, scol, fcol, rows, feats, code, pre, mean, div,
    upd, rst, cand, rstate, w_in, u_h, w_key, g_qkv, parity, keep, send, gates, dpre, expanded,
):
    n, m = mean.shape[0], rows.shape[1]
    f = feats.shape[1]
    hs = m // HEADS
    step = 256
    s = mean.shape[1]
    if cn % 16:
        qe = source
    else:
        qe = expanded
        expand_body(cn, source, hots, qe)

    def block(i, carry):
        b = pl.ds(pl.multiple_of(i * step, step), step)
        mine = scol[b, :]
        mine = jnp.where(mine >= 0, mine, -7)
        hit = mine == nrow[...]
        parts = []
        for h in range(HEADS):
            a = jnp.where(hit, scal[h : h + 1, :].astype(F32), 0.0).astype(BF16)
            parts.append(dot(a, qe[:, h * hs : (h + 1) * hs]).astype(BF16))
        du = partial[b, :] + dot_nt(jnp.concatenate(parts, axis=1), w_key[...])
        state = rows[b, :].astype(F32)
        update = upd[b, :]
        reset = rst[b, :]
        candidate = cand[b, :]
        d_cand = (du * update * (1.0 - candidate * candidate)).astype(BF16)
        d_reset = dot_nt(d_cand, u_h[...]) * state * reset * (1.0 - reset)
        d_update = du * (candidate - state) * update * (1.0 - update)
        d_gates = jnp.concatenate([d_update.astype(BF16), d_reset.astype(BF16), d_cand], axis=1)
        d_mean = dot_nt(d_gates, w_in[...]) / div[b, :]
        act = pre[b, :]
        sg = sigmoid(act)
        dpre[b, :] = (d_mean * sg * (1.0 + act * (1.0 - sg))).astype(BF16)
        gates[b, :] = jnp.where(fcol[b, :] > 0.5, d_gates.astype(F32), 0.0).astype(BF16)
        return carry

    lax.fori_loop(0, n // step, block, 0)
    half = keep.shape[0]
    even = parity[0, 0] == 0
    at = [0]

    def put(value):
        start, size = at[0], value.shape[0]
        low = max(0, min(size, half - start))
        pieces = ((value[:low, :], True, start), (value[low:, :], False, start + low - half))
        for part, first, r in pieces:
            if part.shape[0]:
                part = part.astype(BF16)
                b = slice(r, r + part.shape[0])

                @pl.when(even == first)
                def _():
                    keep[b, :] = part

                @pl.when(even != first)
                def _():
                    send[b, :] = part

        at[0] = start + size

    def put_cols(value):
        for j in range(value.shape[1] // 128):
            put(value[:, j * 128 : (j + 1) * 128])

    state_rows = rows[:n, :]
    put_cols(dot_tn(mean[...], gates[...]))
    put_cols(dot_tn(state_rows, gates[:, : 2 * m]))
    put_cols(dot_tn(rstate[...], gates[:, 2 * m :]))
    put_cols(dot_tn(state_rows, dpre[...]))
    put_cols(dot_tn(feats[...], dpre[...]))
    put_cols(dot_tn(code[...], dpre[...]))
    for j in range(3):
        put_cols(g_qkv[j * m : (j + 1) * m, :].astype(F32))


def spread_body(x, out):
    total = x[0].astype(F32)
    for i in range(1, x.shape[0]):
        total = total + x[i].astype(F32)
    total = total.astype(BF16)
    for i in range(x.shape[0]):
        out[i] = total


def unpack_body(mine, other, parity, g_in, g_zr, g_h, g_msg, g_q, g_k, g_v):
    half = mine.shape[0]
    even = parity[0, 0] == 0
    at = [0]

    def take(ref, r, c, size):
        start = at[0]
        low = max(0, min(size, half - start))
        if low:
            b = slice(start, start + low)
            ref[r : r + low, c : c + 128] = jnp.where(even, mine[b, :], other[b, :]).astype(F32)
        if low < size:
            b = slice(start + low - half, start + size - half)
            ref[r + low : r + size, c : c + 128] = jnp.where(
                even, other[b, :], mine[b, :]
            ).astype(F32)
        at[0] = start + size

    for ref in (g_in, g_zr, g_h, g_msg, g_q, g_k, g_v):
        for c in range(0, ref.shape[1], 128):
            take(ref, 0, c, ref.shape[0])


def exchange(x):
    return lax.all_to_all(x, AXES, split_axis=0, concat_axis=0, tiled=True)


def body(
    memory, features, buckets, src_owner, src_slot, dst_owner, dst_slot, nb_owner, nb_slot,
    w_msg, w_in, u_zr, u_h, w_query, w_key, w_value, emb_grad,
):
    devices = lax.axis_size(AXES)
    events, m = emb_grad.shape
    acc_rows = memory.shape[0]
    neighbours = nb_slot.shape[1]
    feat = features.shape[1]
    width = w_msg.shape[1]
    ce = 2 * events // devices
    cn = 2 * events * neighbours // devices
    n_dst = devices * ce
    n_side = 2 * n_dst
    n_nb = devices * cn
    lanes = 4 * ce + 2 * cn
    grad_all = lax.all_gather(emb_grad, AXES, axis=0, tiled=True)
    no = nb_owner.reshape(events, neighbours).T
    req, side_feats, dplace, nrank = call(
        functools.partial(place_body, ce, cn, devices),
        [
            ((devices, lanes), I32),
            ((n_side, feat), BF16),
            ((1, events), I32),
            ((neighbours, events), I32),
        ],
        (
            src_owner.reshape(1, events), src_slot.reshape(1, events),
            dst_owner.reshape(1, events), dst_slot.reshape(1, events),
            no, nb_slot.T, buckets.reshape(1, events), features,
        ),
        "place",
        56,
    )
    got = exchange(req.reshape(devices, 1, lanes)).reshape(devices, lanes)
    got_feats = exchange(side_feats.reshape(devices, 2 * ce, feat)).reshape(n_side, feat)
    vm = pl.BlockSpec(memory_space=pltpu.VMEM)
    sm = pl.BlockSpec(memory_space=pltpu.SMEM)
    owner_outs = [
        ((n_side, m), BF16), ((n_dst, m), BF16),
        ((1, n_side), I32), ((n_side, 1), I32), ((n_side, 1), F32),
        ((n_side, w_msg.shape[0] - m - feat), BF16),
        ((n_side, width), F32), ((n_side, width), BF16), ((n_side, width), F32),
        ((n_side, m), F32), ((n_side, m), F32), ((n_side, m), F32), ((n_side, m), BF16),
    ]
    fetched = pl.pallas_call(
        functools.partial(sides_body, ce),
        out_shape=jax.ShapeDtypeStruct((n_side, m), BF16),
        in_specs=[vm, sm],
        out_specs=vm,
        scratch_shapes=[
            pltpu.VMEM((m // 128, acc_rows, 128), F32), pltpu.VMEM((m // 128, n_side, 128), F32),
        ],
        compiler_params=room(56),
        name="sides",
    )(memory, got)
    (
        new_side, dst_new, sfirst, scol, fcol, code, pre, mean, div, upd, rst, cand, rstate,
    ) = call(
        functools.partial(owner_body, ce),
        owner_outs,
        (fetched, got_feats, got, w_msg, w_in, u_zr, u_h),
        "owner",
        56,
        scratch=[pltpu.VMEM((n_side, width), BF16), pltpu.VMEM((n_side, 1), F32)],
    )
    nb_reply = pl.pallas_call(
        functools.partial(answer_body, ce, cn),
        out_shape=jax.ShapeDtypeStruct((n_nb, m), BF16),
        in_specs=[vm, vm, sm],
        out_specs=vm,
        scratch_shapes=[
            pltpu.VMEM((m // 128, acc_rows + 8, 128), F32),
            pltpu.VMEM((m // 128, n_side, 128), F32), pltpu.VMEM((m // 128, n_nb, 128), F32),
        ],
        compiler_params=room(56),
        name="answer",
    )(memory, new_side, got)
    back_dst = exchange(dst_new.reshape(devices, ce, m)).reshape(n_dst, m)
    back_nb = exchange(nb_reply.reshape(devices, cn, m))
    back_dst, nb_reply = lax.optimization_barrier((back_dst, nb_reply))
    q_rows, q_proj = call(
        query_body,
        [((events, m), BF16), ((events, m), BF16)],
        (back_dst, dplace, w_query),
        "query",
        4,
    )
    proj_all = lax.all_gather(q_proj, AXES, axis=0, tiled=True)
    each = max(2 * ce, -(-(ce + 4) // 8) * 8)
    late_got, _ = lax.optimization_barrier((got, nb_reply))
    new_memory = refresh(memory, sfirst, new_side)
    late_event = late_got[:, 4 * ce + cn :].reshape(n_nb)
    table = jnp.maximum(late_event, 0) + jnp.arange(n_nb, dtype=I32) // cn * events
    ge = grad_all[table]
    late_slots = late_got[:, 4 * ce : 4 * ce + cn].reshape(n_nb)
    nrow = jnp.where(late_event >= 0, late_slots, -1).reshape(1, n_nb)
    drow = jnp.concatenate(
        [jnp.full((devices, each - ce), -1, I32), late_got[:, ce : 2 * ce]], axis=1
    ).reshape(1, devices * each)
    hots = hot(events, ce, cn, late_got, n_nb)
    nb_place = no * cn + nrank
    back_nb, new_memory, ge, nrow, drow, hots, nb_place, q_rows = lax.optimization_barrier(
        (back_nb, new_memory, ge, nrow, drow, hots, nb_place, q_rows)
    )
    dback = dplace // ce * each + (each - ce) + dplace % ce
    embedding, reply, g_qkv = call(
        functools.partial(attend_body, cn, devices, each),
        [((events, m), BF16), ((devices * each, m), BF16), ((3 * m, m), BF16)],
        (
            back_nb.reshape(n_nb, m), q_rows, q_proj, emb_grad, w_query, w_key, w_value, dback, no,
            nrank, nb_place,
        ),
        "attend",
        20,
        scratch=[pltpu.VMEM((events * neighbours, m), BF16)] * 5
        + [
            pltpu.VMEM((m // 128, n_nb, 128), F32),
            pltpu.VMEM((m // 128, events * neighbours, 128), F32),
        ],
        scalars=1,
    )
    back = exchange(reply.reshape(devices, each, m))
    source = proj_all[table] if cn % 16 else proj_all
    scal = back[:, :4, :cn].transpose(1, 0, 2).reshape(4, n_nb)
    partial = call(
        early_body,
        [((n_side, m), F32)],
        (scal, nrow, ge, back.reshape(devices * each, m), drow, scol, w_value),
        "early",
        56,
    )[0]
    source, partial = lax.optimization_barrier((source, partial))
    index = lax.axis_index(AXES)
    parity = (index % 2).astype(I32).reshape(1, 1)
    total_rows = (w_msg.size + w_in.size + u_zr.size + u_h.size + 3 * w_query.size) // 128
    half = total_rows // 2
    args = (
        scal, nrow, source, hots, partial, scol, fcol, fetched,
        got_feats, code, pre, mean, div, upd, rst, cand, rstate, w_in, u_h, w_key,
        g_qkv, parity,
    )
    keep, send = pl.pallas_call(
        functools.partial(back_body, cn),
        out_shape=[jax.ShapeDtypeStruct((half, 128), BF16)] * 2,
        in_specs=[vm] * (len(args) - 1) + [sm],
        out_specs=[vm] * 2,
        scratch_shapes=[
            pltpu.VMEM((n_side, 3 * m), BF16), pltpu.VMEM((n_side, width), BF16),
            pltpu.VMEM((n_nb, m), BF16),
        ],
        compiler_params=room(56),
        name="back",
    )(*args)
    pairs = [(i, i ^ 1) for i in range(devices)]
    teams = [[i for i in range(devices) if i % 2 == p] for p in range(2)]
    size = devices // 2
    half_sum = (
        keep.astype(F32) + lax.ppermute(send, AXES, pairs).astype(F32)
    ).astype(BF16).reshape(size, half // size, 128)
    shares = lax.all_to_all(
        half_sum, AXES, split_axis=0, concat_axis=0, tiled=True, axis_index_groups=teams
    )
    spread = call(spread_body, [(shares.shape, BF16)], (shares,), "spread", 6)[0]
    mine = lax.all_to_all(
        spread, AXES, split_axis=0, concat_axis=0, tiled=True, axis_index_groups=teams
    ).reshape(half, 128)
    other = lax.ppermute(mine, AXES, pairs)
    outs = [
        ((width, 3 * m), F32), ((m, 2 * m), F32), ((m, m), F32),
        ((w_msg.shape[0], width), F32), ((m, m), F32), ((m, m), F32), ((m, m), F32),
    ]
    g_in, g_zr, g_h, g_msg, g_q, g_k, g_v = pl.pallas_call(
        unpack_body,
        out_shape=[jax.ShapeDtypeStruct(a, d) for a, d in outs],
        in_specs=[vm, vm, sm],
        out_specs=[vm] * len(outs),
        compiler_params=room(8),
        name="unpack",
    )(mine, other, parity)
    return (new_memory, embedding, g_msg, g_in, g_zr, g_h, g_q, g_k, g_v)


def solution(mesh):
    split = P(AXES)
    return jax.shard_map(
        body,
        mesh=mesh,
        in_specs=(split,) * 9 + (P(),) * 7 + (split,),
        out_specs=(split, split) + (P(),) * 7,
        check_vma=False,
    )
```

```python
import functools
import math

import jax
import jax.numpy as jnp
from jax import lax
from jax.experimental import pallas as pl
from jax.experimental.pallas import tpu as pltpu
from jax.sharding import PartitionSpec as P

HEADS = 2
AXES = ("acct", "rep")
CAP_VALUE = 10.0
F32 = jnp.float32
BF16 = jnp.bfloat16
I32 = jnp.int32
EXACT = lax.Precision.HIGHEST

def room(mib):
    return pltpu.CompilerParams(vmem_limit_bytes=mib * 1024 * 1024)


def dot(a, b, **kw):
    return jnp.dot(a, b, preferred_element_type=F32, **kw)


def dot_nt(a, b, **kw):
    return lax.dot_general(a, b, (((1,), (1,)), ((), ())), preferred_element_type=F32, **kw)


def dot_tn(a, b, **kw):
    return lax.dot_general(a, b, (((0,), (0,)), ((), ())), preferred_element_type=F32, **kw)


def iota(shape, axis):
    return lax.broadcasted_iota(I32, shape, axis)


def to_col(table, n, per, lane0, base=0):
    devices, lanes = table.shape
    pick = ((iota((n, devices), 0) + base) // per == iota((n, devices), 1)).astype(F32)
    spread = dot(pick, table, precision=EXACT)
    r = iota((n, lanes), 0) + base
    at = iota((n, lanes), 1) == lane0 + r - r // per * per
    return jnp.sum(jnp.where(at, spread, 0.0), axis=1, keepdims=True)


def to_row(table, n, per, lane0):
    devices, lanes = table.shape
    c = iota((lanes, n), 1)
    pick = (iota((lanes, n), 0) == lane0 + c - c // per * per).astype(F32)
    spread = dot(table, pick, precision=EXACT)
    mine = iota((devices, n), 0) == iota((devices, n), 1) // per
    return jnp.sum(jnp.where(mine, spread, 0.0), axis=0, keepdims=True)


def sigmoid(v):
    return 1.0 / (1.0 + jnp.exp(-v))


def call(body, outs, args, name, mib, scratch=(), scalars=0):
    vm = pl.BlockSpec(memory_space=pltpu.VMEM)
    sm = pl.BlockSpec(memory_space=pltpu.SMEM)
    return pl.pallas_call(
        body,
        out_shape=[jax.ShapeDtypeStruct(s, d) for s, d in outs],
        in_specs=[vm] * (len(args) - scalars) + [sm] * scalars,
        out_specs=[vm] * len(outs),
        scratch_shapes=list(scratch),
        compiler_params=room(mib),
        name=name,
    )(*args)


def place_body(ce, cn, devices, so, ss, do, ds, no, ns, bk, feat, req, feats, dplace, nrank):
    events = so.shape[1]
    neighbours = no.shape[0]
    upper = (iota((events, events), 0) < iota((events, events), 1)).astype(BF16)
    own = iota((devices, events), 0)
    rows = iota((2 * devices * ce, events), 0)

    def fill(onehot, rank, value, cap):
        hits = (iota((cap, events), 0) == rank).astype(F32)
        owner_b = onehot.astype(BF16)
        high = dot_nt(owner_b, (hits * (value >> 7).astype(F32)).astype(BF16))
        low = dot_nt(owner_b, (hits * (value & 127).astype(F32)).astype(BF16))
        return high * 128.0 + low

    chosen = jnp.zeros((2 * devices * ce, events), F32)
    for side, (o_ref, s_ref) in enumerate(((so, ss), (do, ds))):
        owner = o_ref[...]
        onehot = (own == owner).astype(F32)
        before = dot(onehot.astype(BF16), upper)
        rank = jnp.sum(onehot * before, axis=0, keepdims=True).astype(I32)
        req[:, side * ce : (side + 1) * ce] = (
            fill(onehot, rank, s_ref[...] + 1, ce).astype(I32) - 1
        )
        req[:, (2 + side) * ce : (3 + side) * ce] = fill(onehot, rank, bk[...], ce).astype(I32)
        chosen = chosen + (rows == owner * (2 * ce) + (side * ce + rank)).astype(F32)
        if side == 1:
            dplace[...] = owner * ce + rank
    feats[...] = dot(chosen.astype(BF16), feat[...]).astype(BF16)
    base = jnp.zeros((devices, 1), F32)
    slots = jnp.zeros((devices, cn), F32)
    which = jnp.zeros((devices, cn), F32)
    event = iota((1, events), 1)
    for k in range(neighbours):
        onehot = (own == no[k : k + 1, :]).astype(F32)
        before = dot(onehot.astype(BF16), upper) + base
        rank = jnp.sum(onehot * before, axis=0, keepdims=True).astype(I32)
        nrank[k : k + 1, :] = rank
        base = base + jnp.sum(onehot, axis=1, keepdims=True)
        slots = slots + fill(onehot, rank, ns[k : k + 1, :], cn)
        which = which + fill(onehot, rank, event + 1, cn)
    req[:, 4 * ce : 4 * ce + cn] = slots.astype(I32)
    req[:, 4 * ce + cn :] = which.astype(I32) - 1


def widen_rows(source, target):
    step = 256

    def run(i, carry):
        b = pl.ds(pl.multiple_of(i * step, step), step)
        for h in range(target.shape[0]):
            target[h, b, :] = source[b, h * 128 : (h + 1) * 128].astype(F32)
        return carry

    lax.fori_loop(0, source.shape[0] // step, run, 0)


def narrow_rows(source, target):
    for h in range(source.shape[0]):
        target[:, h * 128 : (h + 1) * 128] = source[h].astype(BF16)


def pick_rows(table, target, slots_s, first, count, read):
    rows = math.lcm(count, 8)
    sources = rows // count

    def block(i, carry):
        for g in range(rows // 8):
            where = [
                read(slots_s[i * sources + r // count, first + r % count])
                for r in range(g * 8, g * 8 + 8)
            ]
            base = pl.multiple_of(i * rows + g * 8, 8)
            for h in range(table.shape[0]):
                found = [table[h, pl.ds(w, 1), :] for w in where]
                target[h, pl.ds(base, 8), :] = jnp.concatenate(found, axis=0)
        return carry

    lax.fori_loop(0, slots_s.shape[0] // sources, block, 0)


def sides_body(ce, memory, slots_s, rows, table, wide):
    widen_rows(memory, table)
    pick_rows(table, wide, slots_s, 0, 2 * ce, lambda v: jnp.maximum(v, 0))
    narrow_rows(wide, rows)


def answer_body(ce, cn, memory, new, slots_s, reply, table, wide, copied):
    acc_rows = memory.shape[0]
    widen_rows(memory, table)
    widen_rows(new, wide)

    each = 2 * ce
    rows = math.lcm(each, 8)
    sources = rows // each

    def store(i, carry):
        fresh = [
            wide[h, pl.ds(pl.multiple_of(i * rows, rows), rows), :] for h in range(wide.shape[0])
        ]
        for r in range(rows):
            slot = slots_s[i * sources + r // each, r % each]
            slot = jnp.where(slot >= 0, slot, acc_rows)
            for h in range(wide.shape[0]):
                table[h, pl.ds(slot, 1), :] = fresh[h][r : r + 1, :]
        return carry

    lax.fori_loop(0, slots_s.shape[0] // sources, store, 0)
    pick_rows(table, copied, slots_s, 4 * ce, cn, lambda v: v)
    narrow_rows(copied, reply)


def owner_body(
    ce, rows, feats, got, w_msg, w_in, u_zr, u_h,
    new, dst_new, sfirst, scol, fcol, code, pre, mean, div, upd, rst, cand, rstate, msg, bcol,
):
    n, f = feats.shape
    m = rows.shape[1]
    t = w_msg.shape[0] - m - f
    step = 256
    frequency = jnp.exp(iota((1, t), 1).astype(F32) * (-11.5 / t))
    numbers = got[:, : 4 * ce].astype(F32)
    scol[...] = to_col(numbers, n, 2 * ce, 0).astype(I32)
    bcol[...] = to_col(numbers, n, 2 * ce, 2 * ce)
    slots = to_row(numbers, n, 2 * ce, 0).astype(I32)

    def messages(i, carry):
        b = pl.ds(pl.multiple_of(i * step, step), step)
        enc = jnp.cos(bcol[b, :] * frequency).astype(BF16)
        code[b, :] = enc
        act = (
            dot(rows[b, :], w_msg[:m, :]) + dot(feats[b, :], w_msg[m : m + f, :])
        ) + dot(enc, w_msg[m + f :, :])
        pre[b, :] = act
        msg[b, :] = (act * sigmoid(act)).astype(BF16)
        return carry

    lax.fori_loop(0, n // step, messages, 0)
    def gru(i, early):
        b = pl.ds(pl.multiple_of(i * step, step), step)
        mine = scol[b, :]
        same = (mine == slots) & (mine >= 0)
        eq = same.astype(F32)
        eq_b = eq.astype(BF16)
        counts = dot(eq_b, jnp.ones((n, msg.shape[1]), BF16))
        divisor = jnp.maximum(counts, 1.0)
        div[b, :] = divisor
        earlier = jnp.where(iota((step, n), 1) < iota((step, n), 0) + i * step, eq, 0.0)
        fcol[b, :] = (jnp.sum(earlier, axis=1, keepdims=True) < 0.5).astype(F32)
        later = jnp.where(iota((step, n), 1) > iota((step, n), 0) + i * step, eq, 0.0)
        early = early + jnp.sum(later, axis=0, keepdims=True)
        mean_b = (dot(eq_b, msg[...]) / divisor).astype(BF16)
        mean[b, :] = mean_b
        state = rows[b, :]
        state_wide = state.astype(F32)
        from_input = dot(mean_b, w_in[...])
        from_state = dot(state, u_zr[...])
        update = sigmoid(from_input[:, :m] + from_state[:, :m])
        reset = sigmoid(from_input[:, m : 2 * m] + from_state[:, m:])
        reset_state = (reset * state_wide).astype(BF16)
        candidate = jnp.tanh(from_input[:, 2 * m :] + dot(reset_state, u_h[...]))
        upd[b, :] = update
        rst[b, :] = reset
        cand[b, :] = candidate
        rstate[b, :] = reset_state
        new[b, :] = ((1.0 - update) * state_wide + update * candidate).astype(BF16)
        return early

    early = lax.fori_loop(0, n // step, gru, jnp.zeros((1, n), F32))
    sfirst[...] = jnp.where((early < 0.5) & (slots >= 0), slots, -2)
    half = n // 2
    r = iota((half, n), 0)
    pick = (iota((half, n), 1) == r + (r // ce + 1) * ce).astype(F32).astype(BF16)
    dst_new[...] = dot(pick, new[...]).astype(BF16)


def refresh_body(block, old, sfirst, new, out):
    row = iota((block, 1), 0) + pl.program_id(0) * block
    hit = (row == sfirst[...]).astype(F32).astype(BF16)
    rows = dot(hit, new[...])
    found = dot(hit, jnp.ones((new.shape[0], 128), BF16)) > 0.5
    for h in range(rows.shape[1] // 128):
        c = slice(h * 128, (h + 1) * 128)
        out[:, c] = jnp.where(found, rows[:, c], old[:, c].astype(F32)).astype(BF16)


def refresh(memory, sfirst, new):
    n, m = memory.shape
    s = new.shape[0]
    block = 512
    return pl.pallas_call(
        functools.partial(refresh_body, block),
        grid=(n // block,),
        out_shape=jax.ShapeDtypeStruct((n, m), BF16),
        in_specs=[
            pl.BlockSpec((block, m), lambda i: (i, 0)),
            pl.BlockSpec((1, s), lambda i: (0, 0)),
            pl.BlockSpec((s, m), lambda i: (0, 0)),
        ],
        out_specs=pl.BlockSpec((block, m), lambda i: (i, 0)),
        compiler_params=room(8),
        name="refresh",
    )(memory, sfirst, new)


def hot_body(events, ce, cn, block, got, out):
    table = got[:, 4 * ce + cn :].astype(F32)
    event = to_col(table, block, cn, 0, pl.program_id(0) * block).astype(I32)
    out[...] = (iota((block, events), 1) == event).astype(F32).astype(BF16)


def hot(events, ce, cn, got, n):
    block = 512
    return pl.pallas_call(
        functools.partial(hot_body, events, ce, cn, block),
        grid=(n // block,),
        out_shape=jax.ShapeDtypeStruct((n, events), BF16),
        in_specs=[pl.BlockSpec(got.shape, lambda i: (0, 0))],
        out_specs=pl.BlockSpec((block, events), lambda i: (i, 0)),
        compiler_params=room(6),
        name="hot",
    )(got)


def query_body(back, dplace, w_query, q_rows, q_proj):
    n = back.shape[0]
    events = dplace.shape[1]
    pick = (iota((n, events), 0) == dplace[...]).astype(F32).astype(BF16)
    q = dot_tn(pick, back[...]).astype(BF16)
    q_rows[...] = q
    q_proj[...] = dot(q, w_query[...]).astype(BF16)


def attend_body(
    cn, devices, each, back, q_rows, q_proj, grad, w_query, w_key, w_value, dback, no, nrank, places,
    emb, reply, g_qkv, kp, vp, dk, dv, keys, wide, picked,
):
    events, m = q_rows.shape
    neighbours = no.shape[0]
    hs = m // HEADS
    scaling = 1.0 / math.sqrt(hs)
    widen_rows(back, wide)
    pick_rows(wide, picked, places, 0, events, lambda v: v)
    narrow_rows(picked, keys)
    qf = q_proj[...].astype(F32)
    gf = grad[...].astype(F32)
    lane = iota((events, 128), 1)
    raw = jnp.zeros((events, 128), F32)
    probs = jnp.zeros((events, 128), F32)
    for k in range(neighbours):
        b = slice(k * events, (k + 1) * events)
        rows = keys[b, :]
        kpk = dot(rows, w_key[...]).astype(BF16)
        vpk = dot(rows, w_value[...]).astype(BF16)
        kp[b, :] = kpk
        vp[b, :] = vpk
        pk = qf * kpk.astype(F32)
        pv = gf * vpk.astype(F32)
        for h in range(HEADS):
            c = slice(h * hs, (h + 1) * hs)
            at = lane == h * 64 + k
            raw = jnp.where(at, jnp.sum(pk[:, c], axis=1, keepdims=True), raw)
            probs = jnp.where(at, jnp.sum(pv[:, c], axis=1, keepdims=True), probs)
    raw = raw * scaling
    capped = jnp.tanh(raw / CAP_VALUE)
    first = lane < 64
    live = jnp.where(first, lane, lane - 64) < neighbours
    weights = jnp.where(live, jnp.exp(CAP_VALUE * capped), 0.0)

    def per_head(v):
        a = jnp.sum(jnp.where(first, v, 0.0), axis=1, keepdims=True)
        b = jnp.sum(jnp.where(first, 0.0, v), axis=1, keepdims=True)
        return jnp.where(first, a, b)

    attention = weights / per_head(weights)
    att_b = attention.astype(BF16).astype(F32)
    d_scores = attention * (probs - per_head(attention * probs))
    d_raw = d_scores * (1.0 - capped * capped) * scaling
    mix = [jnp.zeros((events, hs), F32) for _ in range(HEADS)]
    dq = [jnp.zeros((events, hs), F32) for _ in range(HEADS)]
    for k in range(neighbours):
        b = slice(k * events, (k + 1) * events)
        for h in range(HEADS):
            c = slice(h * hs, (h + 1) * hs)
            i = h * 64 + k
            a = att_b[:, i : i + 1]
            d = d_raw[:, i : i + 1]
            mix[h] = mix[h] + a * vp[b, c].astype(F32)
            dq[h] = dq[h] + d * kp[b, c].astype(F32)
            dk[b, c] = (d * qf[:, c]).astype(BF16)
            dv[b, c] = (a * gf[:, c]).astype(BF16)
    q = q_rows[...]
    dq_b = jnp.concatenate(dq, axis=1).astype(BF16)
    emb[...] = (q.astype(F32) + jnp.concatenate(mix, axis=1)).astype(BF16)
    g_qkv[0:m, :] = dot_tn(q, dq_b).astype(BF16)
    g_qkv[m : 2 * m, :] = dot_tn(keys[...], dk[...]).astype(BF16)
    g_qkv[2 * m : 3 * m, :] = dot_tn(keys[...], dv[...]).astype(BF16)
    d_rows = (gf + dot_nt(dq_b, w_query[...])).astype(BF16)
    n = devices * each
    spots = (iota((n, events), 0) == dback[...]).astype(F32).astype(BF16)
    sent = dot(spots, d_rows)
    att_t = att_b.T
    raw_t = d_raw.T
    own = iota((devices, events), 0)
    totals = [jnp.zeros((devices, m), F32) for _ in range(4)]
    for k in range(neighbours):
        onehot = (own == no[k : k + 1, :]).astype(F32).astype(BF16)
        hits = (iota((m, events), 0) == nrank[k : k + 1, :]).astype(F32)
        for j, v in enumerate((raw_t, raw_t, att_t, att_t)):
            i = (j % 2) * 64 + k
            values = (hits * v[i : i + 1, :]).astype(BF16)
            totals[j] = totals[j] + dot_nt(onehot, values)
    for j in range(4):
        spot = iota((n, devices), 0) == iota((n, devices), 1) * each + j
        sent = sent + dot(spot.astype(F32).astype(BF16), totals[j].astype(BF16))
    reply[...] = sent.astype(BF16)


def expand_body(cn, source, hots, out):
    events = hots.shape[1]

    def run(d, carry):
        b = pl.ds(pl.multiple_of(d * cn, cn), cn)
        e = pl.ds(pl.multiple_of(d * events, events), events)
        out[b, :] = dot(hots[b, :], source[e, :]).astype(BF16)
        return carry

    lax.fori_loop(0, hots.shape[0] // cn, run, 0, unroll=4)


def early_body(scal, nrow, ge, dq, drow, scol, w_value, out):
    n, m = out.shape
    hs = m // HEADS
    step = 256

    def block(i, carry):
        b = pl.ds(pl.multiple_of(i * step, step), step)
        mine = scol[b, :]
        mine = jnp.where(mine >= 0, mine, -7)
        hit = mine == nrow[...]
        parts = []
        for h in range(HEADS):
            a = jnp.where(hit, scal[2 + h : 3 + h, :].astype(F32), 0.0).astype(BF16)
            parts.append(dot(a, ge[:, h * hs : (h + 1) * hs]).astype(BF16))
        here = (mine == drow[...]).astype(F32).astype(BF16)
        dval = jnp.concatenate(parts, axis=1)
        out[b, :] = dot(here, dq[...]) + dot_nt(dval, w_value[...])
        return carry

    lax.fori_loop(0, n // step, block, 0)


def back_body(
    cn, scal, nrow, source, hots, partial, scol, fcol, rows, feats, code, pre, mean, div,
    upd, rst, cand, rstate, w_in, u_h, w_key, g_qkv, parity, keep, send, gates, dpre, expanded,
):
    n, m = mean.shape[0], rows.shape[1]
    f = feats.shape[1]
    hs = m // HEADS
    step = 256
    s = mean.shape[1]
    if cn % 16:
        qe = source
    else:
        qe = expanded
        expand_body(cn, source, hots, qe)

    def block(i, carry):
        b = pl.ds(pl.multiple_of(i * step, step), step)
        mine = scol[b, :]
        mine = jnp.where(mine >= 0, mine, -7)
        hit = mine == nrow[...]
        parts = []
        for h in range(HEADS):
            a = jnp.where(hit, scal[h : h + 1, :].astype(F32), 0.0).astype(BF16)
            parts.append(dot(a, qe[:, h * hs : (h + 1) * hs]).astype(BF16))
        du = partial[b, :] + dot_nt(jnp.concatenate(parts, axis=1), w_key[...])
        state = rows[b, :].astype(F32)
        update = upd[b, :]
        reset = rst[b, :]
        candidate = cand[b, :]
        d_cand = (du * update * (1.0 - candidate * candidate)).astype(BF16)
        d_reset = dot_nt(d_cand, u_h[...]) * state * reset * (1.0 - reset)
        d_update = du * (candidate - state) * update * (1.0 - update)
        d_gates = jnp.concatenate([d_update.astype(BF16), d_reset.astype(BF16), d_cand], axis=1)
        d_mean = dot_nt(d_gates, w_in[...]) / div[b, :]
        act = pre[b, :]
        sg = sigmoid(act)
        dpre[b, :] = (d_mean * sg * (1.0 + act * (1.0 - sg))).astype(BF16)
        gates[b, :] = jnp.where(fcol[b, :] > 0.5, d_gates.astype(F32), 0.0).astype(BF16)
        return carry

    lax.fori_loop(0, n // step, block, 0)
    half = keep.shape[0]
    even = parity[0, 0] == 0
    at = [0]

    def put(value):
        start, size = at[0], value.shape[0]
        low = max(0, min(size, half - start))
        pieces = ((value[:low, :], True, start), (value[low:, :], False, start + low - half))
        for part, first, r in pieces:
            if part.shape[0]:
                part = part.astype(BF16)
                b = slice(r, r + part.shape[0])

                @pl.when(even == first)
                def _():
                    keep[b, :] = part

                @pl.when(even != first)
                def _():
                    send[b, :] = part

        at[0] = start + size

    def put_cols(value):
        for j in range(value.shape[1] // 128):
            put(value[:, j * 128 : (j + 1) * 128])

    state_rows = rows[:n, :]
    put_cols(dot_tn(mean[...], gates[...]))
    put_cols(dot_tn(state_rows, gates[:, : 2 * m]))
    put_cols(dot_tn(rstate[...], gates[:, 2 * m :]))
    put_cols(dot_tn(state_rows, dpre[...]))
    put_cols(dot_tn(feats[...], dpre[...]))
    put_cols(dot_tn(code[...], dpre[...]))
    for j in range(3):
        put_cols(g_qkv[j * m : (j + 1) * m, :].astype(F32))


def spread_body(x, out):
    total = x[0].astype(F32)
    for i in range(1, x.shape[0]):
        total = total + x[i].astype(F32)
    total = total.astype(BF16)
    for i in range(x.shape[0]):
        out[i] = total


def unpack_body(mine, other, parity, g_in, g_zr, g_h, g_msg, g_q, g_k, g_v):
    half = mine.shape[0]
    even = parity[0, 0] == 0
    at = [0]

    def take(ref, r, c, size):
        start = at[0]
        low = max(0, min(size, half - start))
        if low:
            b = slice(start, start + low)
            ref[r : r + low, c : c + 128] = jnp.where(even, mine[b, :], other[b, :]).astype(F32)
        if low < size:
            b = slice(start + low - half, start + size - half)
            ref[r + low : r + size, c : c + 128] = jnp.where(
                even, other[b, :], mine[b, :]
            ).astype(F32)
        at[0] = start + size

    for ref in (g_in, g_zr, g_h, g_msg, g_q, g_k, g_v):
        for c in range(0, ref.shape[1], 128):
            take(ref, 0, c, ref.shape[0])


def exchange(x):
    return lax.all_to_all(x, AXES, split_axis=0, concat_axis=0, tiled=True)


def body(
    memory, features, buckets, src_owner, src_slot, dst_owner, dst_slot, nb_owner, nb_slot,
    w_msg, w_in, u_zr, u_h, w_query, w_key, w_value, emb_grad,
):
    devices = lax.axis_size(AXES)
    events, m = emb_grad.shape
    acc_rows = memory.shape[0]
    neighbours = nb_slot.shape[1]
    feat = features.shape[1]
    width = w_msg.shape[1]
    ce = 2 * events // devices
    cn = 2 * events * neighbours // devices
    n_dst = devices * ce
    n_side = 2 * n_dst
    n_nb = devices * cn
    lanes = 4 * ce + 2 * cn
    grad_all = lax.all_gather(emb_grad, AXES, axis=0, tiled=True)
    no = nb_owner.reshape(events, neighbours).T
    req, side_feats, dplace, nrank = call(
        functools.partial(place_body, ce, cn, devices),
        [
            ((devices, lanes), I32),
            ((n_side, feat), BF16),
            ((1, events), I32),
            ((neighbours, events), I32),
        ],
        (
            src_owner.reshape(1, events), src_slot.reshape(1, events),
            dst_owner.reshape(1, events), dst_slot.reshape(1, events),
            no, nb_slot.T, buckets.reshape(1, events), features,
        ),
        "place",
        56,
    )
    got = exchange(req.reshape(devices, 1, lanes)).reshape(devices, lanes)
    got_feats = exchange(side_feats.reshape(devices, 2 * ce, feat)).reshape(n_side, feat)
    vm = pl.BlockSpec(memory_space=pltpu.VMEM)
    sm = pl.BlockSpec(memory_space=pltpu.SMEM)
    owner_outs = [
        ((n_side, m), BF16), ((n_dst, m), BF16),
        ((1, n_side), I32), ((n_side, 1), I32), ((n_side, 1), F32),
        ((n_side, w_msg.shape[0] - m - feat), BF16),
        ((n_side, width), F32), ((n_side, width), BF16), ((n_side, width), F32),
        ((n_side, m), F32), ((n_side, m), F32), ((n_side, m), F32), ((n_side, m), BF16),
    ]
    fetched = pl.pallas_call(
        functools.partial(sides_body, ce),
        out_shape=jax.ShapeDtypeStruct((n_side, m), BF16),
        in_specs=[vm, sm],
        out_specs=vm,
        scratch_shapes=[
            pltpu.VMEM((m // 128, acc_rows, 128), F32), pltpu.VMEM((m // 128, n_side, 128), F32),
        ],
        compiler_params=room(56),
        name="sides",
    )(memory, got)
    (
        new_side, dst_new, sfirst, scol, fcol, code, pre, mean, div, upd, rst, cand, rstate,
    ) = call(
        functools.partial(owner_body, ce),
        owner_outs,
        (fetched, got_feats, got, w_msg, w_in, u_zr, u_h),
        "owner",
        56,
        scratch=[pltpu.VMEM((n_side, width), BF16), pltpu.VMEM((n_side, 1), F32)],
    )
    nb_reply = pl.pallas_call(
        functools.partial(answer_body, ce, cn),
        out_shape=jax.ShapeDtypeStruct((n_nb, m), BF16),
        in_specs=[vm, vm, sm],
        out_specs=vm,
        scratch_shapes=[
            pltpu.VMEM((m // 128, acc_rows + 8, 128), F32),
            pltpu.VMEM((m // 128, n_side, 128), F32), pltpu.VMEM((m // 128, n_nb, 128), F32),
        ],
        compiler_params=room(56),
        name="answer",
    )(memory, new_side, got)
    back_dst = exchange(dst_new.reshape(devices, ce, m)).reshape(n_dst, m)
    back_nb = exchange(nb_reply.reshape(devices, cn, m))
    back_dst, nb_reply = lax.optimization_barrier((back_dst, nb_reply))
    q_rows, q_proj = call(
        query_body,
        [((events, m), BF16), ((events, m), BF16)],
        (back_dst, dplace, w_query),
        "query",
        4,
    )
    proj_all = lax.all_gather(q_proj, AXES, axis=0, tiled=True)
    each = max(2 * ce, -(-(ce + 4) // 8) * 8)
    late_got, _ = lax.optimization_barrier((got, nb_reply))
    new_memory = refresh(memory, sfirst, new_side)
    late_event = late_got[:, 4 * ce + cn :].reshape(n_nb)
    table = jnp.maximum(late_event, 0) + jnp.arange(n_nb, dtype=I32) // cn * events
    ge = grad_all[table]
    late_slots = late_got[:, 4 * ce : 4 * ce + cn].reshape(n_nb)
    nrow = jnp.where(late_event >= 0, late_slots, -1).reshape(1, n_nb)
    drow = jnp.concatenate(
        [jnp.full((devices, each - ce), -1, I32), late_got[:, ce : 2 * ce]], axis=1
    ).reshape(1, devices * each)
    hots = hot(events, ce, cn, late_got, n_nb)
    nb_place = no * cn + nrank
    back_nb, new_memory, ge, nrow, drow, hots, nb_place, q_rows = lax.optimization_barrier(
        (back_nb, new_memory, ge, nrow, drow, hots, nb_place, q_rows)
    )
    dback = dplace // ce * each + (each - ce) + dplace % ce
    embedding, reply, g_qkv = call(
        functools.partial(attend_body, cn, devices, each),
        [((events, m), BF16), ((devices * each, m), BF16), ((3 * m, m), BF16)],
        (
            back_nb.reshape(n_nb, m), q_rows, q_proj, emb_grad, w_query, w_key, w_value, dback, no,
            nrank, nb_place,
        ),
        "attend",
        20,
        scratch=[pltpu.VMEM((events * neighbours, m), BF16)] * 5
        + [
            pltpu.VMEM((m // 128, n_nb, 128), F32),
            pltpu.VMEM((m // 128, events * neighbours, 128), F32),
        ],
        scalars=1,
    )
    back = exchange(reply.reshape(devices, each, m))
    source = proj_all[table] if cn % 16 else proj_all
    scal = back[:, :4, :cn].transpose(1, 0, 2).reshape(4, n_nb)
    partial = call(
        early_body,
        [((n_side, m), F32)],
        (scal, nrow, ge, back.reshape(devices * each, m), drow, scol, w_value),
        "early",
        56,
    )[0]
    source, partial = lax.optimization_barrier((source, partial))
    index = lax.axis_index(AXES)
    parity = (index % 2).astype(I32).reshape(1, 1)
    total_rows = (w_msg.size + w_in.size + u_zr.size + u_h.size + 3 * w_query.size) // 128
    half = total_rows // 2
    args = (
        scal, nrow, source, hots, partial, scol, fcol, fetched,
        got_feats, code, pre, mean, div, upd, rst, cand, rstate, w_in, u_h, w_key,
        g_qkv, parity,
    )
    keep, send = pl.pallas_call(
        functools.partial(back_body, cn),
        out_shape=[jax.ShapeDtypeStruct((half, 128), BF16)] * 2,
        in_specs=[vm] * (len(args) - 1) + [sm],
        out_specs=[vm] * 2,
        scratch_shapes=[
            pltpu.VMEM((n_side, 3 * m), BF16), pltpu.VMEM((n_side, width), BF16),
            pltpu.VMEM((n_nb, m), BF16),
        ],
        compiler_params=room(56),
        name="back",
    )(*args)
    pairs = [(i, i ^ 1) for i in range(devices)]
    teams = [[i for i in range(devices) if i % 2 == p] for p in range(2)]
    size = devices // 2
    half_sum = (
        keep.astype(F32) + lax.ppermute(send, AXES, pairs).astype(F32)
    ).astype(BF16).reshape(size, half // size, 128)
    shares = lax.all_to_all(
        half_sum, AXES, split_axis=0, concat_axis=0, tiled=True, axis_index_groups=teams
    )
    spread = call(spread_body, [(shares.shape, BF16)], (shares,), "spread", 6)[0]
    mine = lax.all_to_all(
        spread, AXES, split_axis=0, concat_axis=0, tiled=True, axis_index_groups=teams
    ).reshape(half, 128)
    other = lax.ppermute(mine, AXES, pairs)
    outs = [
        ((width, 3 * m), F32), ((m, 2 * m), F32), ((m, m), F32),
        ((w_msg.shape[0], width), F32), ((m, m), F32), ((m, m), F32), ((m, m), F32),
    ]
    g_in, g_zr, g_h, g_msg, g_q, g_k, g_v = pl.pallas_call(
        unpack_body,
        out_shape=[jax.ShapeDtypeStruct(a, d) for a, d in outs],
        in_specs=[vm, vm, sm],
        out_specs=[vm] * len(outs),
        compiler_params=room(8),
        name="unpack",
    )(mine, other, parity)
    return (new_memory, embedding, g_msg, g_in, g_zr, g_h, g_q, g_k, g_v)


def solution(mesh):
    split = P(AXES)
    return jax.shard_map(
        body,
        mesh=mesh,
        in_specs=(split,) * 9 + (P(),) * 7 + (split,),
        out_specs=(split, split) + (P(),) * 7,
        check_vma=False,
    )
```
